32 devices in a mesh: slab: 16 (over z, x, core), tpl: 2 (over y).
Axes of the slice: x: 2, y: 2, z: 4, core: 2. Of those that a mesh axis runs over, the one named last changes fastest.
Arguments:
- data: bfloat16 [128, 3, 16384], P('tpl', None, 'slab')
- templates: bfloat16 [64, 8, 3, 512], P(('tpl', 'slab')), may hold values from -6 to 6
- stations: int32 [64, 8], P(('tpl', 'slab')), may hold values from 0 to 127
- shifts: int32 [64, 8], P(('tpl', 'slab')), may hold values from 0 to 255
- used: int32 [64], P(('tpl', 'slab')), may hold values from 1 to 8
Outputs:
- detection: float32 [64, 16384], P('tpl', 'slab')
The draws below stay inside these ranges and needn't reach their ends.
Inputs may be any that keep to these rules, and one draw needn't show every extreme that they name: Only the first used[j] slots of template j count; stations may repeat.
All inputs are finite; a program needn't handle non-finite values.
Results may differ from the reference program's by a relative error of at most 0.0065.
Values may be sent and summed in bfloat16 or wider, within the bound.
A program may use at most 256 MiB of HBM per device.

```python
import math
import jax
import jax.numpy as jnp
from jax import lax

COMP = 3
L = 512
K = 8
MAXSHIFT = 256
STA = 128
NS = 16384
NT = 64
RIM = 768


def draw_data(key, part):
    first, second, third = jax.random.split(key, 3)
    base = jax.random.normal(first, (STA, COMP, NS), jnp.float32)
    top = math.log(10.0)
    station_scale = jnp.exp(jax.random.uniform(second, (STA, 1, 1), jnp.float32, 0.0, math.log(10.0)))
    block_scale = jnp.exp(jax.random.uniform(third, (1, 1, NS // 32), jnp.float32, 0.0, top))
    time_scale = jnp.repeat(block_scale, 32, axis=2)
    return (base * station_scale * time_scale).astype(jnp.bfloat16)


def with_ends(array, stream_key, low, largest):
    shape = array.shape
    index_at = [jax.random.randint(jax.random.fold_in(stream_key, axis), (), 0, shape[axis]) for axis in range(len(shape))]
    array = array.at[tuple(index_at)].set(low)
    longest = shape.index(max(shape))
    index_at[longest] = (index_at[longest] + 1) % shape[longest]
    return array.at[tuple(index_at)].set(largest)


def level_of(key, shape, cuts, smallest, top_value):
    factor_of = 1.0
    for dim, shards_of in cuts:
        heights = jax.random.uniform(jax.random.fold_in(jax.random.fold_in(key, 6), dim), (shards_of,), jnp.float32, smallest / len(cuts), top_value / len(cuts))
        factor_of = factor_of * jnp.repeat(jnp.exp(heights), shape[dim] // shards_of).reshape((-1,) + (1,) * (len(shape) - 1 - dim))
    return factor_of


def centred(stream_key, dims, width, most, cuts=(), kind=jnp.bfloat16):
    values = jax.random.normal(stream_key, dims, jnp.float32) * width
    if len(cuts) > 0:
        values = level_of(stream_key, dims, cuts, -0.22, 0.18) * values
    return jnp.clip(values, min=-most, max=most).astype(kind)


def setup_inputs(seed: int = 0) -> dict:
    splits = jax.random.split(jax.random.key(seed), 6)
    data = draw_data(jax.random.fold_in(splits[5], 71), 0)
    templates = centred(splits[1], (NT, K, COMP, L), 1.0, 6.0, ((0, 32),))
    stations = with_ends(jax.random.randint(splits[2], (NT, K), 0, STA), jax.random.fold_in(splits[2], 1), 0, STA - 1).astype(jnp.int32)
    shifts = with_ends(jax.random.randint(splits[3], (NT, K), 0, MAXSHIFT), jax.random.fold_in(splits[3], 1), 0, MAXSHIFT - 1).astype(jnp.int32)
    used = with_ends(jax.random.randint(splits[4], (NT,), 1, K + 1), jax.random.fold_in(splits[4], 1), 1, K).astype(jnp.int32)
    return dict(data=data, templates=templates, stations=stations, shifts=shifts, used=used)


EPS = 1e-05

def normalize(templates):
    span = templates.shape[-1]
    rows = templates.astype(jnp.float32)
    centered = rows - lax.optimization_barrier(jnp.mean(rows, axis=-1, keepdims=True))
    rms = jnp.sqrt(lax.optimization_barrier(jnp.mean(centered * centered, axis=-1, keepdims=True)) + EPS)
    return (centered / (rms * math.sqrt(span))).astype(jnp.bfloat16)

def reference(data, templates, stations, shifts, used):
    total = data.shape[2]
    length = total + RIM
    extended = jnp.pad(data.astype(jnp.float32), ((0, 0), (0, 0), (0, RIM)))
    spectrum = jnp.fft.rfft(extended, n=length, axis=-1)
    ones_f = jnp.conj(jnp.fft.rfft(jnp.ones((L,), jnp.float32), n=length))
    keep = total + MAXSHIFT
    sums = jnp.fft.irfft(spectrum * ones_f, n=length, axis=-1)[..., :keep]
    squares = jnp.fft.irfft(jnp.fft.rfft(extended * extended, n=length, axis=-1) * ones_f, n=length, axis=-1)[..., :keep]
    spread = (squares - sums * sums / L) / L
    inv_norm = (1.0 / (math.sqrt(L) * jnp.sqrt(jnp.maximum(spread, 0.0) + EPS))).astype(jnp.bfloat16)
    unit = normalize(templates)

    def one(item):
        tn, sta, sh, count = item
        rows = spectrum[sta]
        tf = jnp.conj(jnp.fft.rfft(tn.astype(jnp.float32), n=length, axis=-1))
        full = jnp.fft.irfft(rows * tf, n=length, axis=-1)
        corr = jax.vmap(lambda r, s: lax.dynamic_slice_in_dim(r, s, total, 1))(full, sh)
        norms = jax.vmap(lambda r, s: lax.dynamic_slice_in_dim(r, s, total, 1))(inv_norm[sta], sh)
        slots = jnp.arange(K, dtype=jnp.int32)
        scale = jnp.sqrt(L / (3.0 * count.astype(jnp.float32)))
        weight = jnp.where(slots < count, scale, 0.0).astype(jnp.float32)
        return lax.optimization_barrier(jnp.sum(corr * norms.astype(jnp.float32) * weight[:, None, None], axis=(0, 1)))
    return lax.map(one, (unit, stations, shifts, used))
```

```python
import functools
import math

import jax
import jax.numpy as jnp
from jax import lax
from jax.experimental import pallas as pl
from jax.experimental.pallas import tpu as pltpu
from jax.sharding import PartitionSpec as P

MAXSHIFT = 256
EPS = 1e-05
MESH = pl.DeviceIdType.MESH

LANES = 128
LAGS = 32
TURNS = LANES // LAGS
PASS = 6
PLANE = 16
CHUNKS = 5
AHEAD = 7
FIELDS = 7


def normalized(rows):
    span = rows.shape[-1]
    centered = rows - jnp.mean(rows, axis=-1, keepdims=True)
    rms = jnp.sqrt(jnp.mean(centered * centered, axis=-1, keepdims=True) + EPS)
    return (centered / (rms * math.sqrt(span))).astype(jnp.bfloat16)


def exchange_kernel(reach, hop, data_ref, templates_ref, stations_ref, shifts_ref, used_ref, ext_ref, panels_ref, table_ref, *scratch):
    rows_ref, lists_ref, sta_ref, shf_ref, use_ref, loads = scratch[:6]
    halo_send, halo_recv, far_send, far_recv, side_send, side_recv, peer_send, peer_recv, mate_send, mate_recv = scratch[6:16]
    list_mate_send, list_mate_recv, list_far_send, list_far_recv, list_side_send, list_side_recv, list_peer_send, list_peer_recv = scratch[16:]
    rows, samples = data_ref.shape
    height = templates_ref.shape[0]
    mine, slots = stations_ref.shape
    slabs = lax.axis_size("slab")
    blocks = lax.axis_size("tpl")
    outer = slabs // 4
    slab = lax.axis_index("slab")
    tpl = lax.axis_index("tpl")
    core = lax.rem(slab, 2)
    mate = slab + 1 - 2 * core
    side = slab + 2 - 4 * lax.rem(slab // 2, 2)
    beside = lax.rem(slab + slabs - 1 + 2 * core, slabs)

    local = [
        pltpu.make_async_copy(templates_ref, rows_ref, loads.at[0]),
        pltpu.make_async_copy(stations_ref, sta_ref, loads.at[1]),
        pltpu.make_async_copy(shifts_ref, shf_ref, loads.at[2]),
        pltpu.make_async_copy(used_ref, use_ref, loads.at[3]),
        pltpu.make_async_copy(data_ref, ext_ref.at[:, :samples], loads.at[4]),
    ]
    for copy in local:
        copy.start()

    barrier = pltpu.get_barrier_semaphore()
    for d in range(1, blocks):
        pl.semaphore_signal(barrier, inc=1, device_id={"tpl": lax.rem(tpl + d, blocks)}, device_id_type=MESH)
    for d in range(1, outer):
        pl.semaphore_signal(barrier, inc=1, device_id={"slab": lax.rem(slab + 4 * d, slabs)}, device_id_type=MESH)
    for device in (mate, side, beside):
        pl.semaphore_signal(barrier, inc=1, device_id={"slab": device}, device_id_type=MESH)

    local[0].wait()
    panels_ref[pl.ds(pl.multiple_of(slab * height, height), height), :] = normalized(rows_ref[...].astype(jnp.float32))
    for copy in local[1:4]:
        copy.wait()
    lane = lax.broadcasted_iota(jnp.int32, (mine, LANES), 1)
    line = lax.broadcasted_iota(jnp.int32, (mine, LANES), 0)
    station = jnp.zeros((mine, LANES), jnp.int32)
    shift = jnp.zeros((mine, LANES), jnp.int32)
    used = jnp.zeros((mine, LANES), jnp.int32)
    for j in range(mine):
        used = jnp.where(line == j, use_ref[j], used)
        for k in range(slots):
            spot = jnp.logical_and(line == j, lane == k)
            station = jnp.where(spot, sta_ref[j, k], station)
            shift = jnp.where(spot, shf_ref[j, k], shift)
    owner = lax.div(station, hop)
    local_station = station - owner * hop
    half = lax.bitwise_and(lax.shift_right_logical(shift, 6), 1)
    first = lax.shift_right_logical(shift, 7)
    base = local_station * (TURNS * PLANE) + first
    fields = [
        jnp.where(lane < used, owner, -1),
        lax.bitwise_and(shift, 63),
        (2 * local_station + half) * AHEAD + first,
        (2 * local_station + 1 - half) * AHEAD + first + half,
        base + 2 * PLANE * half,
        base + 2 * PLANE * (1 - half) + half,
        used,
    ]
    packed = jnp.zeros((mine, LANES), jnp.int32)
    for f, values in enumerate(fields):
        kept = jnp.where(lane < slots, values, 0)
        packed = packed + (kept if f == 0 else pltpu.roll(kept, f * slots, 1))
    lists_ref[slab] = packed

    pl.semaphore_wait(barrier, blocks - 1 + outer - 1 + 3)

    def place(block, owner):
        at = (block * slabs + owner) * height
        return panels_ref.at[pl.ds(pl.multiple_of(at, height), height), :]

    def push(source, target, send, recv, device):
        return pltpu.make_async_remote_copy(
            src_ref=source, dst_ref=target, send_sem=send, recv_sem=recv, device_id=device, device_id_type=MESH)

    def owner_of(e, turn):
        return lax.rem((side if turn else slab) + slabs - 4 * e, slabs)

    def halo_copy():
        return push(data_ref.at[:, :reach], ext_ref.at[:, samples:], halo_send, halo_recv, {"slab": lax.rem(slab + slabs - 1, slabs)})

    def far_copy(d):
        return push(place(0, slab), place(0, slab), far_send.at[d], far_recv.at[d], {"slab": lax.rem(slab + 4 * d, slabs)})

    def side_copy(e):
        at = place(0, owner_of(e, 0))
        return push(at, at, side_send.at[e], side_recv.at[e], {"slab": side})

    def peer_copy(d, e, turn):
        at = (d * outer + e) * 2 + turn
        unit = owner_of(e, turn)
        return push(place(0, unit), place(blocks - d, unit), peer_send.at[at], peer_recv.at[at], {"tpl": lax.rem(tpl + d, blocks)})

    def mate_copy(block, e, turn):
        at = (block * outer + e) * 2 + turn
        unit = place(block, owner_of(e, turn))
        return push(unit, unit, mate_send.at[at], mate_recv.at[at], {"slab": mate})

    def list_mate():
        return push(lists_ref.at[slab], lists_ref.at[slab], list_mate_send, list_mate_recv, {"slab": mate})

    def list_far(d):
        at = lists_ref.at[pl.ds(slab - core, 2)]
        return push(at, at, list_far_send.at[d], list_far_recv.at[d], {"slab": lax.rem(slab + 4 * d, slabs)})

    def list_side(e):
        at = lists_ref.at[pl.ds(owner_of(e, 0) - core, 2)]
        return push(at, at, list_side_send.at[e], list_side_recv.at[e], {"slab": side})

    def list_peer(d):
        return push(
            lists_ref.at[pl.ds(0, slabs)], lists_ref.at[pl.ds((blocks - d) * slabs, slabs)],
            list_peer_send.at[d], list_peer_recv.at[d], {"tpl": lax.rem(tpl + d, blocks)})

    def spread(e, turn):
        for d in range(1, blocks):
            peer_copy(d, e, turn).start()
        mate_copy(0, e, turn).start()

    begins = slab == 0
    ends = slab == slabs - 1
    list_mate().start()
    for d in range(1, outer):
        far_copy(d).start()

    @pl.when(jnp.logical_not(begins))
    def _():
        halo_copy().start()

    side_copy(0).start()
    spread(0, 0)
    local[4].wait()

    @pl.when(ends)
    def _():
        ext_ref[:, samples:] = jnp.zeros((rows, reach), ext_ref.dtype)

    list_mate().wait_recv()
    list_side(0).start()
    for d in range(1, outer):
        list_far(d).start()
    for d in range(1, outer):
        far_copy(d).wait_recv()
        side_copy(d).start()
        spread(d, 0)
    for d in range(1, outer):
        list_far(d).wait_recv()
        list_side(d).start()
    for e in range(outer):
        side_copy(e).wait_recv()
        spread(e, 1)
    for e in range(outer):
        list_side(e).wait_recv()
    for d in range(1, blocks):
        list_peer(d).start()
    for turn in range(2):
        for e in range(outer):
            for d in range(1, blocks):
                peer_copy(d, e, turn).wait_recv()
                mate_copy(blocks - d, e, turn).start()
    for d in range(1, blocks):
        list_peer(d).wait_recv()

    @pl.when(jnp.logical_not(ends))
    def _():
        halo_copy().wait_recv()

    near = lists_ref[...]
    lanes = lax.broadcasted_iota(jnp.int32, near.shape, 2)
    table_ref[...] = jnp.where(lanes < slots, jnp.where(near == tpl, 1, 0), near)

    for block in range(blocks):
        for turn in range(2):
            for e in range(outer):
                mate_copy(block, e, turn).wait_recv()

    @pl.when(jnp.logical_not(begins))
    def _():
        halo_copy().wait_send()

    list_mate().wait_send()
    for d in range(1, outer):
        far_copy(d).wait_send()
        list_far(d).wait_send()
    for d in range(1, blocks):
        list_peer(d).wait_send()
    for e in range(outer):
        side_copy(e).wait_send()
        list_side(e).wait_send()
        for turn in range(2):
            for d in range(1, blocks):
                peer_copy(d, e, turn).wait_send()
            for block in range(blocks):
                mate_copy(block, e, turn).wait_send()


def exchange(local, rows, stations, shifts, used, reach, hop):
    slabs = lax.axis_size("slab")
    blocks = lax.axis_size("tpl")
    height, span = rows.shape
    outer = slabs // 4
    anywhere = pl.BlockSpec(memory_space=pl.ANY)
    vmem = pl.BlockSpec(memory_space=pltpu.VMEM)
    dma = pltpu.SemaphoreType.DMA
    one, few, all_units = [dma] * 2, [dma((outer,))] * 2, [dma((blocks * outer * 2,))] * 2
    return pl.pallas_call(
        functools.partial(exchange_kernel, reach, hop),
        out_shape=(
            jax.ShapeDtypeStruct((local.shape[0], local.shape[1] + reach), local.dtype),
            jax.ShapeDtypeStruct((height * slabs * blocks, span), rows.dtype),
            jax.ShapeDtypeStruct((slabs * blocks, stations.shape[0], LANES), jnp.int32),
        ),
        in_specs=[anywhere] * 5,
        out_specs=(vmem, vmem, vmem),
        scratch_shapes=[
            pltpu.VMEM(rows.shape, rows.dtype),
            pltpu.VMEM((slabs * blocks, stations.shape[0], LANES), jnp.int32),
            pltpu.SMEM(stations.shape, jnp.int32),
            pltpu.SMEM(shifts.shape, jnp.int32),
            pltpu.SMEM(used.shape, jnp.int32),
            dma((5,)),
        ] + one + few + few + all_units + all_units + one + few + few + [dma((blocks,))] * 2,
        compiler_params=pltpu.CompilerParams(
            collective_id=0, has_side_effects=True, vmem_limit_bytes=24 << 20
        ),
    )(local, rows, stations, shifts, used)


def window_norms(span, values, band):
    root = math.sqrt(span)
    wide = values.astype(jnp.float32)
    square = wide * wide
    high = square.astype(jnp.bfloat16)
    low = (square - high.astype(jnp.float32)).astype(jnp.bfloat16)
    sums = jnp.dot(values, band, preferred_element_type=jnp.float32)
    squares = jnp.dot(high, band, preferred_element_type=jnp.float32)
    squares += jnp.dot(low, band, preferred_element_type=jnp.float32)
    spread = (squares - sums * sums / span) / span
    inverse = 1.0 / (root * jnp.sqrt(jnp.maximum(spread, 0.0) + EPS))
    return inverse.astype(jnp.bfloat16).astype(jnp.float32)


def turned_tiles(tiles, lane, count):
    for turn in range(TURNS):
        for v in range(count):
            if turn == 0:
                yield turn, v, tiles[v]
            else:
                after = tiles[v + 1] if v + 1 < len(tiles) else jnp.zeros_like(tiles[v])
                yield turn, v, pltpu.roll(jnp.where(lane >= LAGS * turn, tiles[v], after), LANES - LAGS * turn, 1)


def prepare_kernel(span, ext_ref, hankel_ref, norm_ref, wide_ref):
    rows, width = ext_ref.shape
    block = 256
    reach = block + span
    taps = lax.broadcasted_iota(jnp.int32, (reach, block), 0)
    starts = lax.broadcasted_iota(jnp.int32, (reach, block), 1)
    band = jnp.where((taps >= starts) & (taps < starts + span), 1.0, 0.0).astype(jnp.bfloat16)
    nblocks = (width - span) // block
    tiles = width // LANES
    step = 64
    lane = lax.broadcasted_iota(jnp.int32, (step, LANES), 1)

    @pl.loop(0, rows // step)
    def _(s):
        at = pl.ds(pl.multiple_of(s * step, step), step)
        base = pl.multiple_of(s * step * TURNS * PLANE, step * TURNS * PLANE)
        inverse = []
        for n in range(nblocks):
            level = window_norms(span, ext_ref[at, n * block : n * block + reach], band)
            inverse += [level[:, :LANES], level[:, LANES:]]
        for turn, v, tile in turned_tiles(inverse, lane, len(inverse)):
            norm_ref[pl.ds(base + turn * PLANE + v, step, stride=TURNS * PLANE), :] = tile
        for v in range(len(inverse), PLANE):
            for turn in range(TURNS):
                norm_ref[pl.ds(base + turn * PLANE + v, step, stride=TURNS * PLANE), :] = jnp.zeros((step, LANES), jnp.float32)
        samples = [ext_ref[at, v * LANES : (v + 1) * LANES].astype(jnp.float32) for v in range(tiles)]
        for turn, v, tile in turned_tiles(samples, lane, tiles):
            wide_ref[pl.ds(turn * PLANE + v, step, stride=TURNS * PLANE), :] = tile

        @pl.loop(0, step)
        def _(r):
            top = pl.multiple_of(r * TURNS * PLANE, TURNS * PLANE)
            to = (s * step + r) * 2 * AHEAD
            for pair in range(2):
                for ahead in range(AHEAD):
                    parts = [wide_ref[pl.ds(top + (2 * pair + t) * PLANE + ahead, 8), :] for t in range(2)]
                    hankel_ref[to + pair * AHEAD + ahead] = jnp.concatenate(parts, axis=0).astype(jnp.bfloat16)


def prepare(ext, span):
    rows, width = ext.shape
    vmem = pl.BlockSpec(memory_space=pltpu.VMEM)
    return pl.pallas_call(
        functools.partial(prepare_kernel, span),
        out_shape=(
            jax.ShapeDtypeStruct((rows * 2 * AHEAD, 16, LANES), jnp.bfloat16),
            jax.ShapeDtypeStruct((rows * TURNS * PLANE, LANES), jnp.float32),
        ),
        in_specs=[vmem],
        out_specs=(vmem, vmem),
        scratch_shapes=[pltpu.VMEM((64 * TURNS * PLANE, LANES), jnp.float32)],
        compiler_params=pltpu.CompilerParams(vmem_limit_bytes=24 << 20),
    )(ext)


def stack_kernel(span, comps, hop, slots, panel, block, table_ref, hankel_ref, norm_ref, panels_ref, out_ref,
                 unit_ref, turned_ref, right_ref, level_ref, sum_ref, done_ref, item_ref):
    parts = span // LANES
    group = comps * slots
    count = panel * slots

    height = 2 * group
    @pl.loop(0, panel // 2)
    def _(step):
        at = pl.ds(pl.multiple_of((block * panel + 2 * step) * group, height), height)
        values = panels_ref[at, :].astype(jnp.float32)
        for t in range(2):
            for c in range(comps):
                for part in range(parts):
                    piece = values[t * group + c * slots : t * group + (c + 1) * slots, part * LANES : (part + 1) * LANES]
                    unit_ref[pl.ds((step * 2 + t) * slots * PLANE + c * parts + part, slots, stride=PLANE), :] = piece

    unit_ref[count * PLANE : (count + 1) * PLANE, :] = jnp.zeros((PLANE, LANES), jnp.float32)

    def collect(j, total):
        sum_ref[j] = jnp.zeros((TURNS * 8, LAGS), jnp.float32)
        for k in range(slots):
            item_ref[total] = j * LANES + k
            total = total + table_ref[j * LANES + k]
        return total

    total = lax.fori_loop(0, panel, collect, 0)
    for k in range(2 * PASS):
        item_ref[total + k] = panel * LANES
    sum_ref[panel] = jnp.zeros((TURNS * 8, LAGS), jnp.float32)

    lane_half = lax.broadcasted_iota(jnp.int32, (16, LANES), 1).astype(jnp.float32).astype(jnp.bfloat16)
    lag_half = lax.broadcasted_iota(jnp.int32, (16, LANES), 0).astype(jnp.float32).astype(jnp.bfloat16)
    ahead = lane_half - lag_half
    further = ahead - jnp.full((16, LANES), 16.0, jnp.bfloat16)
    none = jnp.zeros((16, LANES), jnp.bfloat16)

    def field(g, n, which):
        return table_ref[item_ref[g * PASS + n] + which * slots]

    def turn_rows(g):
        for n in range(PASS):
            item = item_ref[g * PASS + n]
            slot = lax.shift_right_logical(item, 7) * slots + lax.bitwise_and(item, LANES - 1)
            rows = unit_ref[pl.ds(pl.multiple_of(slot * PLANE, PLANE), PLANE), :]
            turned_ref[n * PLANE : (n + 1) * PLANE, :] = pltpu.roll(rows, field(g, n, 1), 1)

    def build_slot(g, n):
        bound = jnp.full((16, LANES), field(g, n, 1), jnp.int32).astype(jnp.float32).astype(jnp.bfloat16)
        inside = [ahead >= bound, further >= bound]
        for c in range(comps):
            turned = []
            for part in range(parts):
                line = jnp.broadcast_to(turned_ref[n * PLANE + c * parts + part : n * PLANE + c * parts + part + 1, :], (8, LANES))
                lags = pltpu.roll(line, 0, 1, stride=1, stride_axis=0)
                low = jnp.concatenate([lags, pltpu.roll(lags, 8, 1)], axis=0).astype(jnp.bfloat16)
                turned.append((low, pltpu.roll(low, 16, 1)))
            edges = [(none, none)] + turned + [(none, none)]
            at = (n * comps + c) * LAGS
            for b in range(2):
                for p in range(parts + 1):
                    right_ref[at + 16 * b : at + 16 * b + 16, p * LANES : (p + 1) * LANES] = jnp.where(inside[b], edges[p + 1][b], edges[p][b])
        back = LANES - field(g, n, 1)
        for turn in range(TURNS):
            at = field(g, n, 4 + turn // 2)
            for c in range(comps):
                norm = norm_ref[pl.ds(at + c * hop * TURNS * PLANE + (turn % 2) * PLANE, 8), :]
                k = (n * comps + c) * TURNS + turn
                level_ref[k * 8 : k * 8 + 8, :] = pltpu.roll(norm, back, 1)

    def build(g):
        turn_rows(g)
        for n in range(PASS):
            build_slot(g, n)

    def multiply(g):
        for n in range(PASS):
            near = field(g, n, 2)
            far = field(g, n, 3)
            for c in range(comps):
                i = n * comps + c
                left = jnp.concatenate([
                    jnp.concatenate([hankel_ref[at + c * hop * 2 * AHEAD + p] for p in range(CHUNKS)], axis=1)
                    for at in (near, far)], axis=0)
                yield n, c, lax.dot_general(
                    left, right_ref[i * LAGS : (i + 1) * LAGS, :],
                    (((1,), (1,)), ((), ())), preferred_element_type=jnp.float32)

    def gather_slot(g, n, product):
        j = lax.shift_right_logical(item_ref[g * PASS + n], 7)
        added = []
        for turn in range(TURNS):
            value = None
            for c in range(comps):
                k = (n * comps + c) * TURNS + turn
                term = product(n, c, turn) * level_ref[k * 8 : k * 8 + 8, :LAGS]
                value = term if value is None else value + term
            added.append(value)
        sum_ref[j] += jnp.concatenate(added, axis=0)

    build(0)

    def body(g, _):
        products = {}
        for n, c, product in multiply(g):
            products[n, c] = product
            if c == comps - 1:
                gather_slot(g, n, lambda n, c, turn: products[n, c][8 * turn : 8 * turn + 8, :])
        build(g + 1)
        return 0

    lax.fori_loop(0, lax.div(total + PASS - 1, PASS), body, 0)

    def finish(j, _):
        value = sum_ref[j]
        result = jnp.concatenate([value[8 * turn : 8 * turn + 8, :] for turn in range(TURNS)], axis=1)
        used = jnp.full((8, LANES), table_ref[j * LANES + (FIELDS - 1) * slots], jnp.int32).astype(jnp.float32)
        done_ref[pl.ds(pl.multiple_of(j * 8, 8), 8), :] = result * jnp.sqrt(span / (3.0 * used))
        return 0

    lax.fori_loop(0, panel, finish, 0, unroll=4)
    for b in range(panel // 8):
        for a in range(out_ref.shape[1] // LANES):
            out_ref[b * 8 : b * 8 + 8, a * LANES : (a + 1) * LANES] = done_ref[pl.ds(b * 64 + a, 8, stride=8), :]


def stack(table, hankel, norm, panels, block, panel, slots, comps, hop, span, samples):
    smem = pl.BlockSpec(memory_space=pltpu.SMEM)
    vmem = pl.BlockSpec(memory_space=pltpu.VMEM)
    count = panel * slots
    return pl.pallas_call(
        functools.partial(stack_kernel, span, comps, hop, slots, panel, block),
        out_shape=jax.ShapeDtypeStruct((panel, samples), jnp.float32),
        in_specs=[smem, vmem, vmem, vmem],
        out_specs=vmem,
        scratch_shapes=[
            pltpu.VMEM(((count + 1) * PLANE, LANES), jnp.float32),
            pltpu.VMEM((PASS * PLANE, LANES), jnp.float32),
            pltpu.VMEM((PASS * comps * LAGS, CHUNKS * LANES), jnp.bfloat16),
            pltpu.VMEM((PASS * comps * TURNS * 8, LANES), jnp.float32),
            pltpu.VMEM((panel + 1, TURNS * 8, LAGS), jnp.float32),
            pltpu.VMEM((panel * 8, LANES), jnp.float32),
            pltpu.SMEM((count + 3 * PASS,), jnp.int32),
        ],
        compiler_params=pltpu.CompilerParams(vmem_limit_bytes=(count * PLANE * LANES * 4) + (8 << 20)),
        cost_estimate=pl.CostEstimate(flops=6_000_000_000, bytes_accessed=20_000_000, transcendentals=0),
    )(table, hankel, norm, panels)


def per_device(data, templates, stations, shifts, used):
    mine, slots, comps, span = templates.shape
    hop, _, samples = data.shape
    reach = span + MAXSHIFT
    slabs = lax.axis_size("slab")
    blocks = lax.axis_size("tpl")
    local = jnp.transpose(data, (1, 0, 2)).reshape(-1, samples)
    rows = jnp.transpose(templates, (0, 2, 1, 3)).reshape(-1, span)
    ext, panels, lists = exchange(local, rows, stations, shifts, used, reach, hop)
    hankel, norm = prepare(ext, span)
    panel = mine * slabs
    tables = lists.reshape(blocks, panel * LANES)
    tables = jnp.pad(tables, ((0, 0), (0, LANES)))

    def part(block):
        return stack(tables[block], hankel, norm, panels, block, panel, slots, comps, hop, span, samples)

    sent = []
    for d in range(1, blocks):
        pairs = [(t, (t + d) % blocks) for t in range(blocks)]
        sent.append(lax.ppermute(part(d), "tpl", pairs))
    total = part(0)
    for piece in sent:
        total = total + piece
    return total


def solution(mesh):
    return jax.shard_map(
        per_device,
        mesh=mesh,
        in_specs=(
            P("tpl", None, "slab"),
            P(("tpl", "slab"), None, None, None),
            P(("tpl", "slab"), None),
            P(("tpl", "slab"), None),
            P(("tpl", "slab")),
        ),
        out_specs=P("tpl", "slab"),
        check_vma=False,
    )
```

```python
import functools
import math

import jax
import jax.numpy as jnp
from jax import lax
from jax.experimental import pallas as pl
from jax.experimental.pallas import tpu as pltpu
from jax.sharding import PartitionSpec as P

MAXSHIFT = 256
EPS = 1e-05
MESH = pl.DeviceIdType.MESH

LANES = 128
LAGS = 32
TURNS = LANES // LAGS
PASS = 6
PLANE = 16
CHUNKS = 5
AHEAD = 7
FIELDS = 7


def normalized(rows):
    span = rows.shape[-1]
    centered = rows - jnp.mean(rows, axis=-1, keepdims=True)
    rms = jnp.sqrt(jnp.mean(centered * centered, axis=-1, keepdims=True) + EPS)
    return (centered / (rms * math.sqrt(span))).astype(jnp.bfloat16)


def exchange_kernel(reach, hop, data_ref, templates_ref, stations_ref, shifts_ref, used_ref, ext_ref, panels_ref, table_ref, *scratch):
    rows_ref, lists_ref, sta_ref, shf_ref, use_ref, loads = scratch[:6]
    halo_send, halo_recv, far_send, far_recv, side_send, side_recv, peer_send, peer_recv, mate_send, mate_recv = scratch[6:16]
    list_mate_send, list_mate_recv, list_far_send, list_far_recv, list_side_send, list_side_recv, list_peer_send, list_peer_recv = scratch[16:]
    rows, samples = data_ref.shape
    height = templates_ref.shape[0]
    mine, slots = stations_ref.shape
    slabs = lax.axis_size("slab")
    blocks = lax.axis_size("tpl")
    outer = slabs // 4
    slab = lax.axis_index("slab")
    tpl = lax.axis_index("tpl")
    core = lax.rem(slab, 2)
    mate = slab + 1 - 2 * core
    side = slab + 2 - 4 * lax.rem(slab // 2, 2)
    beside = lax.rem(slab + slabs - 1 + 2 * core, slabs)

    local = [
        pltpu.make_async_copy(templates_ref, rows_ref, loads.at[0]),
        pltpu.make_async_copy(stations_ref, sta_ref, loads.at[1]),
        pltpu.make_async_copy(shifts_ref, shf_ref, loads.at[2]),
        pltpu.make_async_copy(used_ref, use_ref, loads.at[3]),
        pltpu.make_async_copy(data_ref, ext_ref.at[:, :samples], loads.at[4]),
    ]
    for copy in local:
        copy.start()

    barrier = pltpu.get_barrier_semaphore()
    for d in range(1, blocks):
        pl.semaphore_signal(barrier, inc=1, device_id={"tpl": lax.rem(tpl + d, blocks)}, device_id_type=MESH)
    for d in range(1, outer):
        pl.semaphore_signal(barrier, inc=1, device_id={"slab": lax.rem(slab + 4 * d, slabs)}, device_id_type=MESH)
    for device in (mate, side, beside):
        pl.semaphore_signal(barrier, inc=1, device_id={"slab": device}, device_id_type=MESH)

    local[0].wait()
    panels_ref[pl.ds(pl.multiple_of(slab * height, height), height), :] = normalized(rows_ref[...].astype(jnp.float32))
    for copy in local[1:4]:
        copy.wait()
    lane = lax.broadcasted_iota(jnp.int32, (mine, LANES), 1)
    line = lax.broadcasted_iota(jnp.int32, (mine, LANES), 0)
    station = jnp.zeros((mine, LANES), jnp.int32)
    shift = jnp.zeros((mine, LANES), jnp.int32)
    used = jnp.zeros((mine, LANES), jnp.int32)
    for j in range(mine):
        used = jnp.where(line == j, use_ref[j], used)
        for k in range(slots):
            spot = jnp.logical_and(line == j, lane == k)
            station = jnp.where(spot, sta_ref[j, k], station)
            shift = jnp.where(spot, shf_ref[j, k], shift)
    owner = lax.div(station, hop)
    local_station = station - owner * hop
    half = lax.bitwise_and(lax.shift_right_logical(shift, 6), 1)
    first = lax.shift_right_logical(shift, 7)
    base = local_station * (TURNS * PLANE) + first
    fields = [
        jnp.where(lane < used, owner, -1),
        lax.bitwise_and(shift, 63),
        (2 * local_station + half) * AHEAD + first,
        (2 * local_station + 1 - half) * AHEAD + first + half,
        base + 2 * PLANE * half,
        base + 2 * PLANE * (1 - half) + half,
        used,
    ]
    packed = jnp.zeros((mine, LANES), jnp.int32)
    for f, values in enumerate(fields):
        kept = jnp.where(lane < slots, values, 0)
        packed = packed + (kept if f == 0 else pltpu.roll(kept, f * slots, 1))
    lists_ref[slab] = packed

    pl.semaphore_wait(barrier, blocks - 1 + outer - 1 + 3)

    def place(block, owner):
        at = (block * slabs + owner) * height
        return panels_ref.at[pl.ds(pl.multiple_of(at, height), height), :]

    def push(source, target, send, recv, device):
        return pltpu.make_async_remote_copy(
            src_ref=source, dst_ref=target, send_sem=send, recv_sem=recv, device_id=device, device_id_type=MESH)

    def owner_of(e, turn):
        return lax.rem((side if turn else slab) + slabs - 4 * e, slabs)

    def halo_copy():
        return push(data_ref.at[:, :reach], ext_ref.at[:, samples:], halo_send, halo_recv, {"slab": lax.rem(slab + slabs - 1, slabs)})

    def far_copy(d):
        return push(place(0, slab), place(0, slab), far_send.at[d], far_recv.at[d], {"slab": lax.rem(slab + 4 * d, slabs)})

    def side_copy(e):
        at = place(0, owner_of(e, 0))
        return push(at, at, side_send.at[e], side_recv.at[e], {"slab": side})

    def peer_copy(d, e, turn):
        at = (d * outer + e) * 2 + turn
        unit = owner_of(e, turn)
        return push(place(0, unit), place(blocks - d, unit), peer_send.at[at], peer_recv.at[at], {"tpl": lax.rem(tpl + d, blocks)})

    def mate_copy(block, e, turn):
        at = (block * outer + e) * 2 + turn
        unit = place(block, owner_of(e, turn))
        return push(unit, unit, mate_send.at[at], mate_recv.at[at], {"slab": mate})

    def list_mate():
        return push(lists_ref.at[slab], lists_ref.at[slab], list_mate_send, list_mate_recv, {"slab": mate})

    def list_far(d):
        at = lists_ref.at[pl.ds(slab - core, 2)]
        return push(at, at, list_far_send.at[d], list_far_recv.at[d], {"slab": lax.rem(slab + 4 * d, slabs)})

    def list_side(e):
        at = lists_ref.at[pl.ds(owner_of(e, 0) - core, 2)]
        return push(at, at, list_side_send.at[e], list_side_recv.at[e], {"slab": side})

    def list_peer(d):
        return push(
            lists_ref.at[pl.ds(0, slabs)], lists_ref.at[pl.ds((blocks - d) * slabs, slabs)],
            list_peer_send.at[d], list_peer_recv.at[d], {"tpl": lax.rem(tpl + d, blocks)})

    def spread(e, turn):
        for d in range(1, blocks):
            peer_copy(d, e, turn).start()
        mate_copy(0, e, turn).start()

    begins = slab == 0
    ends = slab == slabs - 1
    list_mate().start()
    for d in range(1, outer):
        far_copy(d).start()

    @pl.when(jnp.logical_not(begins))
    def _():
        halo_copy().start()

    side_copy(0).start()
    spread(0, 0)
    local[4].wait()

    @pl.when(ends)
    def _():
        ext_ref[:, samples:] = jnp.zeros((rows, reach), ext_ref.dtype)

    list_mate().wait_recv()
    list_side(0).start()
    for d in range(1, outer):
        list_far(d).start()
    for d in range(1, outer):
        far_copy(d).wait_recv()
        side_copy(d).start()
        spread(d, 0)
    for d in range(1, outer):
        list_far(d).wait_recv()
        list_side(d).start()
    for e in range(outer):
        side_copy(e).wait_recv()
        spread(e, 1)
    for e in range(outer):
        list_side(e).wait_recv()
    for d in range(1, blocks):
        list_peer(d).start()
    for turn in range(2):
        for e in range(outer):
            for d in range(1, blocks):
                peer_copy(d, e, turn).wait_recv()
                mate_copy(blocks - d, e, turn).start()
    for d in range(1, blocks):
        list_peer(d).wait_recv()

    @pl.when(jnp.logical_not(ends))
    def _():
        halo_copy().wait_recv()

    near = lists_ref[...]
    lanes = lax.broadcasted_iota(jnp.int32, near.shape, 2)
    table_ref[...] = jnp.where(lanes < slots, jnp.where(near == tpl, 1, 0), near)

    for block in range(blocks):
        for turn in range(2):
            for e in range(outer):
                mate_copy(block, e, turn).wait_recv()

    @pl.when(jnp.logical_not(begins))
    def _():
        halo_copy().wait_send()

    list_mate().wait_send()
    for d in range(1, outer):
        far_copy(d).wait_send()
        list_far(d).wait_send()
    for d in range(1, blocks):
        list_peer(d).wait_send()
    for e in range(outer):
        side_copy(e).wait_send()
        list_side(e).wait_send()
        for turn in range(2):
            for d in range(1, blocks):
                peer_copy(d, e, turn).wait_send()
            for block in range(blocks):
                mate_copy(block, e, turn).wait_send()


def exchange(local, rows, stations, shifts, used, reach, hop):
    slabs = lax.axis_size("slab")
    blocks = lax.axis_size("tpl")
    height, span = rows.shape
    outer = slabs // 4
    vmem = pl.BlockSpec(memory_space=pltpu.VMEM)
    dma = pltpu.SemaphoreType.DMA
    one, few, all_units = [dma] * 2, [dma((outer,))] * 2, [dma((blocks * outer * 2,))] * 2
    return pl.pallas_call(
        functools.partial(exchange_kernel, reach, hop),
        out_shape=(
            jax.ShapeDtypeStruct((local.shape[0], local.shape[1] + reach), local.dtype),
            jax.ShapeDtypeStruct((height * slabs * blocks, span), rows.dtype),
            jax.ShapeDtypeStruct((slabs * blocks, stations.shape[0], LANES), jnp.int32),
        ),
        in_specs=[pl.BlockSpec(memory_space=pltpu.HBM)] * 5,
        out_specs=(vmem, vmem, vmem),
        scratch_shapes=[
            pltpu.VMEM(rows.shape, rows.dtype),
            pltpu.VMEM((slabs * blocks, stations.shape[0], LANES), jnp.int32),
            pltpu.SMEM(stations.shape, jnp.int32),
            pltpu.SMEM(shifts.shape, jnp.int32),
            pltpu.SMEM(used.shape, jnp.int32),
            dma((5,)),
        ] + one + few + few + all_units + all_units + one + few + few + [dma((blocks,))] * 2,
        compiler_params=pltpu.CompilerParams(
            collective_id=0, has_side_effects=True, vmem_limit_bytes=24 << 20
        ),
    )(local, rows, stations, shifts, used)


def fill(span, step, s, ext_ref, hankel_ref, norm_ref, plain_ref, turned_ref):
    width = ext_ref.shape[1]
    block = 256
    near = span // block
    nblocks = (width - span) // block
    tiles = width // LANES
    taps = lax.broadcasted_iota(jnp.int32, (block, block), 0)
    starts = lax.broadcasted_iota(jnp.int32, (block, block), 1)
    tail = jnp.where(taps >= starts, 1.0, 0.0).astype(jnp.bfloat16)
    head = jnp.where(taps < starts, 1.0, 0.0).astype(jnp.bfloat16)
    at = pl.ds(pl.multiple_of(s * step, step), step)
    stride = TURNS * PLANE
    base = pl.multiple_of(s * step * stride, step * stride)

    plain, both = [], []
    for n in range(width // block):
        values = ext_ref[at, n * block : (n + 1) * block]
        wide = values.astype(jnp.float32)
        for half in range(block // LANES):
            v = n * (block // LANES) + half
            plain_ref[pl.ds(v, step, stride=PLANE), :] = wide[:, half * LANES : (half + 1) * LANES]
        square = wide * wide
        high = square.astype(jnp.bfloat16)
        low = (square - high.astype(jnp.float32)).astype(jnp.bfloat16)
        plain.append(values)
        both.append(jnp.concatenate([high, low], axis=1))
    for v in range(tiles, PLANE):
        plain_ref[pl.ds(v, step, stride=PLANE), :] = jnp.zeros((step, LANES), jnp.float32)

    def window(pieces, weight):
        tails = jnp.dot(jnp.concatenate(pieces[:-1], axis=0), jnp.concatenate([tail] * weight, axis=0), preferred_element_type=jnp.float32)
        heads = jnp.dot(jnp.concatenate(pieces[near:], axis=0), jnp.concatenate([head] * weight, axis=0), preferred_element_type=jnp.float32)
        for n in range(nblocks):
            total = tails[n * step : (n + 1) * step, :] + heads[n * step : (n + 1) * step, :]
            for m in range(n + 1, n + near):
                total = total + tails[m * step : (m + 1) * step, :1]
            yield total

    for n, (sums, squares) in enumerate(zip(window(plain, 1), window(both, 2))):
        spread = (squares - sums * sums / span) / span
        inverse = lax.rsqrt(jnp.maximum(spread, 0.0) + EPS) * (1.0 / math.sqrt(span))
        inverse = inverse.astype(jnp.bfloat16).astype(jnp.float32)
        for half in range(block // LANES):
            v = n * (block // LANES) + half
            norm_ref[pl.ds(base + v, step, stride=stride), :] = inverse[:, half * LANES : (half + 1) * LANES]

    lane = lax.broadcasted_iota(jnp.int32, (PLANE, LANES), 1)
    several = 4

    @pl.loop(0, step // several)
    def _(group):
        for q in range(several):
            r = group * several + q
            top = pl.multiple_of(r * PLANE, PLANE)
            here = plain_ref[pl.ds(top, PLANE), :]
            after = plain_ref[pl.ds(top + 1, PLANE), :]
            level_at = pl.multiple_of(base + r * stride, stride)
            level = norm_ref[pl.ds(level_at, PLANE), :]
            level_after = norm_ref[pl.ds(level_at + 1, PLANE), :]
            for turn in range(1, TURNS):
                keep = lane >= LAGS * turn
                back = LANES - LAGS * turn
                turned_ref[(q * TURNS + turn) * PLANE : (q * TURNS + turn + 1) * PLANE, :] = pltpu.roll(jnp.where(keep, here, after), back, 1)
                level_to = pl.ds(pl.multiple_of(level_at + turn * PLANE, PLANE), PLANE)
                norm_ref[level_to, :] = pltpu.roll(jnp.where(keep, level, level_after), back, 1)
        for q in range(several):
            r = group * several + q
            to = (s * step + r) * 2 * AHEAD
            for pair in range(2):
                for ahead in range(AHEAD):
                    parts = []
                    for turn in (2 * pair, 2 * pair + 1):
                        if turn == 0:
                            parts.append(plain_ref[pl.ds(r * PLANE + ahead, 8), :])
                        else:
                            rows = (q * TURNS + turn) * PLANE + ahead
                            parts.append(turned_ref[rows : rows + 8, :])
                    hankel_ref[to + pair * AHEAD + ahead] = jnp.concatenate(parts, axis=0).astype(jnp.bfloat16)


def prepare_kernel(span, ext_ref, hankel_ref, norm_ref, plain_ref, turned_ref):
    step = 64

    @pl.loop(0, ext_ref.shape[0] // step)
    def _(s):
        fill(span, step, s, ext_ref, hankel_ref, norm_ref, plain_ref, turned_ref)


def prepare(ext, span):
    rows, width = ext.shape
    vmem = pl.BlockSpec(memory_space=pltpu.VMEM)
    return pl.pallas_call(
        functools.partial(prepare_kernel, span),
        out_shape=(
            jax.ShapeDtypeStruct((rows * 2 * AHEAD, 16, LANES), jnp.bfloat16),
            jax.ShapeDtypeStruct((rows * TURNS * PLANE, LANES), jnp.float32),
        ),
        in_specs=[vmem],
        out_specs=(vmem, vmem),
        scratch_shapes=[
            pltpu.VMEM((65 * PLANE, LANES), jnp.float32),
            pltpu.VMEM((4 * TURNS * PLANE, LANES), jnp.float32),
        ],
        compiler_params=pltpu.CompilerParams(vmem_limit_bytes=24 << 20),
    )(ext)


def stack_kernel(span, comps, hop, slots, panel, block, table_ref, hankel_ref, norm_ref, panels_ref, out_ref,
                 hankel_out_ref, norm_out_ref, unit_ref, turned_ref, right_ref, level_ref, sum_ref, done_ref, item_ref):
    parts = span // LANES
    group = comps * slots
    count = panel * slots

    height = 2 * group
    @pl.loop(0, panel // 2)
    def _(step):
        at = pl.ds(pl.multiple_of((block * panel + 2 * step) * group, height), height)
        values = panels_ref[at, :].astype(jnp.float32)
        for t in range(2):
            for c in range(comps):
                for part in range(parts):
                    piece = values[t * group + c * slots : t * group + (c + 1) * slots, part * LANES : (part + 1) * LANES]
                    unit_ref[pl.ds((step * 2 + t) * slots * PLANE + c * parts + part, slots, stride=PLANE), :] = piece

    unit_ref[count * PLANE : (count + 1) * PLANE, :] = jnp.zeros((PLANE, LANES), jnp.float32)

    def collect(j, total):
        sum_ref[j] = jnp.zeros((TURNS * 8, LAGS), jnp.float32)
        for k in range(slots):
            item_ref[total] = j * LANES + k
            total = total + table_ref[j * LANES + k]
        return total

    total = lax.fori_loop(0, panel, collect, 0)
    for k in range(2 * PASS):
        item_ref[total + k] = panel * LANES
    sum_ref[panel] = jnp.zeros((TURNS * 8, LAGS), jnp.float32)

    lane_half = lax.broadcasted_iota(jnp.int32, (16, LANES), 1).astype(jnp.float32).astype(jnp.bfloat16)
    lag_half = lax.broadcasted_iota(jnp.int32, (16, LANES), 0).astype(jnp.float32).astype(jnp.bfloat16)
    ahead = lane_half - lag_half
    further = ahead - jnp.full((16, LANES), 16.0, jnp.bfloat16)
    none = jnp.zeros((16, LANES), jnp.bfloat16)

    def field(g, n, which):
        return table_ref[item_ref[g * PASS + n] + which * slots]

    def turn_rows(g):
        for n in range(PASS):
            item = item_ref[g * PASS + n]
            slot = lax.shift_right_logical(item, 7) * slots + lax.bitwise_and(item, LANES - 1)
            rows = unit_ref[pl.ds(pl.multiple_of(slot * PLANE, PLANE), PLANE), :]
            turned_ref[n * PLANE : (n + 1) * PLANE, :] = pltpu.roll(rows, field(g, n, 1), 1)

    def build_slot(g, n):
        bound = jnp.full((16, LANES), field(g, n, 1), jnp.int32).astype(jnp.float32).astype(jnp.bfloat16)
        inside = [ahead >= bound, further >= bound]
        for c in range(comps):
            turned = []
            for part in range(parts):
                line = jnp.broadcast_to(turned_ref[n * PLANE + c * parts + part : n * PLANE + c * parts + part + 1, :], (8, LANES))
                lags = pltpu.roll(line, 0, 1, stride=1, stride_axis=0)
                low = jnp.concatenate([lags, pltpu.roll(lags, 8, 1)], axis=0).astype(jnp.bfloat16)
                turned.append((low, pltpu.roll(low, 16, 1)))
            edges = [(none, none)] + turned + [(none, none)]
            at = (n * comps + c) * LAGS
            for b in range(2):
                for p in range(parts + 1):
                    right_ref[at + 16 * b : at + 16 * b + 16, p * LANES : (p + 1) * LANES] = jnp.where(inside[b], edges[p + 1][b], edges[p][b])
        back = LANES - field(g, n, 1)
        for turn in range(TURNS):
            at = field(g, n, 4 + turn // 2)
            for c in range(comps):
                norm = norm_ref[pl.ds(at + c * hop * TURNS * PLANE + (turn % 2) * PLANE, 8), :]
                k = (n * comps + c) * TURNS + turn
                level_ref[k * 8 : k * 8 + 8, :] = pltpu.roll(norm, back, 1)

    def build(g):
        turn_rows(g)
        for n in range(PASS):
            build_slot(g, n)

    def multiply(g):
        for n in range(PASS):
            near = field(g, n, 2)
            far = field(g, n, 3)
            for c in range(comps):
                i = n * comps + c
                left = jnp.concatenate([
                    jnp.concatenate([hankel_ref[at + c * hop * 2 * AHEAD + p] for p in range(CHUNKS)], axis=1)
                    for at in (near, far)], axis=0)
                yield n, c, lax.dot_general(
                    left, right_ref[i * LAGS : (i + 1) * LAGS, :],
                    (((1,), (1,)), ((), ())), preferred_element_type=jnp.float32)

    def gather_slot(g, n, product):
        j = lax.shift_right_logical(item_ref[g * PASS + n], 7)
        added = []
        for turn in range(TURNS):
            value = None
            for c in range(comps):
                k = (n * comps + c) * TURNS + turn
                term = product(n, c, turn) * level_ref[k * 8 : k * 8 + 8, :LAGS]
                value = term if value is None else value + term
            added.append(value)
        sum_ref[j] += jnp.concatenate(added, axis=0)

    build(0)

    def body(g, _):
        products = {}
        for n, c, product in multiply(g):
            products[n, c] = product
            if c == comps - 1:
                gather_slot(g, n, lambda n, c, turn: products[n, c][8 * turn : 8 * turn + 8, :])
        build(g + 1)
        return 0

    lax.fori_loop(0, lax.div(total + PASS - 1, PASS), body, 0)

    def finish(j, _):
        value = sum_ref[j]
        result = jnp.concatenate([value[8 * turn : 8 * turn + 8, :] for turn in range(TURNS)], axis=1)
        used = jnp.full((8, LANES), table_ref[j * LANES + (FIELDS - 1) * slots], jnp.int32).astype(jnp.float32)
        done_ref[pl.ds(pl.multiple_of(j * 8, 8), 8), :] = result * jnp.sqrt(span / (3.0 * used))
        return 0

    lax.fori_loop(0, panel, finish, 0, unroll=4)
    for b in range(panel // 8):
        for a in range(out_ref.shape[1] // LANES):
            out_ref[b * 8 : b * 8 + 8, a * LANES : (a + 1) * LANES] = done_ref[pl.ds(b * 64 + a, 8, stride=8), :]


def stack(table, hankel, norm, panels, block, panel, slots, comps, hop, span, samples):
    smem = pl.BlockSpec(memory_space=pltpu.SMEM)
    vmem = pl.BlockSpec(memory_space=pltpu.VMEM)
    count = panel * slots
    return pl.pallas_call(
        functools.partial(stack_kernel, span, comps, hop, slots, panel, block),
        out_shape=(
            jax.ShapeDtypeStruct((panel, samples), jnp.float32),
            jax.ShapeDtypeStruct(hankel.shape, hankel.dtype),
            jax.ShapeDtypeStruct(norm.shape, norm.dtype),
        ),
        in_specs=[smem, vmem, vmem, vmem],
        out_specs=(vmem, vmem, vmem),
        input_output_aliases={1: 1, 2: 2},
        scratch_shapes=[
            pltpu.VMEM(((count + 1) * PLANE, LANES), jnp.float32),
            pltpu.VMEM((PASS * PLANE, LANES), jnp.float32),
            pltpu.VMEM((PASS * comps * LAGS, CHUNKS * LANES), jnp.bfloat16),
            pltpu.VMEM((PASS * comps * TURNS * 8, LANES), jnp.float32),
            pltpu.VMEM((panel + 1, TURNS * 8, LAGS), jnp.float32),
            pltpu.VMEM((panel * 8, LANES), jnp.float32),
            pltpu.SMEM((count + 3 * PASS,), jnp.int32),
        ],
        compiler_params=pltpu.CompilerParams(vmem_limit_bytes=(count * PLANE * LANES * 4) + (8 << 20)),
        cost_estimate=pl.CostEstimate(flops=6_000_000_000, bytes_accessed=20_000_000, transcendentals=0),
    )(table, hankel, norm, panels)


def per_device(data, templates, stations, shifts, used):
    mine, slots, comps, span = templates.shape
    hop, _, samples = data.shape
    reach = span + MAXSHIFT
    slabs = lax.axis_size("slab")
    blocks = lax.axis_size("tpl")
    local = jnp.transpose(data, (1, 0, 2)).reshape(-1, samples)
    rows = jnp.transpose(templates, (0, 2, 1, 3)).reshape(-1, span)
    inputs = [pltpu.with_memory_space_constraint(x, pltpu.HBM) for x in (local, rows, stations, shifts, used)]
    ext, panels, lists = exchange(*inputs, reach, hop)
    hankel, norm = prepare(ext, span)
    panel = mine * slabs
    tables = lists.reshape(blocks, panel * LANES)
    tables = jnp.pad(tables, ((0, 0), (0, LANES)))

    sent = []
    for d in range(1, blocks + 1):
        block = d % blocks
        total, hankel, norm = stack(tables[block], hankel, norm, panels, block, panel, slots, comps, hop, span, samples)
        if block:
            pairs = [(t, (t + d) % blocks) for t in range(blocks)]
            sent.append(lax.ppermute(total, "tpl", pairs))
    for piece in sent:
        total = total + piece
    return total


def solution(mesh):
    return jax.shard_map(
        per_device,
        mesh=mesh,
        in_specs=(
            P("tpl", None, "slab"),
            P(("tpl", "slab"), None, None, None),
            P(("tpl", "slab"), None),
            P(("tpl", "slab"), None),
            P(("tpl", "slab")),
        ),
        out_specs=P("tpl", "slab"),
        check_vma=False,
    )
```

```python
import functools
import math

import jax
import jax.numpy as jnp
from jax import lax
from jax.experimental import pallas as pl
from jax.experimental.pallas import tpu as pltpu
from jax.sharding import PartitionSpec as P

MAXSHIFT = 256
EPS = 1e-05
MESH = pl.DeviceIdType.MESH

LANES = 128
LAGS = 32
TURNS = LANES // LAGS
PASS = 6
PLANE = 16
CHUNKS = 5
AHEAD = 7
FIELDS = 7
STEPS = 4
SEVERAL = 4


def normalized(rows):
    span = rows.shape[-1]
    centered = rows - jnp.mean(rows, axis=-1, keepdims=True)
    rms = jnp.sqrt(jnp.mean(centered * centered, axis=-1, keepdims=True) + EPS)
    return (centered / (rms * math.sqrt(span))).astype(jnp.bfloat16)


def fill(span, step, s, ext_ref, hankel_ref, norm_ref, plain_ref, turned_ref):
    width = ext_ref.shape[1]
    block = 256
    near = span // block
    nblocks = (width - span) // block
    tiles = width // LANES
    taps = lax.broadcasted_iota(jnp.int32, (block, block), 0)
    starts = lax.broadcasted_iota(jnp.int32, (block, block), 1)
    tail = jnp.where(taps >= starts, 1.0, 0.0).astype(jnp.bfloat16)
    head = jnp.where(taps < starts, 1.0, 0.0).astype(jnp.bfloat16)
    at = pl.ds(pl.multiple_of(s * step, step), step)
    stride = TURNS * PLANE
    base = pl.multiple_of(s * step * stride, step * stride)

    plain, both = [], []
    for n in range(width // block):
        values = ext_ref[at, n * block : (n + 1) * block]
        wide = values.astype(jnp.float32)
        for half in range(block // LANES):
            v = n * (block // LANES) + half
            plain_ref[pl.ds(v, step, stride=PLANE), :] = wide[:, half * LANES : (half + 1) * LANES]
        square = wide * wide
        high = square.astype(jnp.bfloat16)
        low = (square - high.astype(jnp.float32)).astype(jnp.bfloat16)
        plain.append(values)
        both.append(jnp.concatenate([high, low], axis=1))
    for v in range(tiles, PLANE):
        plain_ref[pl.ds(v, step, stride=PLANE), :] = jnp.zeros((step, LANES), jnp.float32)

    def window(pieces, weight):
        tails = jnp.dot(jnp.concatenate(pieces[:-1], axis=0), jnp.concatenate([tail] * weight, axis=0), preferred_element_type=jnp.float32)
        heads = jnp.dot(jnp.concatenate(pieces[near:], axis=0), jnp.concatenate([head] * weight, axis=0), preferred_element_type=jnp.float32)
        for n in range(nblocks):
            total = tails[n * step : (n + 1) * step, :] + heads[n * step : (n + 1) * step, :]
            for m in range(n + 1, n + near):
                total = total + tails[m * step : (m + 1) * step, :1]
            yield total

    for n, (sums, squares) in enumerate(zip(window(plain, 1), window(both, 2))):
        spread = (squares - sums * sums / span) / span
        inverse = lax.rsqrt(jnp.maximum(spread, 0.0) + EPS) * (1.0 / math.sqrt(span))
        inverse = inverse.astype(jnp.bfloat16).astype(jnp.float32)
        for half in range(block // LANES):
            v = n * (block // LANES) + half
            norm_ref[pl.ds(base + v, step, stride=stride), :] = inverse[:, half * LANES : (half + 1) * LANES]

    lane = lax.broadcasted_iota(jnp.int32, (PLANE, LANES), 1)

    @pl.loop(0, step // SEVERAL)
    def _(group):
        for q in range(SEVERAL):
            r = group * SEVERAL + q
            top = pl.multiple_of(r * PLANE, PLANE)
            here = plain_ref[pl.ds(top, PLANE), :]
            after = plain_ref[pl.ds(top + 1, PLANE), :]
            level_at = pl.multiple_of(base + r * stride, stride)
            level = norm_ref[pl.ds(level_at, PLANE), :]
            level_after = norm_ref[pl.ds(level_at + 1, PLANE), :]
            for turn in range(1, TURNS):
                keep = lane >= LAGS * turn
                back = LANES - LAGS * turn
                turned_ref[(q * TURNS + turn) * PLANE : (q * TURNS + turn + 1) * PLANE, :] = pltpu.roll(jnp.where(keep, here, after), back, 1)
                level_to = pl.ds(pl.multiple_of(level_at + turn * PLANE, PLANE), PLANE)
                norm_ref[level_to, :] = pltpu.roll(jnp.where(keep, level, level_after), back, 1)
        for q in range(SEVERAL):
            r = group * SEVERAL + q
            to = (s * step + r) * 2 * AHEAD
            for pair in range(2):
                for ahead in range(AHEAD):
                    parts = []
                    for turn in (2 * pair, 2 * pair + 1):
                        if turn == 0:
                            parts.append(plain_ref[pl.ds(r * PLANE + ahead, 8), :])
                        else:
                            rows = (q * TURNS + turn) * PLANE + ahead
                            parts.append(turned_ref[rows : rows + 8, :])
                    hankel_ref[to + pair * AHEAD + ahead] = jnp.concatenate(parts, axis=0).astype(jnp.bfloat16)


def exchange_kernel(reach, hop, data_ref, templates_ref, stations_ref, shifts_ref, used_ref, hankel_ref, norm_ref, panels_ref, table_ref, *scratch):
    ext_ref, plain_ref, turned_ref, rows_ref, lists_ref, sta_ref, shf_ref, use_ref, loads = scratch[:9]
    halo_send, halo_recv, far_send, far_recv, side_send, side_recv, peer_send, peer_recv, mate_send, mate_recv = scratch[9:19]
    list_mate_send, list_mate_recv, list_far_send, list_far_recv, list_side_send, list_side_recv, list_peer_send, list_peer_recv = scratch[19:]
    rows, samples = data_ref.shape
    height = templates_ref.shape[0]
    mine, slots = stations_ref.shape
    slabs = lax.axis_size("slab")
    blocks = lax.axis_size("tpl")
    outer = slabs // 4
    slab = lax.axis_index("slab")
    tpl = lax.axis_index("tpl")
    core = lax.rem(slab, 2)
    mate = slab + 1 - 2 * core
    side = slab + 2 - 4 * lax.rem(slab // 2, 2)
    beside = lax.rem(slab + slabs - 1 + 2 * core, slabs)

    local = [
        pltpu.make_async_copy(templates_ref, rows_ref, loads.at[0]),
        pltpu.make_async_copy(stations_ref, sta_ref, loads.at[1]),
        pltpu.make_async_copy(shifts_ref, shf_ref, loads.at[2]),
        pltpu.make_async_copy(used_ref, use_ref, loads.at[3]),
        pltpu.make_async_copy(data_ref, ext_ref.at[:, :samples], loads.at[4]),
    ]
    for copy in local:
        copy.start()

    barrier = pltpu.get_barrier_semaphore()
    for d in range(1, blocks):
        pl.semaphore_signal(barrier, inc=1, device_id={"tpl": lax.rem(tpl + d, blocks)}, device_id_type=MESH)
    for d in range(1, outer):
        pl.semaphore_signal(barrier, inc=1, device_id={"slab": lax.rem(slab + 4 * d, slabs)}, device_id_type=MESH)
    for device in (mate, side, beside):
        pl.semaphore_signal(barrier, inc=1, device_id={"slab": device}, device_id_type=MESH)

    local[0].wait()
    panels_ref[pl.ds(pl.multiple_of(slab * height, height), height), :] = normalized(rows_ref[...].astype(jnp.float32))
    for copy in local[1:4]:
        copy.wait()
    lane = lax.broadcasted_iota(jnp.int32, (mine, LANES), 1)
    line = lax.broadcasted_iota(jnp.int32, (mine, LANES), 0)
    station = jnp.zeros((mine, LANES), jnp.int32)
    shift = jnp.zeros((mine, LANES), jnp.int32)
    used = jnp.zeros((mine, LANES), jnp.int32)
    for j in range(mine):
        used = jnp.where(line == j, use_ref[j], used)
        for k in range(slots):
            spot = jnp.logical_and(line == j, lane == k)
            station = jnp.where(spot, sta_ref[j, k], station)
            shift = jnp.where(spot, shf_ref[j, k], shift)
    owner = lax.div(station, hop)
    local_station = station - owner * hop
    half = lax.bitwise_and(lax.shift_right_logical(shift, 6), 1)
    first = lax.shift_right_logical(shift, 7)
    base = local_station * (TURNS * PLANE) + first
    fields = [
        jnp.where(lane < used, owner, -1),
        lax.bitwise_and(shift, 63),
        (2 * local_station + half) * AHEAD + first,
        (2 * local_station + 1 - half) * AHEAD + first + half,
        base + 2 * PLANE * half,
        base + 2 * PLANE * (1 - half) + half,
        used,
    ]
    packed = jnp.zeros((mine, LANES), jnp.int32)
    for f, values in enumerate(fields):
        kept = jnp.where(lane < slots, values, 0)
        packed = packed + (kept if f == 0 else pltpu.roll(kept, f * slots, 1))
    lists_ref[slab] = packed

    pl.semaphore_wait(barrier, blocks - 1 + outer - 1 + 3)

    def place(block, owner):
        at = (block * slabs + owner) * height
        return panels_ref.at[pl.ds(pl.multiple_of(at, height), height), :]

    def push(source, target, send, recv, device):
        return pltpu.make_async_remote_copy(
            src_ref=source, dst_ref=target, send_sem=send, recv_sem=recv, device_id=device, device_id_type=MESH)

    def owner_of(e, turn):
        start = slab + turn * (side - slab)
        return lax.rem(start + slabs - 4 * e, slabs)

    def halo_copy():
        return push(data_ref.at[:, :reach], ext_ref.at[:, samples:], halo_send, halo_recv, {"slab": lax.rem(slab + slabs - 1, slabs)})

    def far_copy(d):
        return push(place(0, slab), place(0, slab), far_send.at[d], far_recv.at[d], {"slab": lax.rem(slab + 4 * d, slabs)})

    def side_copy(e):
        at = place(0, owner_of(e, 0))
        return push(at, at, side_send.at[e], side_recv.at[e], {"slab": side})

    def peer_copy(d, e, turn):
        at = (d * outer + e) * 2 + turn
        unit = owner_of(e, turn)
        return push(place(0, unit), place(blocks - d, unit), peer_send.at[at], peer_recv.at[at], {"tpl": lax.rem(tpl + d, blocks)})

    def mate_copy(block, e, turn):
        at = (block * outer + e) * 2 + turn
        unit = place(block, owner_of(e, turn))
        return push(unit, unit, mate_send.at[at], mate_recv.at[at], {"slab": mate})

    def list_mate():
        return push(lists_ref.at[slab], lists_ref.at[slab], list_mate_send, list_mate_recv, {"slab": mate})

    def list_far(d):
        at = lists_ref.at[pl.ds(slab - core, 2)]
        return push(at, at, list_far_send.at[d], list_far_recv.at[d], {"slab": lax.rem(slab + 4 * d, slabs)})

    def list_side(e):
        at = lists_ref.at[pl.ds(owner_of(e, 0) - core, 2)]
        return push(at, at, list_side_send.at[e], list_side_recv.at[e], {"slab": side})

    def list_peer(d):
        return push(
            lists_ref.at[pl.ds(0, slabs)], lists_ref.at[pl.ds((blocks - d) * slabs, slabs)],
            list_peer_send.at[d], list_peer_recv.at[d], {"tpl": lax.rem(tpl + d, blocks)})

    def spread(e, turn):
        for d in range(1, blocks):
            peer_copy(d, e, turn).start()
        mate_copy(0, e, turn).start()

    begins = slab == 0
    ends = slab == slabs - 1
    list_mate().start()
    for d in range(1, outer):
        far_copy(d).start()

    @pl.when(jnp.logical_not(begins))
    def _():
        halo_copy().start()

    side_copy(0).start()
    spread(0, 0)
    local[4].wait()

    @pl.when(ends)
    def _():
        ext_ref[:, samples:] = jnp.zeros((rows, reach), ext_ref.dtype)

    list_mate().wait_recv()
    list_side(0).start()
    for d in range(1, outer):
        list_far(d).start()
    for d in range(1, outer):
        far_copy(d).wait_recv()
        side_copy(d).start()
        spread(d, 0)
    for d in range(1, outer):
        list_far(d).wait_recv()
        list_side(d).start()
    for e in range(outer):
        side_copy(e).wait_recv()
        spread(e, 1)
    for e in range(outer):
        list_side(e).wait_recv()
    for d in range(1, blocks):
        list_peer(d).start()

    @pl.when(jnp.logical_not(ends))
    def _():
        halo_copy().wait_recv()

    step = rows // STEPS

    @pl.loop(0, STEPS)
    def _(s):
        fill(templates_ref.shape[1], step, s, ext_ref, hankel_ref, norm_ref, plain_ref, turned_ref)
        for n in range(2 * outer // STEPS):
            unit = s * (2 * outer // STEPS) + n
            e, turn = lax.rem(unit, outer), lax.div(unit, outer)
            for d in range(1, blocks):
                peer_copy(d, e, turn).wait_recv()
                mate_copy(blocks - d, e, turn).start()

    for d in range(1, blocks):
        list_peer(d).wait_recv()

    near = lists_ref[...]
    lanes = lax.broadcasted_iota(jnp.int32, near.shape, 2)
    table_ref[...] = jnp.where(lanes < slots, jnp.where(near == tpl, 1, 0), near)

    for block in range(blocks):
        for turn in range(2):
            for e in range(outer):
                mate_copy(block, e, turn).wait_recv()

    @pl.when(jnp.logical_not(begins))
    def _():
        halo_copy().wait_send()

    list_mate().wait_send()
    for d in range(1, outer):
        far_copy(d).wait_send()
        list_far(d).wait_send()
    for d in range(1, blocks):
        list_peer(d).wait_send()
    for e in range(outer):
        side_copy(e).wait_send()
        list_side(e).wait_send()
        for turn in range(2):
            for d in range(1, blocks):
                peer_copy(d, e, turn).wait_send()
            for block in range(blocks):
                mate_copy(block, e, turn).wait_send()


def exchange(local, rows, stations, shifts, used, reach, hop):
    slabs = lax.axis_size("slab")
    blocks = lax.axis_size("tpl")
    height, span = rows.shape
    outer = slabs // 4
    vmem = pl.BlockSpec(memory_space=pltpu.VMEM)
    dma = pltpu.SemaphoreType.DMA
    one, few, all_units = [dma] * 2, [dma((outer,))] * 2, [dma((blocks * outer * 2,))] * 2
    return pl.pallas_call(
        functools.partial(exchange_kernel, reach, hop),
        out_shape=(
            jax.ShapeDtypeStruct((local.shape[0] * 2 * AHEAD, 16, LANES), local.dtype),
            jax.ShapeDtypeStruct((local.shape[0] * TURNS * PLANE, LANES), jnp.float32),
            jax.ShapeDtypeStruct((height * slabs * blocks, span), rows.dtype),
            jax.ShapeDtypeStruct((slabs * blocks, stations.shape[0], LANES), jnp.int32),
        ),
        in_specs=[pl.BlockSpec(memory_space=pltpu.HBM)] * 5,
        out_specs=(vmem, vmem, vmem, vmem),
        scratch_shapes=[
            pltpu.VMEM((local.shape[0], local.shape[1] + reach), local.dtype),
            pltpu.VMEM(((local.shape[0] // STEPS + 1) * PLANE, LANES), jnp.float32),
            pltpu.VMEM((SEVERAL * TURNS * PLANE, LANES), jnp.float32),
            pltpu.VMEM(rows.shape, rows.dtype),
            pltpu.VMEM((slabs * blocks, stations.shape[0], LANES), jnp.int32),
            pltpu.SMEM(stations.shape, jnp.int32),
            pltpu.SMEM(shifts.shape, jnp.int32),
            pltpu.SMEM(used.shape, jnp.int32),
            dma((5,)),
        ] + one + few + few + all_units + all_units + one + few + few + [dma((blocks,))] * 2,
        compiler_params=pltpu.CompilerParams(
            collective_id=0, has_side_effects=True, vmem_limit_bytes=24 << 20
        ),
    )(local, rows, stations, shifts, used)


def stack_kernel(span, comps, hop, slots, panel, block, table_ref, hankel_ref, norm_ref, panels_ref, out_ref,
                 hankel_out_ref, norm_out_ref, unit_ref, turned_ref, right_ref, level_ref, sum_ref, done_ref, item_ref):
    parts = span // LANES
    group = comps * slots
    count = panel * slots

    height = 2 * group
    @pl.loop(0, panel // 2)
    def _(step):
        at = pl.ds(pl.multiple_of((block * panel + 2 * step) * group, height), height)
        values = panels_ref[at, :].astype(jnp.float32)
        for t in range(2):
            for c in range(comps):
                for part in range(parts):
                    piece = values[t * group + c * slots : t * group + (c + 1) * slots, part * LANES : (part + 1) * LANES]
                    unit_ref[pl.ds((step * 2 + t) * slots * PLANE + c * parts + part, slots, stride=PLANE), :] = piece

    unit_ref[count * PLANE : (count + 1) * PLANE, :] = jnp.zeros((PLANE, LANES), jnp.float32)

    def collect(j, total):
        sum_ref[j] = jnp.zeros((TURNS * 8, LAGS), jnp.float32)
        for k in range(slots):
            item_ref[total] = j * LANES + k
            total = total + table_ref[j * LANES + k]
        return total

    total = lax.fori_loop(0, panel, collect, 0)
    for k in range(2 * PASS):
        item_ref[total + k] = panel * LANES
    sum_ref[panel] = jnp.zeros((TURNS * 8, LAGS), jnp.float32)

    lane_half = lax.broadcasted_iota(jnp.int32, (16, LANES), 1).astype(jnp.float32).astype(jnp.bfloat16)
    lag_half = lax.broadcasted_iota(jnp.int32, (16, LANES), 0).astype(jnp.float32).astype(jnp.bfloat16)
    ahead = lane_half - lag_half
    further = ahead - jnp.full((16, LANES), 16.0, jnp.bfloat16)
    none = jnp.zeros((16, LANES), jnp.bfloat16)

    def field(g, n, which):
        return table_ref[item_ref[g * PASS + n] + which * slots]

    def turn_rows(g):
        for n in range(PASS):
            item = item_ref[g * PASS + n]
            slot = lax.shift_right_logical(item, 7) * slots + lax.bitwise_and(item, LANES - 1)
            rows = unit_ref[pl.ds(pl.multiple_of(slot * PLANE, PLANE), PLANE), :]
            turned_ref[n * PLANE : (n + 1) * PLANE, :] = pltpu.roll(rows, field(g, n, 1), 1)

    def build_slot(g, n):
        bound = jnp.full((16, LANES), field(g, n, 1), jnp.int32).astype(jnp.float32).astype(jnp.bfloat16)
        inside = [ahead >= bound, further >= bound]
        for c in range(comps):
            turned = []
            for part in range(parts):
                line = jnp.broadcast_to(turned_ref[n * PLANE + c * parts + part : n * PLANE + c * parts + part + 1, :], (8, LANES))
                lags = pltpu.roll(line, 0, 1, stride=1, stride_axis=0)
                low = jnp.concatenate([lags, pltpu.roll(lags, 8, 1)], axis=0).astype(jnp.bfloat16)
                turned.append((low, pltpu.roll(low, 16, 1)))
            edges = [(none, none)] + turned + [(none, none)]
            at = (n * comps + c) * LAGS
            for b in range(2):
                for p in range(parts + 1):
                    right_ref[at + 16 * b : at + 16 * b + 16, p * LANES : (p + 1) * LANES] = jnp.where(inside[b], edges[p + 1][b], edges[p][b])
        back = LANES - field(g, n, 1)
        for turn in range(TURNS):
            at = field(g, n, 4 + turn // 2)
            for c in range(comps):
                norm = norm_ref[pl.ds(at + c * hop * TURNS * PLANE + (turn % 2) * PLANE, 8), :]
                k = (n * comps + c) * TURNS + turn
                level_ref[k * 8 : k * 8 + 8, :] = pltpu.roll(norm, back, 1)

    def build(g):
        turn_rows(g)
        for n in range(PASS):
            build_slot(g, n)

    def multiply(g):
        for n in range(PASS):
            near = field(g, n, 2)
            far = field(g, n, 3)
            for c in range(comps):
                i = n * comps + c
                left = jnp.concatenate([
                    jnp.concatenate([hankel_ref[at + c * hop * 2 * AHEAD + p] for p in range(CHUNKS)], axis=1)
                    for at in (near, far)], axis=0)
                yield n, c, lax.dot_general(
                    left, right_ref[i * LAGS : (i + 1) * LAGS, :],
                    (((1,), (1,)), ((), ())), preferred_element_type=jnp.float32)

    def gather_slot(g, n, product):
        j = lax.shift_right_logical(item_ref[g * PASS + n], 7)
        added = []
        for turn in range(TURNS):
            value = None
            for c in range(comps):
                k = (n * comps + c) * TURNS + turn
                term = product(n, c, turn) * level_ref[k * 8 : k * 8 + 8, :LAGS]
                value = term if value is None else value + term
            added.append(value)
        sum_ref[j] += jnp.concatenate(added, axis=0)

    build(0)

    def body(g, _):
        products = {}
        for n, c, product in multiply(g):
            products[n, c] = product
            if c == comps - 1:
                gather_slot(g, n, lambda n, c, turn: products[n, c][8 * turn : 8 * turn + 8, :])
        build(g + 1)
        return 0

    lax.fori_loop(0, lax.div(total + PASS - 1, PASS), body, 0)

    def finish(j, _):
        value = sum_ref[j]
        result = jnp.concatenate([value[8 * turn : 8 * turn + 8, :] for turn in range(TURNS)], axis=1)
        used = jnp.full((8, LANES), table_ref[j * LANES + (FIELDS - 1) * slots], jnp.int32).astype(jnp.float32)
        done_ref[pl.ds(pl.multiple_of(j * 8, 8), 8), :] = result * jnp.sqrt(span / (3.0 * used))
        return 0

    lax.fori_loop(0, panel, finish, 0, unroll=4)
    for b in range(panel // 8):
        for a in range(out_ref.shape[1] // LANES):
            out_ref[b * 8 : b * 8 + 8, a * LANES : (a + 1) * LANES] = done_ref[pl.ds(b * 64 + a, 8, stride=8), :]


def stack(table, hankel, norm, panels, block, panel, slots, comps, hop, span, samples):
    smem = pl.BlockSpec(memory_space=pltpu.SMEM)
    vmem = pl.BlockSpec(memory_space=pltpu.VMEM)
    count = panel * slots
    return pl.pallas_call(
        functools.partial(stack_kernel, span, comps, hop, slots, panel, block),
        out_shape=(
            jax.ShapeDtypeStruct((panel, samples), jnp.float32),
            jax.ShapeDtypeStruct(hankel.shape, hankel.dtype),
            jax.ShapeDtypeStruct(norm.shape, norm.dtype),
        ),
        in_specs=[smem, vmem, vmem, vmem],
        out_specs=(vmem, vmem, vmem),
        input_output_aliases={1: 1, 2: 2},
        scratch_shapes=[
            pltpu.VMEM(((count + 1) * PLANE, LANES), jnp.float32),
            pltpu.VMEM((PASS * PLANE, LANES), jnp.float32),
            pltpu.VMEM((PASS * comps * LAGS, CHUNKS * LANES), jnp.bfloat16),
            pltpu.VMEM((PASS * comps * TURNS * 8, LANES), jnp.float32),
            pltpu.VMEM((panel + 1, TURNS * 8, LAGS), jnp.float32),
            pltpu.VMEM((panel * 8, LANES), jnp.float32),
            pltpu.SMEM((count + 3 * PASS,), jnp.int32),
        ],
        compiler_params=pltpu.CompilerParams(vmem_limit_bytes=(count * PLANE * LANES * 4) + (8 << 20)),
        cost_estimate=pl.CostEstimate(flops=6_000_000_000, bytes_accessed=20_000_000, transcendentals=0),
    )(table, hankel, norm, panels)


def per_device(data, templates, stations, shifts, used):
    mine, slots, comps, span = templates.shape
    hop, _, samples = data.shape
    reach = span + MAXSHIFT
    slabs = lax.axis_size("slab")
    blocks = lax.axis_size("tpl")
    local = jnp.transpose(data, (1, 0, 2)).reshape(-1, samples)
    rows = jnp.transpose(templates, (0, 2, 1, 3)).reshape(-1, span)
    inputs = [pltpu.with_memory_space_constraint(x, pltpu.HBM) for x in (local, rows, stations, shifts, used)]
    hankel, norm, panels, lists = exchange(*inputs, reach, hop)
    panel = mine * slabs
    tables = lists.reshape(blocks, panel * LANES)
    tables = jnp.pad(tables, ((0, 0), (0, LANES)))

    sent = []
    for d in range(1, blocks + 1):
        block = d % blocks
        total, hankel, norm = stack(tables[block], hankel, norm, panels, block, panel, slots, comps, hop, span, samples)
        if block:
            pairs = [(t, (t + d) % blocks) for t in range(blocks)]
            sent.append(lax.ppermute(total, "tpl", pairs))
    for piece in sent:
        total = total + piece
    return total


def solution(mesh):
    return jax.shard_map(
        per_device,
        mesh=mesh,
        in_specs=(
            P("tpl", None, "slab"),
            P(("tpl", "slab"), None, None, None),
            P(("tpl", "slab"), None),
            P(("tpl", "slab"), None),
            P(("tpl", "slab")),
        ),
        out_specs=P("tpl", "slab"),
        check_vma=False,
    )
```

```python
import functools
import math

import jax
import jax.numpy as jnp
from jax import lax
from jax.experimental import pallas as pl
from jax.experimental.pallas import tpu as pltpu
from jax.sharding import PartitionSpec as P

MAXSHIFT = 256
EPS = 1e-05
MESH = pl.DeviceIdType.MESH

LANES = 128
LAGS = 32
TURNS = LANES // LAGS
PASS = 6
PLANE = 16
CHUNKS = 5
AHEAD = 7
FIELDS = 7
STEPS = 4
SEVERAL = 4


def normalized(rows):
    span = rows.shape[-1]
    centered = rows - jnp.mean(rows, axis=-1, keepdims=True)
    rms = jnp.sqrt(jnp.mean(centered * centered, axis=-1, keepdims=True) + EPS)
    return (centered / (rms * math.sqrt(span))).astype(jnp.bfloat16)


def fill(span, step, s, ext_ref, hankel_ref, norm_ref, plain_ref, turned_ref):
    width = ext_ref.shape[1]
    block = 256
    near = span // block
    nblocks = (width - span) // block
    tiles = width // LANES
    taps = lax.broadcasted_iota(jnp.int32, (block, block), 0)
    starts = lax.broadcasted_iota(jnp.int32, (block, block), 1)
    tail = jnp.where(taps >= starts, 1.0, 0.0).astype(jnp.bfloat16)
    head = jnp.where(taps < starts, 1.0, 0.0).astype(jnp.bfloat16)
    at = pl.ds(pl.multiple_of(s * step, step), step)
    stride = TURNS * PLANE
    base = pl.multiple_of(s * step * stride, step * stride)

    plain, both = [], []
    for n in range(width // block):
        values = ext_ref[at, n * block : (n + 1) * block]
        wide = values.astype(jnp.float32)
        for half in range(block // LANES):
            v = n * (block // LANES) + half
            plain_ref[pl.ds(v, step, stride=PLANE), :] = wide[:, half * LANES : (half + 1) * LANES]
        square = wide * wide
        high = square.astype(jnp.bfloat16)
        low = (square - high.astype(jnp.float32)).astype(jnp.bfloat16)
        plain.append(values)
        both.append(jnp.concatenate([high, low], axis=1))
    for v in range(tiles, PLANE):
        plain_ref[pl.ds(v, step, stride=PLANE), :] = jnp.zeros((step, LANES), jnp.float32)

    def window(pieces, weight):
        tails = jnp.dot(jnp.concatenate(pieces[:-1], axis=0), jnp.concatenate([tail] * weight, axis=0), preferred_element_type=jnp.float32)
        heads = jnp.dot(jnp.concatenate(pieces[near:], axis=0), jnp.concatenate([head] * weight, axis=0), preferred_element_type=jnp.float32)
        for n in range(nblocks):
            total = tails[n * step : (n + 1) * step, :] + heads[n * step : (n + 1) * step, :]
            for m in range(n + 1, n + near):
                total = total + tails[m * step : (m + 1) * step, :1]
            yield total

    for n, (sums, squares) in enumerate(zip(window(plain, 1), window(both, 2))):
        spread = (squares - sums * sums / span) / span
        inverse = lax.rsqrt(jnp.maximum(spread, 0.0) + EPS) * (1.0 / math.sqrt(span))
        inverse = inverse.astype(jnp.bfloat16).astype(jnp.float32)
        for half in range(block // LANES):
            v = n * (block // LANES) + half
            norm_ref[pl.ds(base + v, step, stride=stride), :] = inverse[:, half * LANES : (half + 1) * LANES]

    lane = lax.broadcasted_iota(jnp.int32, (PLANE, LANES), 1)

    @pl.loop(0, step // SEVERAL)
    def _(group):
        for q in range(SEVERAL):
            r = group * SEVERAL + q
            top = pl.multiple_of(r * PLANE, PLANE)
            here = plain_ref[pl.ds(top, PLANE), :]
            after = plain_ref[pl.ds(top + 1, PLANE), :]
            level_at = pl.multiple_of(base + r * stride, stride)
            level = norm_ref[pl.ds(level_at, PLANE), :]
            level_after = norm_ref[pl.ds(level_at + 1, PLANE), :]
            for turn in range(1, TURNS):
                keep = lane >= LAGS * turn
                back = LANES - LAGS * turn
                turned_ref[(q * TURNS + turn) * PLANE : (q * TURNS + turn + 1) * PLANE, :] = pltpu.roll(jnp.where(keep, here, after), back, 1)
                level_to = pl.ds(pl.multiple_of(level_at + turn * PLANE, PLANE), PLANE)
                norm_ref[level_to, :] = pltpu.roll(jnp.where(keep, level, level_after), back, 1)
        for q in range(SEVERAL):
            r = group * SEVERAL + q
            to = (s * step + r) * 2 * AHEAD
            for pair in range(2):
                for ahead in range(AHEAD):
                    parts = []
                    for turn in (2 * pair, 2 * pair + 1):
                        if turn == 0:
                            parts.append(plain_ref[pl.ds(r * PLANE + ahead, 8), :])
                        else:
                            rows = (q * TURNS + turn) * PLANE + ahead
                            parts.append(turned_ref[rows : rows + 8, :])
                    hankel_ref[to + pair * AHEAD + ahead] = jnp.concatenate(parts, axis=0).astype(jnp.bfloat16)


def exchange_kernel(reach, hop, data_ref, templates_ref, stations_ref, shifts_ref, used_ref, hankel_ref, norm_ref, panels_ref, *refs):
    table_refs, scratch = refs[: lax.axis_size("tpl")], refs[lax.axis_size("tpl") :]
    ext_ref, plain_ref, turned_ref, rows_ref, lists_ref, sta_ref, shf_ref, use_ref, loads = scratch[:9]
    halo_send, halo_recv, far_send, far_recv, side_send, side_recv, peer_send, peer_recv, mate_send, mate_recv = scratch[9:19]
    list_mate_send, list_mate_recv, list_far_send, list_far_recv, list_side_send, list_side_recv, list_peer_send, list_peer_recv = scratch[19:]
    rows, samples = data_ref.shape
    height = templates_ref.shape[0]
    mine, slots = stations_ref.shape
    slabs = lax.axis_size("slab")
    blocks = lax.axis_size("tpl")
    outer = slabs // 4
    slab = lax.axis_index("slab")
    tpl = lax.axis_index("tpl")
    core = lax.rem(slab, 2)
    mate = slab + 1 - 2 * core
    side = slab + 2 - 4 * lax.rem(slab // 2, 2)
    beside = lax.rem(slab + slabs - 1 + 2 * core, slabs)

    local = [
        pltpu.make_async_copy(templates_ref, rows_ref, loads.at[0]),
        pltpu.make_async_copy(stations_ref, sta_ref, loads.at[1]),
        pltpu.make_async_copy(shifts_ref, shf_ref, loads.at[2]),
        pltpu.make_async_copy(used_ref, use_ref, loads.at[3]),
        pltpu.make_async_copy(data_ref, ext_ref.at[:, :samples], loads.at[4]),
    ]
    for copy in local:
        copy.start()

    barrier = pltpu.get_barrier_semaphore()
    for d in range(1, blocks):
        pl.semaphore_signal(barrier, inc=1, device_id={"tpl": lax.rem(tpl + d, blocks)}, device_id_type=MESH)
    for d in range(1, outer):
        pl.semaphore_signal(barrier, inc=1, device_id={"slab": lax.rem(slab + 4 * d, slabs)}, device_id_type=MESH)
    for device in (mate, side, beside):
        pl.semaphore_signal(barrier, inc=1, device_id={"slab": device}, device_id_type=MESH)

    local[0].wait()
    panels_ref[pl.ds(pl.multiple_of(slab * height, height), height), :] = normalized(rows_ref[...].astype(jnp.float32))
    for copy in local[1:4]:
        copy.wait()
    lane = lax.broadcasted_iota(jnp.int32, (mine, LANES), 1)
    line = lax.broadcasted_iota(jnp.int32, (mine, LANES), 0)
    station = jnp.zeros((mine, LANES), jnp.int32)
    shift = jnp.zeros((mine, LANES), jnp.int32)
    used = jnp.zeros((mine, LANES), jnp.int32)
    for j in range(mine):
        used = jnp.where(line == j, use_ref[j], used)
        for k in range(slots):
            spot = jnp.logical_and(line == j, lane == k)
            station = jnp.where(spot, sta_ref[j, k], station)
            shift = jnp.where(spot, shf_ref[j, k], shift)
    owner = lax.div(station, hop)
    local_station = station - owner * hop
    half = lax.bitwise_and(lax.shift_right_logical(shift, 6), 1)
    first = lax.shift_right_logical(shift, 7)
    base = local_station * (TURNS * PLANE) + first
    fields = [
        jnp.where(lane < used, owner, -1),
        lax.bitwise_and(shift, 63),
        (2 * local_station + half) * AHEAD + first,
        (2 * local_station + 1 - half) * AHEAD + first + half,
        base + 2 * PLANE * half,
        base + 2 * PLANE * (1 - half) + half,
        used,
    ]
    packed = jnp.zeros((mine, LANES), jnp.int32)
    for f, values in enumerate(fields):
        kept = jnp.where(lane < slots, values, 0)
        packed = packed + (kept if f == 0 else pltpu.roll(kept, f * slots, 1))
    lists_ref[slab] = packed

    pl.semaphore_wait(barrier, blocks - 1 + outer - 1 + 3)

    def place(block, owner):
        at = (block * slabs + owner) * height
        return panels_ref.at[pl.ds(pl.multiple_of(at, height), height), :]

    def push(source, target, send, recv, device):
        return pltpu.make_async_remote_copy(
            src_ref=source, dst_ref=target, send_sem=send, recv_sem=recv, device_id=device, device_id_type=MESH)

    def owner_of(e, turn):
        start = slab + turn * (side - slab)
        return lax.rem(start + slabs - 4 * e, slabs)

    def halo_copy():
        return push(data_ref.at[:, :reach], ext_ref.at[:, samples:], halo_send, halo_recv, {"slab": lax.rem(slab + slabs - 1, slabs)})

    def far_copy(d):
        return push(place(0, slab), place(0, slab), far_send.at[d], far_recv.at[d], {"slab": lax.rem(slab + 4 * d, slabs)})

    def side_copy(e):
        at = place(0, owner_of(e, 0))
        return push(at, at, side_send.at[e], side_recv.at[e], {"slab": side})

    def peer_copy(d, e, turn):
        at = (d * outer + e) * 2 + turn
        unit = owner_of(e, turn)
        return push(place(0, unit), place(blocks - d, unit), peer_send.at[at], peer_recv.at[at], {"tpl": lax.rem(tpl + d, blocks)})

    def mate_copy(block, e, turn):
        at = (block * outer + e) * 2 + turn
        unit = place(block, owner_of(e, turn))
        return push(unit, unit, mate_send.at[at], mate_recv.at[at], {"slab": mate})

    def list_mate():
        return push(lists_ref.at[slab], lists_ref.at[slab], list_mate_send, list_mate_recv, {"slab": mate})

    def list_far(d):
        at = lists_ref.at[pl.ds(slab - core, 2)]
        return push(at, at, list_far_send.at[d], list_far_recv.at[d], {"slab": lax.rem(slab + 4 * d, slabs)})

    def list_side(e):
        at = lists_ref.at[pl.ds(owner_of(e, 0) - core, 2)]
        return push(at, at, list_side_send.at[e], list_side_recv.at[e], {"slab": side})

    def list_peer(d):
        return push(
            lists_ref.at[pl.ds(0, slabs)], lists_ref.at[pl.ds((blocks - d) * slabs, slabs)],
            list_peer_send.at[d], list_peer_recv.at[d], {"tpl": lax.rem(tpl + d, blocks)})

    def spread(e, turn):
        for d in range(1, blocks):
            peer_copy(d, e, turn).start()
        mate_copy(0, e, turn).start()

    begins = slab == 0
    ends = slab == slabs - 1
    list_mate().start()
    for d in range(1, outer):
        far_copy(d).start()

    @pl.when(jnp.logical_not(begins))
    def _():
        halo_copy().start()

    side_copy(0).start()
    spread(0, 0)
    local[4].wait()

    @pl.when(ends)
    def _():
        ext_ref[:, samples:] = jnp.zeros((rows, reach), ext_ref.dtype)

    list_mate().wait_recv()
    list_side(0).start()
    for d in range(1, outer):
        list_far(d).start()
    for d in range(1, outer):
        far_copy(d).wait_recv()
        side_copy(d).start()
        spread(d, 0)
    for d in range(1, outer):
        list_far(d).wait_recv()
        list_side(d).start()
    for e in range(outer):
        side_copy(e).wait_recv()
        spread(e, 1)
    for e in range(outer):
        list_side(e).wait_recv()
    for d in range(1, blocks):
        list_peer(d).start()

    @pl.when(jnp.logical_not(ends))
    def _():
        halo_copy().wait_recv()

    step = rows // STEPS

    @pl.loop(0, STEPS)
    def _(s):
        fill(templates_ref.shape[1], step, s, ext_ref, hankel_ref, norm_ref, plain_ref, turned_ref)
        for n in range(2 * outer // STEPS):
            unit = s * (2 * outer // STEPS) + n
            e, turn = lax.rem(unit, outer), lax.div(unit, outer)
            for d in range(1, blocks):
                peer_copy(d, e, turn).wait_recv()
                mate_copy(blocks - d, e, turn).start()

    for d in range(1, blocks):
        list_peer(d).wait_recv()

    lanes = lax.broadcasted_iota(jnp.int32, (slabs, LANES), 1)
    for block in range(blocks):
        for j in range(mine):
            values = lists_ref[block * slabs : (block + 1) * slabs, j, :]
            near = jnp.where(values == tpl, 1, 0)
            table_refs[block][pl.ds(j, slabs, stride=mine), :] = jnp.where(lanes < slots, near, values)
        table_refs[block][slabs * mine :, :] = jnp.zeros((8, LANES), jnp.int32)

    for block in range(blocks):
        for turn in range(2):
            for e in range(outer):
                mate_copy(block, e, turn).wait_recv()

    @pl.when(jnp.logical_not(begins))
    def _():
        halo_copy().wait_send()

    list_mate().wait_send()
    for d in range(1, outer):
        far_copy(d).wait_send()
        list_far(d).wait_send()
    for d in range(1, blocks):
        list_peer(d).wait_send()
    for e in range(outer):
        side_copy(e).wait_send()
        list_side(e).wait_send()
        for turn in range(2):
            for d in range(1, blocks):
                peer_copy(d, e, turn).wait_send()
            for block in range(blocks):
                mate_copy(block, e, turn).wait_send()


def exchange(local, rows, stations, shifts, used, reach, hop):
    slabs = lax.axis_size("slab")
    blocks = lax.axis_size("tpl")
    height, span = rows.shape
    outer = slabs // 4
    vmem = pl.BlockSpec(memory_space=pltpu.VMEM)
    dma = pltpu.SemaphoreType.DMA
    one, few, all_units = [dma] * 2, [dma((outer,))] * 2, [dma((blocks * outer * 2,))] * 2
    return pl.pallas_call(
        functools.partial(exchange_kernel, reach, hop),
        out_shape=(
            jax.ShapeDtypeStruct((local.shape[0] * 2 * AHEAD, 16, LANES), local.dtype),
            jax.ShapeDtypeStruct((local.shape[0] * TURNS * PLANE, LANES), jnp.float32),
            jax.ShapeDtypeStruct((height * slabs * blocks, span), rows.dtype),
        ) + (jax.ShapeDtypeStruct((slabs * stations.shape[0] + 8, LANES), jnp.int32),) * blocks,
        in_specs=[pl.BlockSpec(memory_space=pltpu.HBM)] * 5,
        out_specs=(vmem,) * (3 + blocks),
        scratch_shapes=[
            pltpu.VMEM((local.shape[0], local.shape[1] + reach), local.dtype),
            pltpu.VMEM(((local.shape[0] // STEPS + 1) * PLANE, LANES), jnp.float32),
            pltpu.VMEM((SEVERAL * TURNS * PLANE, LANES), jnp.float32),
            pltpu.VMEM(rows.shape, rows.dtype),
            pltpu.VMEM((slabs * blocks, stations.shape[0], LANES), jnp.int32),
            pltpu.SMEM(stations.shape, jnp.int32),
            pltpu.SMEM(shifts.shape, jnp.int32),
            pltpu.SMEM(used.shape, jnp.int32),
            dma((5,)),
        ] + one + few + few + all_units + all_units + one + few + few + [dma((blocks,))] * 2,
        compiler_params=pltpu.CompilerParams(
            collective_id=0, has_side_effects=True, vmem_limit_bytes=24 << 20
        ),
    )(local, rows, stations, shifts, used)


def stack_kernel(span, comps, hop, slots, panel, block, table_ref, hankel_ref, norm_ref, panels_ref, out_ref,
                 hankel_out_ref, norm_out_ref, unit_ref, turned_ref, right_ref, level_ref, sum_ref, done_ref, item_ref):
    parts = span // LANES
    group = comps * slots
    count = panel * slots

    height = 2 * group
    @pl.loop(0, panel // 2)
    def _(step):
        at = pl.ds(pl.multiple_of((block * panel + 2 * step) * group, height), height)
        values = panels_ref[at, :].astype(jnp.float32)
        for t in range(2):
            for c in range(comps):
                for part in range(parts):
                    piece = values[t * group + c * slots : t * group + (c + 1) * slots, part * LANES : (part + 1) * LANES]
                    unit_ref[pl.ds((step * 2 + t) * slots * PLANE + c * parts + part, slots, stride=PLANE), :] = piece

    unit_ref[count * PLANE : (count + 1) * PLANE, :] = jnp.zeros((PLANE, LANES), jnp.float32)

    def collect(j, total):
        sum_ref[j] = jnp.zeros((TURNS * 8, LAGS), jnp.float32)
        for k in range(slots):
            item_ref[total] = j * LANES + k
            total = total + table_ref[j, k]
        return total

    total = lax.fori_loop(0, panel, collect, 0)
    for k in range(2 * PASS):
        item_ref[total + k] = panel * LANES
    sum_ref[panel] = jnp.zeros((TURNS * 8, LAGS), jnp.float32)

    lane_half = lax.broadcasted_iota(jnp.int32, (16, LANES), 1).astype(jnp.float32).astype(jnp.bfloat16)
    lag_half = lax.broadcasted_iota(jnp.int32, (16, LANES), 0).astype(jnp.float32).astype(jnp.bfloat16)
    ahead = lane_half - lag_half
    further = ahead - jnp.full((16, LANES), 16.0, jnp.bfloat16)
    none = jnp.zeros((16, LANES), jnp.bfloat16)

    def field(g, n, which):
        item = item_ref[g * PASS + n]
        return table_ref[lax.shift_right_logical(item, 7), lax.bitwise_and(item, LANES - 1) + which * slots]

    def turn_rows(g):
        for n in range(PASS):
            item = item_ref[g * PASS + n]
            slot = lax.shift_right_logical(item, 7) * slots + lax.bitwise_and(item, LANES - 1)
            rows = unit_ref[pl.ds(pl.multiple_of(slot * PLANE, PLANE), PLANE), :]
            turned_ref[n * PLANE : (n + 1) * PLANE, :] = pltpu.roll(rows, field(g, n, 1), 1)

    def build_slot(g, n):
        bound = jnp.full((16, LANES), field(g, n, 1), jnp.int32).astype(jnp.float32).astype(jnp.bfloat16)
        inside = [ahead >= bound, further >= bound]
        for c in range(comps):
            turned = []
            for part in range(parts):
                line = jnp.broadcast_to(turned_ref[n * PLANE + c * parts + part : n * PLANE + c * parts + part + 1, :], (8, LANES))
                lags = pltpu.roll(line, 0, 1, stride=1, stride_axis=0)
                low = jnp.concatenate([lags, pltpu.roll(lags, 8, 1)], axis=0).astype(jnp.bfloat16)
                turned.append((low, pltpu.roll(low, 16, 1)))
            edges = [(none, none)] + turned + [(none, none)]
            at = (n * comps + c) * LAGS
            for b in range(2):
                for p in range(parts + 1):
                    right_ref[at + 16 * b : at + 16 * b + 16, p * LANES : (p + 1) * LANES] = jnp.where(inside[b], edges[p + 1][b], edges[p][b])
        back = LANES - field(g, n, 1)
        for turn in range(TURNS):
            at = field(g, n, 4 + turn // 2)
            for c in range(comps):
                norm = norm_ref[pl.ds(at + c * hop * TURNS * PLANE + (turn % 2) * PLANE, 8), :]
                k = (n * comps + c) * TURNS + turn
                level_ref[k * 8 : k * 8 + 8, :] = pltpu.roll(norm, back, 1)

    def build(g):
        turn_rows(g)
        for n in range(PASS):
            build_slot(g, n)

    def multiply(g):
        for n in range(PASS):
            near = field(g, n, 2)
            far = field(g, n, 3)
            for c in range(comps):
                i = n * comps + c
                left = jnp.concatenate([
                    jnp.concatenate([hankel_ref[at + c * hop * 2 * AHEAD + p] for p in range(CHUNKS)], axis=1)
                    for at in (near, far)], axis=0)
                yield n, c, lax.dot_general(
                    left, right_ref[i * LAGS : (i + 1) * LAGS, :],
                    (((1,), (1,)), ((), ())), preferred_element_type=jnp.float32)

    def gather_slot(g, n, product):
        j = lax.shift_right_logical(item_ref[g * PASS + n], 7)
        added = []
        for turn in range(TURNS):
            value = None
            for c in range(comps):
                k = (n * comps + c) * TURNS + turn
                term = product(n, c, turn) * level_ref[k * 8 : k * 8 + 8, :LAGS]
                value = term if value is None else value + term
            added.append(value)
        sum_ref[j] += jnp.concatenate(added, axis=0)

    build(0)

    def body(g, _):
        products = {}
        for n, c, product in multiply(g):
            products[n, c] = product
            if c == comps - 1:
                gather_slot(g, n, lambda n, c, turn: products[n, c][8 * turn : 8 * turn + 8, :])
        build(g + 1)
        return 0

    lax.fori_loop(0, lax.div(total + PASS - 1, PASS), body, 0)

    def finish(j, _):
        value = sum_ref[j]
        result = jnp.concatenate([value[8 * turn : 8 * turn + 8, :] for turn in range(TURNS)], axis=1)
        used = jnp.full((8, LANES), table_ref[j, (FIELDS - 1) * slots], jnp.int32).astype(jnp.float32)
        done_ref[pl.ds(pl.multiple_of(j * 8, 8), 8), :] = result * jnp.sqrt(span / (3.0 * used))
        return 0

    lax.fori_loop(0, panel, finish, 0, unroll=4)
    for b in range(panel // 8):
        for a in range(out_ref.shape[1] // LANES):
            out_ref[b * 8 : b * 8 + 8, a * LANES : (a + 1) * LANES] = done_ref[pl.ds(b * 64 + a, 8, stride=8), :]


def stack(table, hankel, norm, panels, block, panel, slots, comps, hop, span, samples):
    smem = pl.BlockSpec(memory_space=pltpu.SMEM)
    vmem = pl.BlockSpec(memory_space=pltpu.VMEM)
    count = panel * slots
    return pl.pallas_call(
        functools.partial(stack_kernel, span, comps, hop, slots, panel, block),
        out_shape=(
            jax.ShapeDtypeStruct((panel, samples), jnp.float32),
            jax.ShapeDtypeStruct(hankel.shape, hankel.dtype),
            jax.ShapeDtypeStruct(norm.shape, norm.dtype),
        ),
        in_specs=[smem, vmem, vmem, vmem],
        out_specs=(vmem, vmem, vmem),
        input_output_aliases={1: 1, 2: 2},
        scratch_shapes=[
            pltpu.VMEM(((count + 1) * PLANE, LANES), jnp.float32),
            pltpu.VMEM((PASS * PLANE, LANES), jnp.float32),
            pltpu.VMEM((PASS * comps * LAGS, CHUNKS * LANES), jnp.bfloat16),
            pltpu.VMEM((PASS * comps * TURNS * 8, LANES), jnp.float32),
            pltpu.VMEM((panel + 1, TURNS * 8, LAGS), jnp.float32),
            pltpu.VMEM((panel * 8, LANES), jnp.float32),
            pltpu.SMEM((count + 3 * PASS,), jnp.int32),
        ],
        compiler_params=pltpu.CompilerParams(vmem_limit_bytes=(count * PLANE * LANES * 4) + (8 << 20)),
        cost_estimate=pl.CostEstimate(flops=6_000_000_000, bytes_accessed=20_000_000, transcendentals=0),
    )(table, hankel, norm, panels)


def per_device(data, templates, stations, shifts, used):
    mine, slots, comps, span = templates.shape
    hop, _, samples = data.shape
    reach = span + MAXSHIFT
    slabs = lax.axis_size("slab")
    blocks = lax.axis_size("tpl")
    local = jnp.transpose(data, (1, 0, 2)).reshape(-1, samples)
    rows = jnp.transpose(templates, (0, 2, 1, 3)).reshape(-1, span)
    inputs = [pltpu.with_memory_space_constraint(x, pltpu.HBM) for x in (local, rows, stations, shifts, used)]
    hankel, norm, panels, *tables = exchange(*inputs, reach, hop)
    panel = mine * slabs

    sent = []
    for d in range(1, blocks + 1):
        block = d % blocks
        total, hankel, norm = stack(tables[block], hankel, norm, panels, block, panel, slots, comps, hop, span, samples)
        if block:
            pairs = [(t, (t + d) % blocks) for t in range(blocks)]
            sent.append(lax.ppermute(total, "tpl", pairs))
    for piece in sent:
        total = total + piece
    return total


def solution(mesh):
    return jax.shard_map(
        per_device,
        mesh=mesh,
        in_specs=(
            P("tpl", None, "slab"),
            P(("tpl", "slab"), None, None, None),
            P(("tpl", "slab"), None),
            P(("tpl", "slab"), None),
            P(("tpl", "slab")),
        ),
        out_specs=P("tpl", "slab"),
        check_vma=False,
    )
```

```python
import functools
import math

import jax
import jax.numpy as jnp
from jax import lax
from jax.experimental import pallas as pl
from jax.experimental.pallas import tpu as pltpu
from jax.sharding import PartitionSpec as P

MAXSHIFT = 256
EPS = 1e-05
MESH = pl.DeviceIdType.MESH

LANES = 128
LAGS = 32
TURNS = LANES // LAGS
PASS = 6
PLANE = 16
CHUNKS = 5
AHEAD = 7
FIELDS = 7
STEPS = 4
SEVERAL = 4


def normalized(rows):
    span = rows.shape[-1]
    centered = rows - jnp.mean(rows, axis=-1, keepdims=True)
    rms = jnp.sqrt(jnp.mean(centered * centered, axis=-1, keepdims=True) + EPS)
    return (centered / (rms * math.sqrt(span))).astype(jnp.bfloat16)


def fill(span, step, s, ext_ref, hankel_ref, norm_ref, plain_ref, turned_ref):
    width = ext_ref.shape[1]
    block = 256
    near = span // block
    nblocks = (width - span) // block
    tiles = width // LANES
    taps = lax.broadcasted_iota(jnp.int32, (block, block), 0)
    starts = lax.broadcasted_iota(jnp.int32, (block, block), 1)
    tail = jnp.where(taps >= starts, 1.0, 0.0).astype(jnp.bfloat16)
    head = jnp.where(taps < starts, 1.0, 0.0).astype(jnp.bfloat16)
    at = pl.ds(pl.multiple_of(s * step, step), step)
    stride = TURNS * PLANE
    base = pl.multiple_of(s * step * stride, step * stride)

    plain, both = [], []
    for n in range(width // block):
        values = ext_ref[at, n * block : (n + 1) * block]
        wide = values.astype(jnp.float32)
        for half in range(block // LANES):
            v = n * (block // LANES) + half
            plain_ref[pl.ds(v, step, stride=PLANE), :] = wide[:, half * LANES : (half + 1) * LANES]
        square = wide * wide
        high = square.astype(jnp.bfloat16)
        low = (square - high.astype(jnp.float32)).astype(jnp.bfloat16)
        plain.append(values)
        both.append(jnp.concatenate([high, low], axis=1))
    for v in range(tiles, PLANE):
        plain_ref[pl.ds(v, step, stride=PLANE), :] = jnp.zeros((step, LANES), jnp.float32)

    def window(pieces, weight):
        tails = jnp.dot(jnp.concatenate(pieces[:-1], axis=0), jnp.concatenate([tail] * weight, axis=0), preferred_element_type=jnp.float32)
        heads = jnp.dot(jnp.concatenate(pieces[near:], axis=0), jnp.concatenate([head] * weight, axis=0), preferred_element_type=jnp.float32)
        for n in range(nblocks):
            total = tails[n * step : (n + 1) * step, :] + heads[n * step : (n + 1) * step, :]
            for m in range(n + 1, n + near):
                total = total + tails[m * step : (m + 1) * step, :1]
            yield total

    for n, (sums, squares) in enumerate(zip(window(plain, 1), window(both, 2))):
        spread = (squares - sums * sums / span) / span
        inverse = lax.rsqrt(jnp.maximum(spread, 0.0) + EPS) * (1.0 / math.sqrt(span))
        inverse = inverse.astype(jnp.bfloat16).astype(jnp.float32)
        for half in range(block // LANES):
            v = n * (block // LANES) + half
            norm_ref[pl.ds(base + v, step, stride=stride), :] = inverse[:, half * LANES : (half + 1) * LANES]

    lane = lax.broadcasted_iota(jnp.int32, (PLANE, LANES), 1)

    @pl.loop(0, step // SEVERAL)
    def _(group):
        for q in range(SEVERAL):
            r = group * SEVERAL + q
            top = pl.multiple_of(r * PLANE, PLANE)
            here = plain_ref[pl.ds(top, PLANE), :]
            after = plain_ref[pl.ds(top + 1, PLANE), :]
            level_at = pl.multiple_of(base + r * stride, stride)
            level = norm_ref[pl.ds(level_at, PLANE), :]
            level_after = norm_ref[pl.ds(level_at + 1, PLANE), :]
            for turn in range(1, TURNS):
                keep = lane >= LAGS * turn
                back = LANES - LAGS * turn
                turned_ref[(q * TURNS + turn) * PLANE : (q * TURNS + turn + 1) * PLANE, :] = pltpu.roll(jnp.where(keep, here, after), back, 1)
                level_to = pl.ds(pl.multiple_of(level_at + turn * PLANE, PLANE), PLANE)
                norm_ref[level_to, :] = pltpu.roll(jnp.where(keep, level, level_after), back, 1)
        for q in range(SEVERAL):
            r = group * SEVERAL + q
            to = (s * step + r) * 2 * AHEAD
            for pair in range(2):
                for ahead in range(AHEAD):
                    parts = []
                    for turn in (2 * pair, 2 * pair + 1):
                        if turn == 0:
                            parts.append(plain_ref[pl.ds(r * PLANE + ahead, 8), :])
                        else:
                            rows = (q * TURNS + turn) * PLANE + ahead
                            parts.append(turned_ref[rows : rows + 8, :])
                    hankel_ref[to + pair * AHEAD + ahead] = jnp.concatenate(parts, axis=0).astype(jnp.bfloat16)


def exchange_kernel(reach, hop, data_ref, templates_ref, stations_ref, shifts_ref, used_ref, hankel_ref, norm_ref, panels_ref, *refs):
    table_refs, scratch = refs[: lax.axis_size("tpl")], refs[lax.axis_size("tpl") :]
    ext_ref, plain_ref, turned_ref, rows_ref, lists_ref, sta_ref, shf_ref, use_ref, loads = scratch[:9]
    halo_send, halo_recv, far_send, far_recv, side_send, side_recv, peer_send, peer_recv, mate_send, mate_recv = scratch[9:19]
    list_mate_send, list_mate_recv, list_far_send, list_far_recv, list_side_send, list_side_recv, list_peer_send, list_peer_recv = scratch[19:]
    rows, samples = data_ref.shape
    height = templates_ref.shape[0]
    mine, slots = stations_ref.shape
    slabs = lax.axis_size("slab")
    blocks = lax.axis_size("tpl")
    outer = slabs // 4
    slab = lax.axis_index("slab")
    tpl = lax.axis_index("tpl")
    core = lax.rem(slab, 2)
    mate = slab + 1 - 2 * core
    side = slab + 2 - 4 * lax.rem(slab // 2, 2)
    beside = lax.rem(slab + slabs - 1 + 2 * core, slabs)

    local = [
        pltpu.make_async_copy(templates_ref, rows_ref, loads.at[0]),
        pltpu.make_async_copy(stations_ref, sta_ref, loads.at[1]),
        pltpu.make_async_copy(shifts_ref, shf_ref, loads.at[2]),
        pltpu.make_async_copy(used_ref, use_ref, loads.at[3]),
        pltpu.make_async_copy(data_ref, ext_ref.at[:, :samples], loads.at[4]),
    ]
    for copy in local:
        copy.start()

    barrier = pltpu.get_barrier_semaphore()
    for d in range(1, blocks):
        pl.semaphore_signal(barrier, inc=1, device_id={"tpl": lax.rem(tpl + d, blocks)}, device_id_type=MESH)
    for d in range(1, outer):
        pl.semaphore_signal(barrier, inc=1, device_id={"slab": lax.rem(slab + 4 * d, slabs)}, device_id_type=MESH)
    for device in (mate, side, beside):
        pl.semaphore_signal(barrier, inc=1, device_id={"slab": device}, device_id_type=MESH)

    local[0].wait()
    panels_ref[pl.ds(pl.multiple_of(slab * height, height), height), :] = normalized(rows_ref[...].astype(jnp.float32))
    for copy in local[1:4]:
        copy.wait()
    lane = lax.broadcasted_iota(jnp.int32, (mine, LANES), 1)
    line = lax.broadcasted_iota(jnp.int32, (mine, LANES), 0)
    station = jnp.zeros((mine, LANES), jnp.int32)
    shift = jnp.zeros((mine, LANES), jnp.int32)
    used = jnp.zeros((mine, LANES), jnp.int32)
    for j in range(mine):
        used = jnp.where(line == j, use_ref[j], used)
        for k in range(slots):
            spot = jnp.logical_and(line == j, lane == k)
            station = jnp.where(spot, sta_ref[j, k], station)
            shift = jnp.where(spot, shf_ref[j, k], shift)
    owner = lax.div(station, hop)
    local_station = station - owner * hop
    half = lax.bitwise_and(lax.shift_right_logical(shift, 6), 1)
    first = lax.shift_right_logical(shift, 7)
    base = local_station * (TURNS * PLANE) + first
    fields = [
        jnp.where(lane < used, owner, -1),
        lax.bitwise_and(shift, 63),
        (2 * local_station + half) * AHEAD + first,
        (2 * local_station + 1 - half) * AHEAD + first + half,
        base + 2 * PLANE * half,
        base + 2 * PLANE * (1 - half) + half,
        used,
    ]
    packed = jnp.zeros((mine, LANES), jnp.int32)
    for f, values in enumerate(fields):
        kept = jnp.where(lane < slots, values, 0)
        packed = packed + (kept if f == 0 else pltpu.roll(kept, f * slots, 1))
    lists_ref[slab] = packed

    pl.semaphore_wait(barrier, blocks - 1 + outer - 1 + 3)

    def place(block, owner):
        at = (block * slabs + owner) * height
        return panels_ref.at[pl.ds(pl.multiple_of(at, height), height), :]

    def push(source, target, send, recv, device):
        return pltpu.make_async_remote_copy(
            src_ref=source, dst_ref=target, send_sem=send, recv_sem=recv, device_id=device, device_id_type=MESH)

    def owner_of(e, turn):
        start = slab + turn * (side - slab)
        return lax.rem(start + slabs - 4 * e, slabs)

    def halo_copy():
        return push(data_ref.at[:, :reach], ext_ref.at[:, samples:], halo_send, halo_recv, {"slab": lax.rem(slab + slabs - 1, slabs)})

    def far_copy(d):
        return push(place(0, slab), place(0, slab), far_send.at[d], far_recv.at[d], {"slab": lax.rem(slab + 4 * d, slabs)})

    def side_copy(e):
        at = place(0, owner_of(e, 0))
        return push(at, at, side_send.at[e], side_recv.at[e], {"slab": side})

    def peer_copy(d, e, turn):
        at = (d * outer + e) * 2 + turn
        unit = owner_of(e, turn)
        return push(place(0, unit), place(blocks - d, unit), peer_send.at[at], peer_recv.at[at], {"tpl": lax.rem(tpl + d, blocks)})

    def mate_copy(block, e, turn):
        at = (block * outer + e) * 2 + turn
        unit = place(block, owner_of(e, turn))
        return push(unit, unit, mate_send.at[at], mate_recv.at[at], {"slab": mate})

    def list_mate():
        return push(lists_ref.at[slab], lists_ref.at[slab], list_mate_send, list_mate_recv, {"slab": mate})

    def list_far(d):
        at = lists_ref.at[pl.ds(slab - core, 2)]
        return push(at, at, list_far_send.at[d], list_far_recv.at[d], {"slab": lax.rem(slab + 4 * d, slabs)})

    def list_side(e):
        at = lists_ref.at[pl.ds(owner_of(e, 0) - core, 2)]
        return push(at, at, list_side_send.at[e], list_side_recv.at[e], {"slab": side})

    def list_peer(d):
        return push(
            lists_ref.at[pl.ds(0, slabs)], lists_ref.at[pl.ds((blocks - d) * slabs, slabs)],
            list_peer_send.at[d], list_peer_recv.at[d], {"tpl": lax.rem(tpl + d, blocks)})

    def spread(e, turn):
        for d in range(1, blocks):
            peer_copy(d, e, turn).start()
        mate_copy(0, e, turn).start()

    begins = slab == 0
    ends = slab == slabs - 1
    list_mate().start()
    for d in range(1, outer):
        far_copy(d).start()

    @pl.when(jnp.logical_not(begins))
    def _():
        halo_copy().start()

    side_copy(0).start()
    spread(0, 0)
    local[4].wait()

    @pl.when(ends)
    def _():
        ext_ref[:, samples:] = jnp.zeros((rows, reach), ext_ref.dtype)

    for d in range(1, outer):
        far_copy(d).wait_recv()
        side_copy(d).start()
        spread(d, 0)
    list_mate().wait_recv()
    list_side(0).start()
    for d in range(1, outer):
        list_far(d).start()

    @pl.when(jnp.logical_not(ends))
    def _():
        halo_copy().wait_recv()

    @pl.loop(0, STEPS)
    def _(s):
        fill(templates_ref.shape[1], rows // STEPS, s, ext_ref, hankel_ref, norm_ref, plain_ref, turned_ref)

        @pl.when(s == 0)
        def _():
            for e in range(outer):
                side_copy(e).wait_recv()
                spread(e, 1)
            for d in range(1, outer):
                list_far(d).wait_recv()
                list_side(d).start()

        @pl.when(s == 1)
        def _():
            for e in range(outer):
                list_side(e).wait_recv()
            for d in range(1, blocks):
                list_peer(d).start()

        @pl.when(s >= 2)
        def _():
            for e in range(outer):
                for d in range(1, blocks):
                    peer_copy(d, e, s - 2).wait_recv()
                    mate_copy(blocks - d, e, s - 2).start()

    for d in range(1, blocks):
        list_peer(d).wait_recv()

    lanes = lax.broadcasted_iota(jnp.int32, (slabs, LANES), 1)
    for block in range(blocks):
        for j in range(mine):
            values = lists_ref[block * slabs : (block + 1) * slabs, j, :]
            near = jnp.where(values == tpl, 1, 0)
            table_refs[block][pl.ds(j, slabs, stride=mine), :] = jnp.where(lanes < slots, near, values)
        table_refs[block][slabs * mine :, :] = jnp.zeros((8, LANES), jnp.int32)

    for block in range(blocks):
        for turn in range(2):
            for e in range(outer):
                mate_copy(block, e, turn).wait_recv()

    @pl.when(jnp.logical_not(begins))
    def _():
        halo_copy().wait_send()

    list_mate().wait_send()
    for d in range(1, outer):
        far_copy(d).wait_send()
        list_far(d).wait_send()
    for d in range(1, blocks):
        list_peer(d).wait_send()
    for e in range(outer):
        side_copy(e).wait_send()
        list_side(e).wait_send()
        for turn in range(2):
            for d in range(1, blocks):
                peer_copy(d, e, turn).wait_send()
            for block in range(blocks):
                mate_copy(block, e, turn).wait_send()


def exchange(local, rows, stations, shifts, used, reach, hop):
    slabs = lax.axis_size("slab")
    blocks = lax.axis_size("tpl")
    height, span = rows.shape
    outer = slabs // 4
    vmem = pl.BlockSpec(memory_space=pltpu.VMEM)
    dma = pltpu.SemaphoreType.DMA
    one, few, all_units = [dma] * 2, [dma((outer,))] * 2, [dma((blocks * outer * 2,))] * 2
    return pl.pallas_call(
        functools.partial(exchange_kernel, reach, hop),
        out_shape=(
            jax.ShapeDtypeStruct((local.shape[0] * 2 * AHEAD, 16, LANES), local.dtype),
            jax.ShapeDtypeStruct((local.shape[0] * TURNS * PLANE, LANES), jnp.float32),
            jax.ShapeDtypeStruct((height * slabs * blocks, span), rows.dtype),
        ) + (jax.ShapeDtypeStruct((slabs * stations.shape[0] + 8, LANES), jnp.int32),) * blocks,
        in_specs=[pl.BlockSpec(memory_space=pltpu.HBM)] * 5,
        out_specs=(vmem,) * (3 + blocks),
        scratch_shapes=[
            pltpu.VMEM((local.shape[0], local.shape[1] + reach), local.dtype),
            pltpu.VMEM(((local.shape[0] // STEPS + 1) * PLANE, LANES), jnp.float32),
            pltpu.VMEM((SEVERAL * TURNS * PLANE, LANES), jnp.float32),
            pltpu.VMEM(rows.shape, rows.dtype),
            pltpu.VMEM((slabs * blocks, stations.shape[0], LANES), jnp.int32),
            pltpu.SMEM(stations.shape, jnp.int32),
            pltpu.SMEM(shifts.shape, jnp.int32),
            pltpu.SMEM(used.shape, jnp.int32),
            dma((5,)),
        ] + one + few + few + all_units + all_units + one + few + few + [dma((blocks,))] * 2,
        compiler_params=pltpu.CompilerParams(
            collective_id=0, has_side_effects=True, vmem_limit_bytes=24 << 20
        ),
    )(local, rows, stations, shifts, used)


def stack_kernel(span, comps, hop, slots, panel, block, table_ref, hankel_ref, norm_ref, panels_ref, out_ref,
                 hankel_out_ref, norm_out_ref, unit_ref, turned_ref, right_ref, level_ref, sum_ref, done_ref, item_ref):
    parts = span // LANES
    group = comps * slots
    count = panel * slots

    height = 2 * group
    @pl.loop(0, panel // 2)
    def _(step):
        at = pl.ds(pl.multiple_of((block * panel + 2 * step) * group, height), height)
        values = panels_ref[at, :].astype(jnp.float32)
        for t in range(2):
            for c in range(comps):
                for part in range(parts):
                    piece = values[t * group + c * slots : t * group + (c + 1) * slots, part * LANES : (part + 1) * LANES]
                    unit_ref[pl.ds((step * 2 + t) * slots * PLANE + c * parts + part, slots, stride=PLANE), :] = piece

    unit_ref[count * PLANE : (count + 1) * PLANE, :] = jnp.zeros((PLANE, LANES), jnp.float32)

    def collect(j, total):
        sum_ref[j] = jnp.zeros((TURNS * 8, LAGS), jnp.float32)
        for k in range(slots):
            item_ref[total] = j * LANES + k
            total = total + table_ref[j, k]
        return total

    total = lax.fori_loop(0, panel, collect, 0)
    for k in range(2 * PASS):
        item_ref[total + k] = panel * LANES
    sum_ref[panel] = jnp.zeros((TURNS * 8, LAGS), jnp.float32)

    lane_half = lax.broadcasted_iota(jnp.int32, (16, LANES), 1).astype(jnp.float32).astype(jnp.bfloat16)
    lag_half = lax.broadcasted_iota(jnp.int32, (16, LANES), 0).astype(jnp.float32).astype(jnp.bfloat16)
    ahead = lane_half - lag_half
    further = ahead - jnp.full((16, LANES), 16.0, jnp.bfloat16)
    none = jnp.zeros((16, LANES), jnp.bfloat16)

    def field(g, n, which):
        item = item_ref[g * PASS + n]
        return table_ref[lax.shift_right_logical(item, 7), lax.bitwise_and(item, LANES - 1) + which * slots]

    def turn_rows(g):
        for n in range(PASS):
            item = item_ref[g * PASS + n]
            slot = lax.shift_right_logical(item, 7) * slots + lax.bitwise_and(item, LANES - 1)
            rows = unit_ref[pl.ds(pl.multiple_of(slot * PLANE, PLANE), PLANE), :]
            turned_ref[n * PLANE : (n + 1) * PLANE, :] = pltpu.roll(rows, field(g, n, 1), 1)

    def build_slot(g, n):
        bound = jnp.full((16, LANES), field(g, n, 1), jnp.int32).astype(jnp.float32).astype(jnp.bfloat16)
        inside = [ahead >= bound, further >= bound]
        for c in range(comps):
            turned = []
            for part in range(parts):
                line = jnp.broadcast_to(turned_ref[n * PLANE + c * parts + part : n * PLANE + c * parts + part + 1, :], (8, LANES))
                lags = pltpu.roll(line, 0, 1, stride=1, stride_axis=0)
                low = jnp.concatenate([lags, pltpu.roll(lags, 8, 1)], axis=0).astype(jnp.bfloat16)
                turned.append((low, pltpu.roll(low, 16, 1)))
            edges = [(none, none)] + turned + [(none, none)]
            at = (n * comps + c) * LAGS
            for b in range(2):
                for p in range(parts + 1):
                    right_ref[at + 16 * b : at + 16 * b + 16, p * LANES : (p + 1) * LANES] = jnp.where(inside[b], edges[p + 1][b], edges[p][b])
        back = LANES - field(g, n, 1)
        for turn in range(TURNS):
            at = field(g, n, 4 + turn // 2)
            for c in range(comps):
                norm = norm_ref[pl.ds(at + c * hop * TURNS * PLANE + (turn % 2) * PLANE, 8), :]
                k = (n * comps + c) * TURNS + turn
                level_ref[k * 8 : k * 8 + 8, :] = pltpu.roll(norm, back, 1)

    def build(g):
        turn_rows(g)
        for n in range(PASS):
            build_slot(g, n)

    def multiply(g):
        for n in range(PASS):
            near = field(g, n, 2)
            far = field(g, n, 3)
            for c in range(comps):
                i = n * comps + c
                left = jnp.concatenate([
                    jnp.concatenate([hankel_ref[at + c * hop * 2 * AHEAD + p] for p in range(CHUNKS)], axis=1)
                    for at in (near, far)], axis=0)
                yield n, c, lax.dot_general(
                    left, right_ref[i * LAGS : (i + 1) * LAGS, :],
                    (((1,), (1,)), ((), ())), preferred_element_type=jnp.float32)

    def gather_slot(g, n, product):
        j = lax.shift_right_logical(item_ref[g * PASS + n], 7)
        added = []
        for turn in range(TURNS):
            value = None
            for c in range(comps):
                k = (n * comps + c) * TURNS + turn
                term = product(n, c, turn) * level_ref[k * 8 : k * 8 + 8, :LAGS]
                value = term if value is None else value + term
            added.append(value)
        sum_ref[j] += jnp.concatenate(added, axis=0)

    build(0)

    def body(g, _):
        products = {}
        for n, c, product in multiply(g):
            products[n, c] = product
            if c == comps - 1:
                gather_slot(g, n, lambda n, c, turn: products[n, c][8 * turn : 8 * turn + 8, :])
        build(g + 1)
        return 0

    lax.fori_loop(0, lax.div(total + PASS - 1, PASS), body, 0)

    def finish(j, _):
        value = sum_ref[j]
        result = jnp.concatenate([value[8 * turn : 8 * turn + 8, :] for turn in range(TURNS)], axis=1)
        used = jnp.full((8, LANES), table_ref[j, (FIELDS - 1) * slots], jnp.int32).astype(jnp.float32)
        done_ref[pl.ds(pl.multiple_of(j * 8, 8), 8), :] = result * jnp.sqrt(span / (3.0 * used))
        return 0

    lax.fori_loop(0, panel, finish, 0, unroll=4)
    for b in range(panel // 8):
        for a in range(out_ref.shape[1] // LANES):
            out_ref[b * 8 : b * 8 + 8, a * LANES : (a + 1) * LANES] = done_ref[pl.ds(b * 64 + a, 8, stride=8), :]


def stack(table, hankel, norm, panels, block, panel, slots, comps, hop, span, samples):
    smem = pl.BlockSpec(memory_space=pltpu.SMEM)
    vmem = pl.BlockSpec(memory_space=pltpu.VMEM)
    count = panel * slots
    return pl.pallas_call(
        functools.partial(stack_kernel, span, comps, hop, slots, panel, block),
        out_shape=(
            jax.ShapeDtypeStruct((panel, samples), jnp.float32),
            jax.ShapeDtypeStruct(hankel.shape, hankel.dtype),
            jax.ShapeDtypeStruct(norm.shape, norm.dtype),
        ),
        in_specs=[smem, vmem, vmem, vmem],
        out_specs=(vmem, vmem, vmem),
        input_output_aliases={1: 1, 2: 2},
        scratch_shapes=[
            pltpu.VMEM(((count + 1) * PLANE, LANES), jnp.float32),
            pltpu.VMEM((PASS * PLANE, LANES), jnp.float32),
            pltpu.VMEM((PASS * comps * LAGS, CHUNKS * LANES), jnp.bfloat16),
            pltpu.VMEM((PASS * comps * TURNS * 8, LANES), jnp.float32),
            pltpu.VMEM((panel + 1, TURNS * 8, LAGS), jnp.float32),
            pltpu.VMEM((panel * 8, LANES), jnp.float32),
            pltpu.SMEM((count + 3 * PASS,), jnp.int32),
        ],
        compiler_params=pltpu.CompilerParams(vmem_limit_bytes=(count * PLANE * LANES * 4) + (8 << 20)),
        cost_estimate=pl.CostEstimate(flops=6_000_000_000, bytes_accessed=20_000_000, transcendentals=0),
    )(table, hankel, norm, panels)


def per_device(data, templates, stations, shifts, used):
    mine, slots, comps, span = templates.shape
    hop, _, samples = data.shape
    reach = span + MAXSHIFT
    slabs = lax.axis_size("slab")
    blocks = lax.axis_size("tpl")
    local = jnp.transpose(data, (1, 0, 2)).reshape(-1, samples)
    rows = jnp.transpose(templates, (0, 2, 1, 3)).reshape(-1, span)
    inputs = [pltpu.with_memory_space_constraint(x, pltpu.HBM) for x in (local, rows, stations, shifts, used)]
    hankel, norm, panels, *tables = exchange(*inputs, reach, hop)
    panel = mine * slabs

    sent = []
    for d in range(1, blocks + 1):
        block = d % blocks
        total, hankel, norm = stack(tables[block], hankel, norm, panels, block, panel, slots, comps, hop, span, samples)
        if block:
            pairs = [(t, (t + d) % blocks) for t in range(blocks)]
            sent.append(lax.ppermute(total, "tpl", pairs))
    for piece in sent:
        total = total + piece
    return total


def solution(mesh):
    return jax.shard_map(
        per_device,
        mesh=mesh,
        in_specs=(
            P("tpl", None, "slab"),
            P(("tpl", "slab"), None, None, None),
            P(("tpl", "slab"), None),
            P(("tpl", "slab"), None),
            P(("tpl", "slab")),
        ),
        out_specs=P("tpl", "slab"),
        check_vma=False,
    )
```

```python
import functools
import math

import jax
import jax.numpy as jnp
from jax import lax
from jax.experimental import pallas as pl
from jax.experimental.pallas import tpu as pltpu
from jax.sharding import PartitionSpec as P

MAXSHIFT = 256
EPS = 1e-05
MESH = pl.DeviceIdType.MESH

LANES = 128
LAGS = 32
TURNS = LANES // LAGS
PASS = 6
PLANE = 16
CHUNKS = 5
AHEAD = 7
FIELDS = 7
STEPS = 4
SEVERAL = 16


def normalized(rows):
    span = rows.shape[-1]
    centered = rows - jnp.mean(rows, axis=-1, keepdims=True)
    rms = jnp.sqrt(jnp.mean(centered * centered, axis=-1, keepdims=True) + EPS)
    return (centered / (rms * math.sqrt(span))).astype(jnp.bfloat16)


def fill(span, step, s, ext_ref, hankel_ref, norm_ref, plain_ref, turned_ref):
    width = ext_ref.shape[1]
    block = 256
    near = span // block
    nblocks = (width - span) // block
    tiles = width // LANES
    taps = lax.broadcasted_iota(jnp.int32, (block, block), 0)
    starts = lax.broadcasted_iota(jnp.int32, (block, block), 1)
    tail = jnp.where(taps >= starts, 1.0, 0.0).astype(jnp.bfloat16)
    head = jnp.where(taps < starts, 1.0, 0.0).astype(jnp.bfloat16)
    at = pl.ds(pl.multiple_of(s * step, step), step)
    stride = TURNS * PLANE
    base = pl.multiple_of(s * step * stride, step * stride)

    plain, both = [], []
    for n in range(width // block):
        values = ext_ref[at, n * block : (n + 1) * block]
        wide = values.astype(jnp.float32)
        for half in range(block // LANES):
            v = n * (block // LANES) + half
            plain_ref[pl.ds(v, step, stride=PLANE), :] = wide[:, half * LANES : (half + 1) * LANES]
        square = wide * wide
        high = square.astype(jnp.bfloat16)
        low = (square - high.astype(jnp.float32)).astype(jnp.bfloat16)
        plain.append(values)
        both.append(jnp.concatenate([high, low], axis=1))
    for v in range(tiles, PLANE):
        plain_ref[pl.ds(v, step, stride=PLANE), :] = jnp.zeros((step, LANES), jnp.float32)

    def window(pieces, weight):
        tails = jnp.dot(jnp.concatenate(pieces[:-1], axis=0), jnp.concatenate([tail] * weight, axis=0), preferred_element_type=jnp.float32)
        heads = jnp.dot(jnp.concatenate(pieces[near:], axis=0), jnp.concatenate([head] * weight, axis=0), preferred_element_type=jnp.float32)
        for n in range(nblocks):
            total = tails[n * step : (n + 1) * step, :] + heads[n * step : (n + 1) * step, :]
            for m in range(n + 1, n + near):
                total = total + tails[m * step : (m + 1) * step, :1]
            yield total

    for n, (sums, squares) in enumerate(zip(window(plain, 1), window(both, 2))):
        spread = (squares - sums * sums / span) / span
        inverse = lax.rsqrt(jnp.maximum(spread, 0.0) + EPS) * (1.0 / math.sqrt(span))
        inverse = inverse.astype(jnp.bfloat16).astype(jnp.float32)
        for half in range(block // LANES):
            v = n * (block // LANES) + half
            norm_ref[pl.ds(base + v, step, stride=stride), :] = inverse[:, half * LANES : (half + 1) * LANES]

    lane = lax.broadcasted_iota(jnp.int32, (PLANE, LANES), 1)

    @pl.loop(0, step // SEVERAL)
    def _(group):
        for q in range(SEVERAL):
            r = group * SEVERAL + q
            top = pl.multiple_of(r * PLANE, PLANE)
            here = plain_ref[pl.ds(top, PLANE), :]
            after = plain_ref[pl.ds(top + 1, PLANE), :]
            level_at = pl.multiple_of(base + r * stride, stride)
            level = norm_ref[pl.ds(level_at, PLANE), :]
            level_after = norm_ref[pl.ds(level_at + 1, PLANE), :]
            for turn in range(1, TURNS):
                keep = lane >= LAGS * turn
                back = LANES - LAGS * turn
                turned_ref[(q * TURNS + turn) * PLANE : (q * TURNS + turn + 1) * PLANE, :] = pltpu.roll(jnp.where(keep, here, after), back, 1)
                level_to = pl.ds(pl.multiple_of(level_at + turn * PLANE, PLANE), PLANE)
                norm_ref[level_to, :] = pltpu.roll(jnp.where(keep, level, level_after), back, 1)
        for q in range(SEVERAL):
            r = group * SEVERAL + q
            to = (s * step + r) * 2 * AHEAD
            for pair in range(2):
                for ahead in range(AHEAD):
                    parts = []
                    for turn in (2 * pair, 2 * pair + 1):
                        if turn == 0:
                            parts.append(plain_ref[pl.ds(r * PLANE + ahead, 8), :])
                        else:
                            rows = (q * TURNS + turn) * PLANE + ahead
                            parts.append(turned_ref[rows : rows + 8, :])
                    hankel_ref[to + pair * AHEAD + ahead] = jnp.concatenate(parts, axis=0).astype(jnp.bfloat16)


def exchange_kernel(reach, hop, data_ref, templates_ref, stations_ref, shifts_ref, used_ref, hankel_ref, norm_ref, panels_ref, *refs):
    table_refs, scratch = refs[: lax.axis_size("tpl")], refs[lax.axis_size("tpl") :]
    ext_ref, plain_ref, turned_ref, rows_ref, lists_ref, sta_ref, shf_ref, use_ref, loads = scratch[:9]
    halo_send, halo_recv, far_send, far_recv, side_send, side_recv, peer_send, peer_recv, mate_send, mate_recv = scratch[9:19]
    list_mate_send, list_mate_recv, list_far_send, list_far_recv, list_side_send, list_side_recv, list_peer_send, list_peer_recv = scratch[19:]
    rows, samples = data_ref.shape
    height = templates_ref.shape[0]
    mine, slots = stations_ref.shape
    slabs = lax.axis_size("slab")
    blocks = lax.axis_size("tpl")
    outer = slabs // 4
    slab = lax.axis_index("slab")
    tpl = lax.axis_index("tpl")
    core = lax.rem(slab, 2)
    mate = slab + 1 - 2 * core
    side = slab + 2 - 4 * lax.rem(slab // 2, 2)
    beside = lax.rem(slab + slabs - 1 + 2 * core, slabs)

    local = [
        pltpu.make_async_copy(templates_ref, rows_ref, loads.at[0]),
        pltpu.make_async_copy(stations_ref, sta_ref, loads.at[1]),
        pltpu.make_async_copy(shifts_ref, shf_ref, loads.at[2]),
        pltpu.make_async_copy(used_ref, use_ref, loads.at[3]),
        pltpu.make_async_copy(data_ref, ext_ref.at[:, :samples], loads.at[4]),
    ]
    for copy in local:
        copy.start()

    barrier = pltpu.get_barrier_semaphore()
    for d in range(1, blocks):
        pl.semaphore_signal(barrier, inc=1, device_id={"tpl": lax.rem(tpl + d, blocks)}, device_id_type=MESH)
    for d in range(1, outer):
        pl.semaphore_signal(barrier, inc=1, device_id={"slab": lax.rem(slab + 4 * d, slabs)}, device_id_type=MESH)
    for device in (mate, side, beside):
        pl.semaphore_signal(barrier, inc=1, device_id={"slab": device}, device_id_type=MESH)

    local[0].wait()
    panels_ref[pl.ds(pl.multiple_of(slab * height, height), height), :] = normalized(rows_ref[...].astype(jnp.float32))
    for copy in local[1:4]:
        copy.wait()
    lane = lax.broadcasted_iota(jnp.int32, (mine, LANES), 1)
    line = lax.broadcasted_iota(jnp.int32, (mine, LANES), 0)
    station = jnp.zeros((mine, LANES), jnp.int32)
    shift = jnp.zeros((mine, LANES), jnp.int32)
    used = jnp.zeros((mine, LANES), jnp.int32)
    for j in range(mine):
        used = jnp.where(line == j, use_ref[j], used)
        for k in range(slots):
            spot = jnp.logical_and(line == j, lane == k)
            station = jnp.where(spot, sta_ref[j, k], station)
            shift = jnp.where(spot, shf_ref[j, k], shift)
    owner = lax.div(station, hop)
    local_station = station - owner * hop
    half = lax.bitwise_and(lax.shift_right_logical(shift, 6), 1)
    first = lax.shift_right_logical(shift, 7)
    base = local_station * (TURNS * PLANE) + first
    fields = [
        jnp.where(lane < used, owner, -1),
        lax.bitwise_and(shift, 63),
        (2 * local_station + half) * AHEAD + first,
        (2 * local_station + 1 - half) * AHEAD + first + half,
        base + 2 * PLANE * half,
        base + 2 * PLANE * (1 - half) + half,
        used,
    ]
    packed = jnp.zeros((mine, LANES), jnp.int32)
    for f, values in enumerate(fields):
        kept = jnp.where(lane < slots, values, 0)
        packed = packed + (kept if f == 0 else pltpu.roll(kept, f * slots, 1))
    lists_ref[slab] = packed

    pl.semaphore_wait(barrier, blocks - 1 + outer - 1 + 3)

    def place(block, owner):
        at = (block * slabs + owner) * height
        return panels_ref.at[pl.ds(pl.multiple_of(at, height), height), :]

    def push(source, target, send, recv, device):
        return pltpu.make_async_remote_copy(
            src_ref=source, dst_ref=target, send_sem=send, recv_sem=recv, device_id=device, device_id_type=MESH)

    def owner_of(e, turn):
        start = slab + turn * (side - slab)
        return lax.rem(start + slabs - 4 * e, slabs)

    def halo_copy():
        return push(data_ref.at[:, :reach], ext_ref.at[:, samples:], halo_send, halo_recv, {"slab": lax.rem(slab + slabs - 1, slabs)})

    def far_copy(d):
        return push(place(0, slab), place(0, slab), far_send.at[d], far_recv.at[d], {"slab": lax.rem(slab + 4 * d, slabs)})

    def side_copy(e):
        at = place(0, owner_of(e, 0))
        return push(at, at, side_send.at[e], side_recv.at[e], {"slab": side})

    def peer_copy(d, e, turn):
        at = (d * outer + e) * 2 + turn
        unit = owner_of(e, turn)
        return push(place(0, unit), place(blocks - d, unit), peer_send.at[at], peer_recv.at[at], {"tpl": lax.rem(tpl + d, blocks)})

    def mate_copy(block, e, turn):
        at = (block * outer + e) * 2 + turn
        unit = place(block, owner_of(e, turn))
        return push(unit, unit, mate_send.at[at], mate_recv.at[at], {"slab": mate})

    def list_mate():
        return push(lists_ref.at[slab], lists_ref.at[slab], list_mate_send, list_mate_recv, {"slab": mate})

    def list_far(d):
        at = lists_ref.at[pl.ds(slab - core, 2)]
        return push(at, at, list_far_send.at[d], list_far_recv.at[d], {"slab": lax.rem(slab + 4 * d, slabs)})

    def list_side(e):
        at = lists_ref.at[pl.ds(owner_of(e, 0) - core, 2)]
        return push(at, at, list_side_send.at[e], list_side_recv.at[e], {"slab": side})

    def list_peer(d):
        return push(
            lists_ref.at[pl.ds(0, slabs)], lists_ref.at[pl.ds((blocks - d) * slabs, slabs)],
            list_peer_send.at[d], list_peer_recv.at[d], {"tpl": lax.rem(tpl + d, blocks)})

    def spread(e, turn):
        for d in range(1, blocks):
            peer_copy(d, e, turn).start()
        mate_copy(0, e, turn).start()

    begins = slab == 0
    ends = slab == slabs - 1
    list_mate().start()
    for d in range(1, outer):
        far_copy(d).start()

    @pl.when(jnp.logical_not(begins))
    def _():
        halo_copy().start()

    side_copy(0).start()
    spread(0, 0)
    local[4].wait()

    @pl.when(ends)
    def _():
        ext_ref[:, samples:] = jnp.zeros((rows, reach), ext_ref.dtype)

    for d in range(1, outer):
        far_copy(d).wait_recv()
        side_copy(d).start()
        spread(d, 0)
    list_mate().wait_recv()
    list_side(0).start()
    for d in range(1, outer):
        list_far(d).start()

    @pl.when(jnp.logical_not(ends))
    def _():
        halo_copy().wait_recv()

    @pl.loop(0, STEPS)
    def _(s):
        fill(templates_ref.shape[1], rows // STEPS, s, ext_ref, hankel_ref, norm_ref, plain_ref, turned_ref)

        @pl.when(s == 0)
        def _():
            for e in range(outer):
                side_copy(e).wait_recv()
                spread(e, 1)
            for d in range(1, outer):
                list_far(d).wait_recv()
                list_side(d).start()

        @pl.when(s == 1)
        def _():
            for e in range(outer):
                list_side(e).wait_recv()
            for d in range(1, blocks):
                list_peer(d).start()

        @pl.when(s >= 2)
        def _():
            for e in range(outer):
                for d in range(1, blocks):
                    peer_copy(d, e, s - 2).wait_recv()
                    mate_copy(blocks - d, e, s - 2).start()

    for d in range(1, blocks):
        list_peer(d).wait_recv()

    lanes = lax.broadcasted_iota(jnp.int32, (slabs, LANES), 1)
    for block in range(blocks):
        for j in range(mine):
            values = lists_ref[block * slabs : (block + 1) * slabs, j, :]
            near = jnp.where(values == tpl, 1, 0)
            table_refs[block][pl.ds(j, slabs, stride=mine), :] = jnp.where(lanes < slots, near, values)
        table_refs[block][slabs * mine :, :] = jnp.zeros((8, LANES), jnp.int32)

    for block in range(blocks):
        for turn in range(2):
            for e in range(outer):
                mate_copy(block, e, turn).wait_recv()

    @pl.when(jnp.logical_not(begins))
    def _():
        halo_copy().wait_send()

    list_mate().wait_send()
    for d in range(1, outer):
        far_copy(d).wait_send()
        list_far(d).wait_send()
    for d in range(1, blocks):
        list_peer(d).wait_send()
    for e in range(outer):
        side_copy(e).wait_send()
        list_side(e).wait_send()
        for turn in range(2):
            for d in range(1, blocks):
                peer_copy(d, e, turn).wait_send()
            for block in range(blocks):
                mate_copy(block, e, turn).wait_send()


def exchange(local, rows, stations, shifts, used, reach, hop):
    slabs = lax.axis_size("slab")
    blocks = lax.axis_size("tpl")
    height, span = rows.shape
    outer = slabs // 4
    vmem = pl.BlockSpec(memory_space=pltpu.VMEM)
    dma = pltpu.SemaphoreType.DMA
    one, few, all_units = [dma] * 2, [dma((outer,))] * 2, [dma((blocks * outer * 2,))] * 2
    return pl.pallas_call(
        functools.partial(exchange_kernel, reach, hop),
        out_shape=(
            jax.ShapeDtypeStruct((local.shape[0] * 2 * AHEAD, 16, LANES), local.dtype),
            jax.ShapeDtypeStruct((local.shape[0] * TURNS * PLANE, LANES), jnp.float32),
            jax.ShapeDtypeStruct((height * slabs * blocks, span), rows.dtype),
        ) + (jax.ShapeDtypeStruct((slabs * stations.shape[0] + 8, LANES), jnp.int32),) * blocks,
        in_specs=[pl.BlockSpec(memory_space=pltpu.HBM)] * 5,
        out_specs=(vmem,) * (3 + blocks),
        scratch_shapes=[
            pltpu.VMEM((local.shape[0], local.shape[1] + reach), local.dtype),
            pltpu.VMEM(((local.shape[0] // STEPS + 1) * PLANE, LANES), jnp.float32),
            pltpu.VMEM((SEVERAL * TURNS * PLANE, LANES), jnp.float32),
            pltpu.VMEM(rows.shape, rows.dtype),
            pltpu.VMEM((slabs * blocks, stations.shape[0], LANES), jnp.int32),
            pltpu.SMEM(stations.shape, jnp.int32),
            pltpu.SMEM(shifts.shape, jnp.int32),
            pltpu.SMEM(used.shape, jnp.int32),
            dma((5,)),
        ] + one + few + few + all_units + all_units + one + few + few + [dma((blocks,))] * 2,
        compiler_params=pltpu.CompilerParams(
            collective_id=0, has_side_effects=True, vmem_limit_bytes=24 << 20
        ),
    )(local, rows, stations, shifts, used)


def stack_kernel(span, comps, hop, slots, panel, block, table_ref, hankel_ref, norm_ref, panels_ref, out_ref,
                 hankel_out_ref, norm_out_ref, unit_ref, turned_ref, right_ref, level_ref, sum_ref, done_ref, item_ref):
    parts = span // LANES
    group = comps * slots
    count = panel * slots

    height = 2 * group
    unit_ref[count * PLANE : (count + 1) * PLANE, :] = jnp.zeros((PLANE, LANES), jnp.float32)

    def collect(step, total):
        at = pl.ds(pl.multiple_of((block * panel + 2 * step) * group, height), height)
        values = panels_ref[at, :].astype(jnp.float32)
        for t in range(2):
            j = 2 * step + t
            for c in range(comps):
                for part in range(parts):
                    piece = values[t * group + c * slots : t * group + (c + 1) * slots, part * LANES : (part + 1) * LANES]
                    unit_ref[pl.ds(j * slots * PLANE + c * parts + part, slots, stride=PLANE), :] = piece
            sum_ref[j] = jnp.zeros((TURNS * 8, LAGS), jnp.float32)
            for k in range(slots):
                item_ref[total] = j * LANES + k
                total = total + table_ref[j, k]
        return total

    total = lax.fori_loop(0, panel // 2, collect, 0, unroll=2)
    for k in range(2 * PASS):
        item_ref[total + k] = panel * LANES
    sum_ref[panel] = jnp.zeros((TURNS * 8, LAGS), jnp.float32)

    lane_half = lax.broadcasted_iota(jnp.int32, (16, LANES), 1).astype(jnp.float32).astype(jnp.bfloat16)
    lag_half = lax.broadcasted_iota(jnp.int32, (16, LANES), 0).astype(jnp.float32).astype(jnp.bfloat16)
    ahead = lane_half - lag_half
    further = ahead - jnp.full((16, LANES), 16.0, jnp.bfloat16)
    none = jnp.zeros((16, LANES), jnp.bfloat16)

    def field(g, n, which):
        item = item_ref[g * PASS + n]
        return table_ref[lax.shift_right_logical(item, 7), lax.bitwise_and(item, LANES - 1) + which * slots]

    def turn_rows(g):
        for n in range(PASS):
            item = item_ref[g * PASS + n]
            slot = lax.shift_right_logical(item, 7) * slots + lax.bitwise_and(item, LANES - 1)
            rows = unit_ref[pl.ds(pl.multiple_of(slot * PLANE, PLANE), PLANE), :]
            turned_ref[n * PLANE : (n + 1) * PLANE, :] = pltpu.roll(rows, field(g, n, 1), 1)

    def build_slot(g, n):
        bound = jnp.full((16, LANES), field(g, n, 1), jnp.int32).astype(jnp.float32).astype(jnp.bfloat16)
        inside = [ahead >= bound, further >= bound]
        for c in range(comps):
            turned = []
            for part in range(parts):
                line = jnp.broadcast_to(turned_ref[n * PLANE + c * parts + part : n * PLANE + c * parts + part + 1, :], (8, LANES))
                lags = pltpu.roll(line, 0, 1, stride=1, stride_axis=0)
                low = jnp.concatenate([lags, pltpu.roll(lags, 8, 1)], axis=0).astype(jnp.bfloat16)
                turned.append((low, pltpu.roll(low, 16, 1)))
            edges = [(none, none)] + turned + [(none, none)]
            at = (n * comps + c) * LAGS
            for b in range(2):
                for p in range(parts + 1):
                    right_ref[at + 16 * b : at + 16 * b + 16, p * LANES : (p + 1) * LANES] = jnp.where(inside[b], edges[p + 1][b], edges[p][b])
        back = LANES - field(g, n, 1)
        for turn in range(TURNS):
            at = field(g, n, 4 + turn // 2)
            for c in range(comps):
                norm = norm_ref[pl.ds(at + c * hop * TURNS * PLANE + (turn % 2) * PLANE, 8), :]
                k = (n * comps + c) * TURNS + turn
                level_ref[k * 8 : k * 8 + 8, :] = pltpu.roll(norm, back, 1)

    def build(g):
        turn_rows(g)
        for n in range(PASS):
            build_slot(g, n)

    def multiply(g):
        for n in range(PASS):
            near = field(g, n, 2)
            far = field(g, n, 3)
            for c in range(comps):
                i = n * comps + c
                left = jnp.concatenate([
                    jnp.concatenate([hankel_ref[at + c * hop * 2 * AHEAD + p] for p in range(CHUNKS)], axis=1)
                    for at in (near, far)], axis=0)
                yield n, c, lax.dot_general(
                    left, right_ref[i * LAGS : (i + 1) * LAGS, :],
                    (((1,), (1,)), ((), ())), preferred_element_type=jnp.float32)

    def gather_slot(g, n, product):
        j = lax.shift_right_logical(item_ref[g * PASS + n], 7)
        added = []
        for turn in range(TURNS):
            value = None
            for c in range(comps):
                k = (n * comps + c) * TURNS + turn
                term = product(n, c, turn) * level_ref[k * 8 : k * 8 + 8, :LAGS]
                value = term if value is None else value + term
            added.append(value)
        sum_ref[j] += jnp.concatenate(added, axis=0)

    build(0)

    def body(g, _):
        products = {}
        for n, c, product in multiply(g):
            products[n, c] = product
            if c == comps - 1:
                gather_slot(g, n, lambda n, c, turn: products[n, c][8 * turn : 8 * turn + 8, :])
        build(g + 1)
        return 0

    lax.fori_loop(0, lax.div(total + PASS - 1, PASS), body, 0)

    def finish(j, _):
        value = sum_ref[j]
        result = jnp.concatenate([value[8 * turn : 8 * turn + 8, :] for turn in range(TURNS)], axis=1)
        used = jnp.full((8, LANES), table_ref[j, (FIELDS - 1) * slots], jnp.int32).astype(jnp.float32)
        done_ref[pl.ds(pl.multiple_of(j * 8, 8), 8), :] = result * jnp.sqrt(span / (3.0 * used))
        return 0

    lax.fori_loop(0, panel, finish, 0, unroll=16)
    for b in range(panel // 8):
        for a in range(out_ref.shape[1] // LANES):
            out_ref[b * 8 : b * 8 + 8, a * LANES : (a + 1) * LANES] = done_ref[pl.ds(b * 64 + a, 8, stride=8), :]


def stack(table, hankel, norm, panels, block, panel, slots, comps, hop, span, samples):
    smem = pl.BlockSpec(memory_space=pltpu.SMEM)
    vmem = pl.BlockSpec(memory_space=pltpu.VMEM)
    count = panel * slots
    return pl.pallas_call(
        functools.partial(stack_kernel, span, comps, hop, slots, panel, block),
        out_shape=(
            jax.ShapeDtypeStruct((panel, samples), jnp.float32),
            jax.ShapeDtypeStruct(hankel.shape, hankel.dtype),
            jax.ShapeDtypeStruct(norm.shape, norm.dtype),
        ),
        in_specs=[smem, vmem, vmem, vmem],
        out_specs=(vmem, vmem, vmem),
        input_output_aliases={1: 1, 2: 2},
        scratch_shapes=[
            pltpu.VMEM(((count + 1) * PLANE, LANES), jnp.float32),
            pltpu.VMEM((PASS * PLANE, LANES), jnp.float32),
            pltpu.VMEM((PASS * comps * LAGS, CHUNKS * LANES), jnp.bfloat16),
            pltpu.VMEM((PASS * comps * TURNS * 8, LANES), jnp.float32),
            pltpu.VMEM((panel + 1, TURNS * 8, LAGS), jnp.float32),
            pltpu.VMEM((panel * 8, LANES), jnp.float32),
            pltpu.SMEM((count + 3 * PASS,), jnp.int32),
        ],
        compiler_params=pltpu.CompilerParams(vmem_limit_bytes=(count * PLANE * LANES * 4) + (8 << 20)),
        cost_estimate=pl.CostEstimate(flops=6_000_000_000, bytes_accessed=20_000_000, transcendentals=0),
    )(table, hankel, norm, panels)


def per_device(data, templates, stations, shifts, used):
    mine, slots, comps, span = templates.shape
    hop, _, samples = data.shape
    reach = span + MAXSHIFT
    slabs = lax.axis_size("slab")
    blocks = lax.axis_size("tpl")
    local = jnp.transpose(data, (1, 0, 2)).reshape(-1, samples)
    rows = jnp.transpose(templates, (0, 2, 1, 3)).reshape(-1, span)
    inputs = [pltpu.with_memory_space_constraint(x, pltpu.HBM) for x in (local, rows, stations, shifts, used)]
    hankel, norm, panels, *tables = exchange(*inputs, reach, hop)
    panel = mine * slabs

    sent = []
    for d in range(1, blocks + 1):
        block = d % blocks
        total, hankel, norm = stack(tables[block], hankel, norm, panels, block, panel, slots, comps, hop, span, samples)
        if block:
            pairs = [(t, (t + d) % blocks) for t in range(blocks)]
            sent.append(lax.ppermute(total, "tpl", pairs))
    for piece in sent:
        total = total + piece
    return total


def solution(mesh):
    return jax.shard_map(
        per_device,
        mesh=mesh,
        in_specs=(
            P("tpl", None, "slab"),
            P(("tpl", "slab"), None, None, None),
            P(("tpl", "slab"), None),
            P(("tpl", "slab"), None),
            P(("tpl", "slab")),
        ),
        out_specs=P("tpl", "slab"),
        check_vma=False,
    )
```

```python
import functools
import math

import jax
import jax.numpy as jnp
from jax import lax
from jax.experimental import pallas as pl
from jax.experimental.pallas import tpu as pltpu
from jax.sharding import PartitionSpec as P

MAXSHIFT = 256
EPS = 1e-05
MESH = pl.DeviceIdType.MESH

LANES = 128
LAGS = 32
TURNS = LANES // LAGS
PASS = 6
PLANE = 16
CHUNKS = 5
AHEAD = 7
FIELDS = 7
STEPS = 4
SEVERAL = 16


def normalized(rows):
    span = rows.shape[-1]
    centered = rows - jnp.mean(rows, axis=-1, keepdims=True)
    rms = jnp.sqrt(jnp.mean(centered * centered, axis=-1, keepdims=True) + EPS)
    return (centered / (rms * math.sqrt(span))).astype(jnp.bfloat16)


def fill(span, step, s, ext_ref, hankel_ref, norm_ref, plain_ref, turned_ref):
    width = ext_ref.shape[1]
    block = 256
    near = span // block
    nblocks = (width - span) // block
    tiles = width // LANES
    taps = lax.broadcasted_iota(jnp.int32, (block, block), 0)
    starts = lax.broadcasted_iota(jnp.int32, (block, block), 1)
    tail = jnp.where(taps >= starts, 1.0, 0.0).astype(jnp.bfloat16)
    head = jnp.where(taps < starts, 1.0, 0.0).astype(jnp.bfloat16)
    at = pl.ds(pl.multiple_of(s * step, step), step)
    stride = TURNS * PLANE
    base = pl.multiple_of(s * step * stride, step * stride)

    plain, both = [], []
    for n in range(width // block):
        values = ext_ref[at, n * block : (n + 1) * block]
        wide = values.astype(jnp.float32)
        for half in range(block // LANES):
            v = n * (block // LANES) + half
            plain_ref[pl.ds(v, step, stride=PLANE), :] = wide[:, half * LANES : (half + 1) * LANES]
        square = wide * wide
        high = square.astype(jnp.bfloat16)
        low = (square - high.astype(jnp.float32)).astype(jnp.bfloat16)
        plain.append(values)
        both.append(jnp.concatenate([high, low], axis=1))
    for v in range(tiles, PLANE):
        plain_ref[pl.ds(v, step, stride=PLANE), :] = jnp.zeros((step, LANES), jnp.float32)

    def window(pieces, weight):
        tails = jnp.dot(jnp.concatenate(pieces[:-1], axis=0), jnp.concatenate([tail] * weight, axis=0), preferred_element_type=jnp.float32)
        heads = jnp.dot(jnp.concatenate(pieces[near:], axis=0), jnp.concatenate([head] * weight, axis=0), preferred_element_type=jnp.float32)
        for n in range(nblocks):
            total = tails[n * step : (n + 1) * step, :] + heads[n * step : (n + 1) * step, :]
            for m in range(n + 1, n + near):
                total = total + tails[m * step : (m + 1) * step, :1]
            yield total

    for n, (sums, squares) in enumerate(zip(window(plain, 1), window(both, 2))):
        spread = (squares - sums * sums / span) / span
        inverse = lax.rsqrt(jnp.maximum(spread, 0.0) + EPS) * (1.0 / math.sqrt(span))
        inverse = inverse.astype(jnp.bfloat16).astype(jnp.float32)
        for half in range(block // LANES):
            v = n * (block // LANES) + half
            norm_ref[pl.ds(base + v, step, stride=stride), :] = inverse[:, half * LANES : (half + 1) * LANES]

    lane = lax.broadcasted_iota(jnp.int32, (PLANE, LANES), 1)

    @pl.loop(0, step // SEVERAL)
    def _(group):
        for q in range(SEVERAL):
            r = group * SEVERAL + q
            top = pl.multiple_of(r * PLANE, PLANE)
            here = plain_ref[pl.ds(top, PLANE), :]
            after = plain_ref[pl.ds(top + 1, PLANE), :]
            level_at = pl.multiple_of(base + r * stride, stride)
            level = norm_ref[pl.ds(level_at, PLANE), :]
            level_after = norm_ref[pl.ds(level_at + 1, PLANE), :]
            for turn in range(1, TURNS):
                keep = lane >= LAGS * turn
                back = LANES - LAGS * turn
                turned_ref[(q * TURNS + turn) * PLANE : (q * TURNS + turn + 1) * PLANE, :] = pltpu.roll(jnp.where(keep, here, after), back, 1)
                level_to = pl.ds(pl.multiple_of(level_at + turn * PLANE, PLANE), PLANE)
                norm_ref[level_to, :] = pltpu.roll(jnp.where(keep, level, level_after), back, 1)
        for q in range(SEVERAL):
            r = group * SEVERAL + q
            to = (s * step + r) * 2 * AHEAD
            for pair in range(2):
                for ahead in range(AHEAD):
                    parts = []
                    for turn in (2 * pair, 2 * pair + 1):
                        if turn == 0:
                            parts.append(plain_ref[pl.ds(r * PLANE + ahead, 8), :])
                        else:
                            rows = (q * TURNS + turn) * PLANE + ahead
                            parts.append(turned_ref[rows : rows + 8, :])
                    hankel_ref[to + pair * AHEAD + ahead] = jnp.concatenate(parts, axis=0).astype(jnp.bfloat16)


def exchange_kernel(reach, hop, data_ref, templates_ref, stations_ref, shifts_ref, used_ref, hankel_ref, norm_ref, panels_ref, *refs):
    table_refs, scratch = refs[: lax.axis_size("tpl")], refs[lax.axis_size("tpl") :]
    ext_ref, plain_ref, turned_ref, rows_ref, lists_ref, sta_ref, shf_ref, use_ref, loads = scratch[:9]
    halo_send, halo_recv, far_send, far_recv, side_send, side_recv, peer_send, peer_recv, mate_send, mate_recv = scratch[9:19]
    list_mate_send, list_mate_recv, list_far_send, list_far_recv, list_side_send, list_side_recv, list_peer_send, list_peer_recv = scratch[19:]
    rows, samples = data_ref.shape
    height = templates_ref.shape[0]
    mine, slots = stations_ref.shape
    slabs = lax.axis_size("slab")
    blocks = lax.axis_size("tpl")
    outer = slabs // 4
    slab = lax.axis_index("slab")
    tpl = lax.axis_index("tpl")
    core = lax.rem(slab, 2)
    mate = slab + 1 - 2 * core
    side = slab + 2 - 4 * lax.rem(slab // 2, 2)
    beside = lax.rem(slab + slabs - 1 + 2 * core, slabs)

    local = [
        pltpu.make_async_copy(templates_ref, rows_ref, loads.at[0]),
        pltpu.make_async_copy(stations_ref, sta_ref, loads.at[1]),
        pltpu.make_async_copy(shifts_ref, shf_ref, loads.at[2]),
        pltpu.make_async_copy(used_ref, use_ref, loads.at[3]),
        pltpu.make_async_copy(data_ref, ext_ref.at[:, :samples], loads.at[4]),
    ]
    for copy in local:
        copy.start()

    barrier = pltpu.get_barrier_semaphore()
    for d in range(1, blocks):
        pl.semaphore_signal(barrier, inc=1, device_id={"tpl": lax.rem(tpl + d, blocks)}, device_id_type=MESH)
    for d in range(1, outer):
        pl.semaphore_signal(barrier, inc=1, device_id={"slab": lax.rem(slab + 4 * d, slabs)}, device_id_type=MESH)
    for device in (mate, side, beside):
        pl.semaphore_signal(barrier, inc=1, device_id={"slab": device}, device_id_type=MESH)

    local[0].wait()
    panels_ref[pl.ds(pl.multiple_of(slab * height, height), height), :] = normalized(rows_ref[...].astype(jnp.float32))
    for copy in local[1:4]:
        copy.wait()
    lane = lax.broadcasted_iota(jnp.int32, (mine, LANES), 1)
    line = lax.broadcasted_iota(jnp.int32, (mine, LANES), 0)
    station = jnp.zeros((mine, LANES), jnp.int32)
    shift = jnp.zeros((mine, LANES), jnp.int32)
    used = jnp.zeros((mine, LANES), jnp.int32)
    for j in range(mine):
        used = jnp.where(line == j, use_ref[j], used)
        for k in range(slots):
            spot = jnp.logical_and(line == j, lane == k)
            station = jnp.where(spot, sta_ref[j, k], station)
            shift = jnp.where(spot, shf_ref[j, k], shift)
    owner = lax.div(station, hop)
    local_station = station - owner * hop
    half = lax.bitwise_and(lax.shift_right_logical(shift, 6), 1)
    first = lax.shift_right_logical(shift, 7)
    base = local_station * (TURNS * PLANE) + first
    fields = [
        jnp.where(lane < used, owner, -1),
        lax.bitwise_and(shift, 63),
        (2 * local_station + half) * AHEAD + first,
        (2 * local_station + 1 - half) * AHEAD + first + half,
        base + 2 * PLANE * half,
        base + 2 * PLANE * (1 - half) + half,
        used,
    ]
    packed = jnp.zeros((mine, LANES), jnp.int32)
    for f, values in enumerate(fields):
        kept = jnp.where(lane < slots, values, 0)
        packed = packed + (kept if f == 0 else pltpu.roll(kept, f * slots, 1))
    lists_ref[slab] = packed

    pl.semaphore_wait(barrier, blocks - 1 + outer - 1 + 3)

    def place(block, owner):
        at = (block * slabs + owner) * height
        return panels_ref.at[pl.ds(pl.multiple_of(at, height), height), :]

    def push(source, target, send, recv, device):
        return pltpu.make_async_remote_copy(
            src_ref=source, dst_ref=target, send_sem=send, recv_sem=recv, device_id=device, device_id_type=MESH)

    def owner_of(e, turn):
        start = slab + turn * (side - slab)
        return lax.rem(start + slabs - 4 * e, slabs)

    def halo_copy():
        return push(data_ref.at[:, :reach], ext_ref.at[:, samples:], halo_send, halo_recv, {"slab": lax.rem(slab + slabs - 1, slabs)})

    def far_copy(d):
        return push(place(0, slab), place(0, slab), far_send.at[d], far_recv.at[d], {"slab": lax.rem(slab + 4 * d, slabs)})

    def side_copy(e):
        at = place(0, owner_of(e, 0))
        return push(at, at, side_send.at[e], side_recv.at[e], {"slab": side})

    def peer_copy(d, e, turn):
        at = (d * outer + e) * 2 + turn
        unit = owner_of(e, turn)
        return push(place(0, unit), place(blocks - d, unit), peer_send.at[at], peer_recv.at[at], {"tpl": lax.rem(tpl + d, blocks)})

    def mate_copy(block, e, turn):
        at = (block * outer + e) * 2 + turn
        unit = place(block, owner_of(e, turn))
        return push(unit, unit, mate_send.at[at], mate_recv.at[at], {"slab": mate})

    def list_mate():
        return push(lists_ref.at[slab], lists_ref.at[slab], list_mate_send, list_mate_recv, {"slab": mate})

    def list_far(d):
        at = lists_ref.at[pl.ds(slab - core, 2)]
        return push(at, at, list_far_send.at[d], list_far_recv.at[d], {"slab": lax.rem(slab + 4 * d, slabs)})

    def list_side(e):
        at = lists_ref.at[pl.ds(owner_of(e, 0) - core, 2)]
        return push(at, at, list_side_send.at[e], list_side_recv.at[e], {"slab": side})

    def list_peer(d):
        return push(
            lists_ref.at[pl.ds(0, slabs)], lists_ref.at[pl.ds((blocks - d) * slabs, slabs)],
            list_peer_send.at[d], list_peer_recv.at[d], {"tpl": lax.rem(tpl + d, blocks)})

    def spread(e, turn):
        for d in range(1, blocks):
            peer_copy(d, e, turn).start()
        mate_copy(0, e, turn).start()

    begins = slab == 0
    ends = slab == slabs - 1
    list_mate().start()
    for d in range(1, outer):
        far_copy(d).start()

    @pl.when(jnp.logical_not(begins))
    def _():
        halo_copy().start()

    side_copy(0).start()
    spread(0, 0)
    local[4].wait()

    @pl.when(ends)
    def _():
        ext_ref[:, samples:] = jnp.zeros((rows, reach), ext_ref.dtype)

    list_mate().wait_recv()
    list_side(0).start()
    for d in range(1, outer):
        list_far(d).start()

    @pl.when(jnp.logical_not(ends))
    def _():
        halo_copy().wait_recv()

    def forward(e, turn):
        for d in range(1, blocks):
            peer_copy(d, e, turn).wait_recv()
            mate_copy(blocks - d, e, turn).start()

    @pl.loop(0, STEPS)
    def _(s):
        fill(templates_ref.shape[1], rows // STEPS, s, ext_ref, hankel_ref, norm_ref, plain_ref, turned_ref)

        @pl.when(s == 0)
        def _():
            for d in range(1, outer):
                far_copy(d).wait_recv()
                side_copy(d).start()
                spread(d, 0)

        @pl.when(s == 1)
        def _():
            for e in range(outer):
                side_copy(e).wait_recv()
                spread(e, 1)
            for d in range(1, outer):
                list_far(d).wait_recv()
                list_side(d).start()

        @pl.when(s == 2)
        def _():
            for e in range(outer):
                list_side(e).wait_recv()
            for d in range(1, blocks):
                list_peer(d).start()
            for e in range(outer):
                forward(e, 0)

    for e in range(outer):
        forward(e, 1)
    for d in range(1, blocks):
        list_peer(d).wait_recv()

    lanes = lax.broadcasted_iota(jnp.int32, (slabs, LANES), 1)
    for block in range(blocks):
        for j in range(mine):
            values = lists_ref[block * slabs : (block + 1) * slabs, j, :]
            near = jnp.where(values == tpl, 1, 0)
            table_refs[block][pl.ds(j, slabs, stride=mine), :] = jnp.where(lanes < slots, near, values)
        table_refs[block][slabs * mine :, :] = jnp.zeros((8, LANES), jnp.int32)

    for block in range(blocks):
        for turn in range(2):
            for e in range(outer):
                mate_copy(block, e, turn).wait_recv()

    @pl.when(jnp.logical_not(begins))
    def _():
        halo_copy().wait_send()

    list_mate().wait_send()
    for d in range(1, outer):
        far_copy(d).wait_send()
        list_far(d).wait_send()
    for d in range(1, blocks):
        list_peer(d).wait_send()
    for e in range(outer):
        side_copy(e).wait_send()
        list_side(e).wait_send()
        for turn in range(2):
            for d in range(1, blocks):
                peer_copy(d, e, turn).wait_send()
            for block in range(blocks):
                mate_copy(block, e, turn).wait_send()


def exchange(local, rows, stations, shifts, used, reach, hop):
    slabs = lax.axis_size("slab")
    blocks = lax.axis_size("tpl")
    height, span = rows.shape
    outer = slabs // 4
    vmem = pl.BlockSpec(memory_space=pltpu.VMEM)
    dma = pltpu.SemaphoreType.DMA
    one, few, all_units = [dma] * 2, [dma((outer,))] * 2, [dma((blocks * outer * 2,))] * 2
    return pl.pallas_call(
        functools.partial(exchange_kernel, reach, hop),
        out_shape=(
            jax.ShapeDtypeStruct((local.shape[0] * 2 * AHEAD, 16, LANES), local.dtype),
            jax.ShapeDtypeStruct((local.shape[0] * TURNS * PLANE, LANES), jnp.float32),
            jax.ShapeDtypeStruct((height * slabs * blocks, span), rows.dtype),
        ) + (jax.ShapeDtypeStruct((slabs * stations.shape[0] + 8, LANES), jnp.int32),) * blocks,
        in_specs=[pl.BlockSpec(memory_space=pltpu.HBM)] * 5,
        out_specs=(vmem,) * (3 + blocks),
        scratch_shapes=[
            pltpu.VMEM((local.shape[0], local.shape[1] + reach), local.dtype),
            pltpu.VMEM(((local.shape[0] // STEPS + 1) * PLANE, LANES), jnp.float32),
            pltpu.VMEM((SEVERAL * TURNS * PLANE, LANES), jnp.float32),
            pltpu.VMEM(rows.shape, rows.dtype),
            pltpu.VMEM((slabs * blocks, stations.shape[0], LANES), jnp.int32),
            pltpu.SMEM(stations.shape, jnp.int32),
            pltpu.SMEM(shifts.shape, jnp.int32),
            pltpu.SMEM(used.shape, jnp.int32),
            dma((5,)),
        ] + one + few + few + all_units + all_units + one + few + few + [dma((blocks,))] * 2,
        compiler_params=pltpu.CompilerParams(
            collective_id=0, has_side_effects=True, vmem_limit_bytes=24 << 20
        ),
    )(local, rows, stations, shifts, used)


def stack_kernel(span, comps, hop, slots, panel, block, table_ref, hankel_ref, norm_ref, panels_ref, out_ref,
                 hankel_out_ref, norm_out_ref, unit_ref, turned_ref, right_ref, level_ref, sum_ref, done_ref, item_ref):
    parts = span // LANES
    group = comps * slots
    count = panel * slots

    height = 2 * group
    unit_ref[count * PLANE : (count + 1) * PLANE, :] = jnp.zeros((PLANE, LANES), jnp.float32)

    def collect(step, total):
        at = pl.ds(pl.multiple_of((block * panel + 2 * step) * group, height), height)
        values = panels_ref[at, :].astype(jnp.float32)
        for t in range(2):
            j = 2 * step + t
            for c in range(comps):
                for part in range(parts):
                    piece = values[t * group + c * slots : t * group + (c + 1) * slots, part * LANES : (part + 1) * LANES]
                    unit_ref[pl.ds(j * slots * PLANE + c * parts + part, slots, stride=PLANE), :] = piece
            sum_ref[j] = jnp.zeros((TURNS * 8, LAGS), jnp.float32)
            for k in range(slots):
                item_ref[total] = j * LANES + k
                total = total + table_ref[j, k]
        return total

    total = lax.fori_loop(0, panel // 2, collect, 0, unroll=2)
    for k in range(2 * PASS):
        item_ref[total + k] = panel * LANES
    sum_ref[panel] = jnp.zeros((TURNS * 8, LAGS), jnp.float32)

    lane_half = lax.broadcasted_iota(jnp.int32, (16, LANES), 1).astype(jnp.float32).astype(jnp.bfloat16)
    lag_half = lax.broadcasted_iota(jnp.int32, (16, LANES), 0).astype(jnp.float32).astype(jnp.bfloat16)
    ahead = lane_half - lag_half
    further = ahead - jnp.full((16, LANES), 16.0, jnp.bfloat16)
    none = jnp.zeros((16, LANES), jnp.bfloat16)

    def field(g, n, which):
        item = item_ref[g * PASS + n]
        return table_ref[lax.shift_right_logical(item, 7), lax.bitwise_and(item, LANES - 1) + which * slots]

    def turn_rows(g):
        for n in range(PASS):
            item = item_ref[g * PASS + n]
            slot = lax.shift_right_logical(item, 7) * slots + lax.bitwise_and(item, LANES - 1)
            rows = unit_ref[pl.ds(pl.multiple_of(slot * PLANE, PLANE), PLANE), :]
            turned_ref[n * PLANE : (n + 1) * PLANE, :] = pltpu.roll(rows, field(g, n, 1), 1)

    def build_slot(g, n):
        bound = jnp.full((16, LANES), field(g, n, 1), jnp.int32).astype(jnp.float32).astype(jnp.bfloat16)
        inside = [ahead >= bound, further >= bound]
        for c in range(comps):
            turned = []
            for part in range(parts):
                line = jnp.broadcast_to(turned_ref[n * PLANE + c * parts + part : n * PLANE + c * parts + part + 1, :], (8, LANES))
                lags = pltpu.roll(line, 0, 1, stride=1, stride_axis=0)
                low = jnp.concatenate([lags, pltpu.roll(lags, 8, 1)], axis=0).astype(jnp.bfloat16)
                turned.append((low, pltpu.roll(low, 16, 1)))
            edges = [(none, none)] + turned + [(none, none)]
            at = (n * comps + c) * LAGS
            for b in range(2):
                for p in range(parts + 1):
                    right_ref[at + 16 * b : at + 16 * b + 16, p * LANES : (p + 1) * LANES] = jnp.where(inside[b], edges[p + 1][b], edges[p][b])
        back = LANES - field(g, n, 1)
        for turn in range(TURNS):
            at = field(g, n, 4 + turn // 2)
            for c in range(comps):
                norm = norm_ref[pl.ds(at + c * hop * TURNS * PLANE + (turn % 2) * PLANE, 8), :]
                k = (n * comps + c) * TURNS + turn
                level_ref[k * 8 : k * 8 + 8, :] = pltpu.roll(norm, back, 1)

    def build(g):
        turn_rows(g)
        for n in range(PASS):
            build_slot(g, n)

    def multiply(g):
        for n in range(PASS):
            near = field(g, n, 2)
            far = field(g, n, 3)
            for c in range(comps):
                i = n * comps + c
                left = jnp.concatenate([
                    jnp.concatenate([hankel_ref[at + c * hop * 2 * AHEAD + p] for p in range(CHUNKS)], axis=1)
                    for at in (near, far)], axis=0)
                yield n, c, lax.dot_general(
                    left, right_ref[i * LAGS : (i + 1) * LAGS, :],
                    (((1,), (1,)), ((), ())), preferred_element_type=jnp.float32)

    def gather_slot(g, n, product):
        j = lax.shift_right_logical(item_ref[g * PASS + n], 7)
        added = []
        for turn in range(TURNS):
            value = None
            for c in range(comps):
                k = (n * comps + c) * TURNS + turn
                term = product(n, c, turn) * level_ref[k * 8 : k * 8 + 8, :LAGS]
                value = term if value is None else value + term
            added.append(value)
        sum_ref[j] += jnp.concatenate(added, axis=0)

    build(0)

    def body(g, _):
        products = {}
        for n, c, product in multiply(g):
            products[n, c] = product
            if c == comps - 1:
                gather_slot(g, n, lambda n, c, turn: products[n, c][8 * turn : 8 * turn + 8, :])
        build(g + 1)
        return 0

    lax.fori_loop(0, lax.div(total + PASS - 1, PASS), body, 0)

    def finish(j, _):
        value = sum_ref[j]
        result = jnp.concatenate([value[8 * turn : 8 * turn + 8, :] for turn in range(TURNS)], axis=1)
        used = jnp.full((8, LANES), table_ref[j, (FIELDS - 1) * slots], jnp.int32).astype(jnp.float32)
        done_ref[pl.ds(pl.multiple_of(j * 8, 8), 8), :] = result * jnp.sqrt(span / (3.0 * used))
        return 0

    lax.fori_loop(0, panel, finish, 0, unroll=16)
    for b in range(panel // 8):
        for a in range(out_ref.shape[1] // LANES):
            out_ref[b * 8 : b * 8 + 8, a * LANES : (a + 1) * LANES] = done_ref[pl.ds(b * 64 + a, 8, stride=8), :]


def stack(table, hankel, norm, panels, block, panel, slots, comps, hop, span, samples):
    smem = pl.BlockSpec(memory_space=pltpu.SMEM)
    vmem = pl.BlockSpec(memory_space=pltpu.VMEM)
    count = panel * slots
    return pl.pallas_call(
        functools.partial(stack_kernel, span, comps, hop, slots, panel, block),
        out_shape=(
            jax.ShapeDtypeStruct((panel, samples), jnp.float32),
            jax.ShapeDtypeStruct(hankel.shape, hankel.dtype),
            jax.ShapeDtypeStruct(norm.shape, norm.dtype),
        ),
        in_specs=[smem, vmem, vmem, vmem],
        out_specs=(vmem, vmem, vmem),
        input_output_aliases={1: 1, 2: 2},
        scratch_shapes=[
            pltpu.VMEM(((count + 1) * PLANE, LANES), jnp.float32),
            pltpu.VMEM((PASS * PLANE, LANES), jnp.float32),
            pltpu.VMEM((PASS * comps * LAGS, CHUNKS * LANES), jnp.bfloat16),
            pltpu.VMEM((PASS * comps * TURNS * 8, LANES), jnp.float32),
            pltpu.VMEM((panel + 1, TURNS * 8, LAGS), jnp.float32),
            pltpu.VMEM((panel * 8, LANES), jnp.float32),
            pltpu.SMEM((count + 3 * PASS,), jnp.int32),
        ],
        compiler_params=pltpu.CompilerParams(vmem_limit_bytes=(count * PLANE * LANES * 4) + (8 << 20)),
        cost_estimate=pl.CostEstimate(flops=6_000_000_000, bytes_accessed=20_000_000, transcendentals=0),
    )(table, hankel, norm, panels)


def per_device(data, templates, stations, shifts, used):
    mine, slots, comps, span = templates.shape
    hop, _, samples = data.shape
    reach = span + MAXSHIFT
    slabs = lax.axis_size("slab")
    blocks = lax.axis_size("tpl")
    local = jnp.transpose(data, (1, 0, 2)).reshape(-1, samples)
    rows = jnp.transpose(templates, (0, 2, 1, 3)).reshape(-1, span)
    inputs = [pltpu.with_memory_space_constraint(x, pltpu.HBM) for x in (local, rows, stations, shifts, used)]
    hankel, norm, panels, *tables = exchange(*inputs, reach, hop)
    panel = mine * slabs

    sent = []
    for d in range(1, blocks + 1):
        block = d % blocks
        total, hankel, norm = stack(tables[block], hankel, norm, panels, block, panel, slots, comps, hop, span, samples)
        if block:
            pairs = [(t, (t + d) % blocks) for t in range(blocks)]
            sent.append(lax.ppermute(total, "tpl", pairs))
    for piece in sent:
        total = total + piece
    return total


def solution(mesh):
    return jax.shard_map(
        per_device,
        mesh=mesh,
        in_specs=(
            P("tpl", None, "slab"),
            P(("tpl", "slab"), None, None, None),
            P(("tpl", "slab"), None),
            P(("tpl", "slab"), None),
            P(("tpl", "slab")),
        ),
        out_specs=P("tpl", "slab"),
        check_vma=False,
    )
```

```python
import functools
import math

import jax
import jax.numpy as jnp
from jax import lax
from jax.experimental import pallas as pl
from jax.experimental.pallas import tpu as pltpu
from jax.sharding import PartitionSpec as P

MAXSHIFT = 256
EPS = 1e-05
MESH = pl.DeviceIdType.MESH

LANES = 128
LAGS = 32
TURNS = LANES // LAGS
PASS = 6
PLANE = 16
CHUNKS = 5
AHEAD = 7
FIELDS = 7
STEPS = 4
SEVERAL = 16


def normalized(rows):
    span = rows.shape[-1]
    centered = rows - jnp.mean(rows, axis=-1, keepdims=True)
    rms = jnp.sqrt(jnp.mean(centered * centered, axis=-1, keepdims=True) + EPS)
    return (centered / (rms * math.sqrt(span))).astype(jnp.bfloat16)


def fill(span, step, s, ext_ref, hankel_ref, norm_ref, plain_ref, turned_ref):
    width = ext_ref.shape[1]
    block = 256
    near = span // block
    nblocks = (width - span) // block
    tiles = width // LANES
    taps = lax.broadcasted_iota(jnp.int32, (block, block), 0)
    starts = lax.broadcasted_iota(jnp.int32, (block, block), 1)
    tail = jnp.where(taps >= starts, 1.0, 0.0).astype(jnp.bfloat16)
    head = jnp.where(taps < starts, 1.0, 0.0).astype(jnp.bfloat16)
    at = pl.ds(pl.multiple_of(s * step, step), step)
    stride = TURNS * PLANE
    base = pl.multiple_of(s * step * stride, step * stride)

    plain, both = [], []
    for n in range(width // block):
        values = ext_ref[at, n * block : (n + 1) * block]
        wide = values.astype(jnp.float32)
        for half in range(block // LANES):
            v = n * (block // LANES) + half
            plain_ref[pl.ds(v, step, stride=PLANE), :] = wide[:, half * LANES : (half + 1) * LANES]
        square = wide * wide
        high = square.astype(jnp.bfloat16)
        low = (square - high.astype(jnp.float32)).astype(jnp.bfloat16)
        plain.append(values)
        both.append(jnp.concatenate([high, low], axis=1))
    for v in range(tiles, PLANE):
        plain_ref[pl.ds(v, step, stride=PLANE), :] = jnp.zeros((step, LANES), jnp.float32)

    def window(pieces, weight):
        tails = jnp.dot(jnp.concatenate(pieces[:-1], axis=0), jnp.concatenate([tail] * weight, axis=0), preferred_element_type=jnp.float32)
        heads = jnp.dot(jnp.concatenate(pieces[near:], axis=0), jnp.concatenate([head] * weight, axis=0), preferred_element_type=jnp.float32)
        for n in range(nblocks):
            total = tails[n * step : (n + 1) * step, :] + heads[n * step : (n + 1) * step, :]
            for m in range(n + 1, n + near):
                total = total + tails[m * step : (m + 1) * step, :1]
            yield total

    for n, (sums, squares) in enumerate(zip(window(plain, 1), window(both, 2))):
        spread = (squares - sums * sums / span) / span
        inverse = lax.rsqrt(jnp.maximum(spread, 0.0) + EPS) * (1.0 / math.sqrt(span))
        inverse = inverse.astype(jnp.bfloat16).astype(jnp.float32)
        for half in range(block // LANES):
            v = n * (block // LANES) + half
            norm_ref[pl.ds(base + v, step, stride=stride), :] = inverse[:, half * LANES : (half + 1) * LANES]

    lane = lax.broadcasted_iota(jnp.int32, (PLANE, LANES), 1)

    @pl.loop(0, step // SEVERAL)
    def _(group):
        for q in range(SEVERAL):
            r = group * SEVERAL + q
            top = pl.multiple_of(r * PLANE, PLANE)
            here = plain_ref[pl.ds(top, PLANE), :]
            after = plain_ref[pl.ds(top + 1, PLANE), :]
            level_at = pl.multiple_of(base + r * stride, stride)
            level = norm_ref[pl.ds(level_at, PLANE), :]
            level_after = norm_ref[pl.ds(level_at + 1, PLANE), :]
            for turn in range(1, TURNS):
                keep = lane >= LAGS * turn
                back = LANES - LAGS * turn
                turned_ref[(q * TURNS + turn) * PLANE : (q * TURNS + turn + 1) * PLANE, :] = pltpu.roll(jnp.where(keep, here, after), back, 1)
                level_to = pl.ds(pl.multiple_of(level_at + turn * PLANE, PLANE), PLANE)
                norm_ref[level_to, :] = pltpu.roll(jnp.where(keep, level, level_after), back, 1)
        for q in range(SEVERAL):
            r = group * SEVERAL + q
            to = (s * step + r) * 2 * AHEAD
            for pair in range(2):
                for ahead in range(AHEAD):
                    parts = []
                    for turn in (2 * pair, 2 * pair + 1):
                        if turn == 0:
                            parts.append(plain_ref[pl.ds(r * PLANE + ahead, 8), :])
                        else:
                            rows = (q * TURNS + turn) * PLANE + ahead
                            parts.append(turned_ref[rows : rows + 8, :])
                    hankel_ref[to + pair * AHEAD + ahead] = jnp.concatenate(parts, axis=0).astype(jnp.bfloat16)


def exchange_kernel(reach, hop, data_ref, templates_ref, stations_ref, shifts_ref, used_ref, hankel_ref, norm_ref, panels_ref, *refs):
    table_refs, scratch = refs[: lax.axis_size("tpl")], refs[lax.axis_size("tpl") :]
    ext_ref, plain_ref, turned_ref, rows_ref, lists_ref, sta_ref, shf_ref, use_ref, loads = scratch[:9]
    halo_send, halo_recv, far_send, far_recv, side_send, side_recv, peer_send, peer_recv, mate_send, mate_recv = scratch[9:19]
    list_mate_send, list_mate_recv, list_far_send, list_far_recv, list_side_send, list_side_recv, list_peer_send, list_peer_recv = scratch[19:]
    rows, samples = data_ref.shape
    height = templates_ref.shape[0]
    mine, slots = stations_ref.shape
    slabs = lax.axis_size("slab")
    blocks = lax.axis_size("tpl")
    outer = slabs // 4
    slab = lax.axis_index("slab")
    tpl = lax.axis_index("tpl")
    core = lax.rem(slab, 2)
    mate = slab + 1 - 2 * core
    side = slab + 2 - 4 * lax.rem(slab // 2, 2)
    beside = lax.rem(slab + slabs - 1 + 2 * core, slabs)

    local = [
        pltpu.make_async_copy(templates_ref, rows_ref, loads.at[0]),
        pltpu.make_async_copy(stations_ref, sta_ref, loads.at[1]),
        pltpu.make_async_copy(shifts_ref, shf_ref, loads.at[2]),
        pltpu.make_async_copy(used_ref, use_ref, loads.at[3]),
        pltpu.make_async_copy(data_ref, ext_ref.at[:, :samples], loads.at[4]),
    ]
    for copy in local:
        copy.start()

    barrier = pltpu.get_barrier_semaphore()
    for d in range(1, blocks):
        pl.semaphore_signal(barrier, inc=1, device_id={"tpl": lax.rem(tpl + d, blocks)}, device_id_type=MESH)
    for d in range(1, outer):
        pl.semaphore_signal(barrier, inc=1, device_id={"slab": lax.rem(slab + 4 * d, slabs)}, device_id_type=MESH)
    for device in (mate, side, beside):
        pl.semaphore_signal(barrier, inc=1, device_id={"slab": device}, device_id_type=MESH)

    local[0].wait()
    panels_ref[pl.ds(pl.multiple_of(slab * height, height), height), :] = normalized(rows_ref[...].astype(jnp.float32))
    for copy in local[1:4]:
        copy.wait()
    lane = lax.broadcasted_iota(jnp.int32, (mine, LANES), 1)
    line = lax.broadcasted_iota(jnp.int32, (mine, LANES), 0)
    station = jnp.zeros((mine, LANES), jnp.int32)
    shift = jnp.zeros((mine, LANES), jnp.int32)
    used = jnp.zeros((mine, LANES), jnp.int32)
    for j in range(mine):
        used = jnp.where(line == j, use_ref[j], used)
        for k in range(slots):
            spot = jnp.logical_and(line == j, lane == k)
            station = jnp.where(spot, sta_ref[j, k], station)
            shift = jnp.where(spot, shf_ref[j, k], shift)
    owner = lax.div(station, hop)
    local_station = station - owner * hop
    half = lax.bitwise_and(lax.shift_right_logical(shift, 6), 1)
    first = lax.shift_right_logical(shift, 7)
    base = local_station * (TURNS * PLANE) + first
    fields = [
        jnp.where(lane < used, owner, -1),
        lax.bitwise_and(shift, 63),
        (2 * local_station + half) * AHEAD + first,
        (2 * local_station + 1 - half) * AHEAD + first + half,
        base + 2 * PLANE * half,
        base + 2 * PLANE * (1 - half) + half,
        used,
    ]
    packed = jnp.zeros((mine, LANES), jnp.int32)
    for f, values in enumerate(fields):
        kept = jnp.where(lane < slots, values, 0)
        packed = packed + (kept if f == 0 else pltpu.roll(kept, f * slots, 1))
    row, seat = lax.div(slab, 4), lax.rem(slab, 4)
    lists_ref[row, seat] = packed

    pl.semaphore_wait(barrier, blocks - 1 + outer - 1 + 3)

    def place(block, owner):
        at = (block * slabs + owner) * height
        return panels_ref.at[pl.ds(pl.multiple_of(at, height), height), :]

    def push(source, target, send, recv, device):
        return pltpu.make_async_remote_copy(
            src_ref=source, dst_ref=target, send_sem=send, recv_sem=recv, device_id=device, device_id_type=MESH)

    def owner_of(e, turn):
        start = slab + turn * (side - slab)
        return lax.rem(start + slabs - 4 * e, slabs)

    def halo_copy():
        return push(data_ref.at[:, :reach], ext_ref.at[:, samples:], halo_send, halo_recv, {"slab": lax.rem(slab + slabs - 1, slabs)})

    def far_copy(d):
        return push(place(0, slab), place(0, slab), far_send.at[d], far_recv.at[d], {"slab": lax.rem(slab + 4 * d, slabs)})

    def side_copy(e):
        at = place(0, owner_of(e, 0))
        return push(at, at, side_send.at[e], side_recv.at[e], {"slab": side})

    def peer_copy(d, e, turn):
        at = (d * outer + e) * 2 + turn
        unit = owner_of(e, turn)
        return push(place(0, unit), place(blocks - d, unit), peer_send.at[at], peer_recv.at[at], {"tpl": lax.rem(tpl + d, blocks)})

    def mate_copy(block, e, turn):
        at = (block * outer + e) * 2 + turn
        unit = place(block, owner_of(e, turn))
        return push(unit, unit, mate_send.at[at], mate_recv.at[at], {"slab": mate})

    def list_mate():
        return push(lists_ref.at[row, seat], lists_ref.at[row, seat], list_mate_send, list_mate_recv, {"slab": mate})

    def list_far(d):
        at = lists_ref.at[row, pl.ds(seat - core, 2)]
        return push(at, at, list_far_send.at[d], list_far_recv.at[d], {"slab": lax.rem(slab + 4 * d, slabs)})

    def list_side():
        at = lists_ref.at[pl.ds(0, outer), pl.ds(seat - core, 2)]
        return push(at, at, list_side_send, list_side_recv, {"slab": side})

    def list_peer(d):
        return push(
            lists_ref.at[pl.ds(0, outer)], lists_ref.at[pl.ds((blocks - d) * outer, outer)],
            list_peer_send.at[d], list_peer_recv.at[d], {"tpl": lax.rem(tpl + d, blocks)})

    def spread(e, turn):
        for d in range(1, blocks):
            peer_copy(d, e, turn).start()
        mate_copy(0, e, turn).start()

    begins = slab == 0
    ends = slab == slabs - 1
    list_mate().start()
    for d in range(1, outer):
        far_copy(d).start()

    @pl.when(jnp.logical_not(begins))
    def _():
        halo_copy().start()

    side_copy(0).start()
    spread(0, 0)
    local[4].wait()

    @pl.when(ends)
    def _():
        ext_ref[:, samples:] = jnp.zeros((rows, reach), ext_ref.dtype)

    list_mate().wait_recv()
    for d in range(1, outer):
        list_far(d).start()

    @pl.when(jnp.logical_not(ends))
    def _():
        halo_copy().wait_recv()

    def forward(e, turn):
        for d in range(1, blocks):
            peer_copy(d, e, turn).wait_recv()
            mate_copy(blocks - d, e, turn).start()

    @pl.loop(0, STEPS)
    def _(s):
        fill(templates_ref.shape[1], rows // STEPS, s, ext_ref, hankel_ref, norm_ref, plain_ref, turned_ref)

        @pl.when(s == 0)
        def _():
            for d in range(1, outer):
                far_copy(d).wait_recv()
                side_copy(d).start()
                spread(d, 0)

        @pl.when(s == 1)
        def _():
            for e in range(outer):
                side_copy(e).wait_recv()
                spread(e, 1)
            for d in range(1, outer):
                list_far(d).wait_recv()
            list_side().start()

        @pl.when(s == 2)
        def _():
            list_side().wait_recv()
            for d in range(1, blocks):
                list_peer(d).start()
            for e in range(outer):
                forward(e, 0)

    for e in range(outer):
        forward(e, 1)
    for d in range(1, blocks):
        list_peer(d).wait_recv()

    lanes = lax.broadcasted_iota(jnp.int32, (slabs, LANES), 1)
    for block in range(blocks):
        for j in range(mine):
            values = lists_ref[block * outer : (block + 1) * outer, :, j, :].reshape(slabs, LANES)
            near = jnp.where(values == tpl, 1, 0)
            table_refs[block][pl.ds(j, slabs, stride=mine), :] = jnp.where(lanes < slots, near, values)
        table_refs[block][slabs * mine :, :] = jnp.zeros((8, LANES), jnp.int32)

    for block in range(blocks):
        for turn in range(2):
            for e in range(outer):
                mate_copy(block, e, turn).wait_recv()

    @pl.when(jnp.logical_not(begins))
    def _():
        halo_copy().wait_send()

    list_mate().wait_send()
    list_side().wait_send()
    for d in range(1, outer):
        far_copy(d).wait_send()
        list_far(d).wait_send()
    for d in range(1, blocks):
        list_peer(d).wait_send()
    for e in range(outer):
        side_copy(e).wait_send()
        for turn in range(2):
            for d in range(1, blocks):
                peer_copy(d, e, turn).wait_send()
            for block in range(blocks):
                mate_copy(block, e, turn).wait_send()


def exchange(local, rows, stations, shifts, used, reach, hop):
    slabs = lax.axis_size("slab")
    blocks = lax.axis_size("tpl")
    height, span = rows.shape
    outer = slabs // 4
    vmem = pl.BlockSpec(memory_space=pltpu.VMEM)
    dma = pltpu.SemaphoreType.DMA
    one, few, all_units = [dma] * 2, [dma((outer,))] * 2, [dma((blocks * outer * 2,))] * 2
    return pl.pallas_call(
        functools.partial(exchange_kernel, reach, hop),
        out_shape=(
            jax.ShapeDtypeStruct((local.shape[0] * 2 * AHEAD, 16, LANES), local.dtype),
            jax.ShapeDtypeStruct((local.shape[0] * TURNS * PLANE, LANES), jnp.float32),
            jax.ShapeDtypeStruct((height * slabs * blocks, span), rows.dtype),
        ) + (jax.ShapeDtypeStruct((slabs * stations.shape[0] + 8, LANES), jnp.int32),) * blocks,
        in_specs=[pl.BlockSpec(memory_space=pltpu.HBM)] * 5,
        out_specs=(vmem,) * (3 + blocks),
        scratch_shapes=[
            pltpu.VMEM((local.shape[0], local.shape[1] + reach), local.dtype),
            pltpu.VMEM(((local.shape[0] // STEPS + 1) * PLANE, LANES), jnp.float32),
            pltpu.VMEM((SEVERAL * TURNS * PLANE, LANES), jnp.float32),
            pltpu.VMEM(rows.shape, rows.dtype),
            pltpu.VMEM((blocks * outer, 4, stations.shape[0], LANES), jnp.int32),
            pltpu.SMEM(stations.shape, jnp.int32),
            pltpu.SMEM(shifts.shape, jnp.int32),
            pltpu.SMEM(used.shape, jnp.int32),
            dma((5,)),
        ] + one + few + few + all_units + all_units + one + few + one + [dma((blocks,))] * 2,
        compiler_params=pltpu.CompilerParams(
            collective_id=0, has_side_effects=True, vmem_limit_bytes=24 << 20
        ),
    )(local, rows, stations, shifts, used)


def stack_kernel(span, comps, hop, slots, panel, block, table_ref, hankel_ref, norm_ref, panels_ref, out_ref,
                 hankel_out_ref, norm_out_ref, unit_ref, turned_ref, right_ref, level_ref, sum_ref, done_ref, item_ref):
    parts = span // LANES
    group = comps * slots
    count = panel * slots

    height = 2 * group
    unit_ref[count * PLANE : (count + 1) * PLANE, :] = jnp.zeros((PLANE, LANES), jnp.float32)

    def collect(step, total):
        at = pl.ds(pl.multiple_of((block * panel + 2 * step) * group, height), height)
        values = panels_ref[at, :].astype(jnp.float32)
        for t in range(2):
            j = 2 * step + t
            for c in range(comps):
                for part in range(parts):
                    piece = values[t * group + c * slots : t * group + (c + 1) * slots, part * LANES : (part + 1) * LANES]
                    unit_ref[pl.ds(j * slots * PLANE + c * parts + part, slots, stride=PLANE), :] = piece
            sum_ref[j] = jnp.zeros((TURNS * 8, LAGS), jnp.float32)
            for k in range(slots):
                item_ref[total] = j * LANES + k
                total = total + table_ref[j, k]
        return total

    total = lax.fori_loop(0, panel // 2, collect, 0, unroll=2)
    for k in range(2 * PASS):
        item_ref[total + k] = panel * LANES
    sum_ref[panel] = jnp.zeros((TURNS * 8, LAGS), jnp.float32)

    lane_half = lax.broadcasted_iota(jnp.int32, (16, LANES), 1).astype(jnp.float32).astype(jnp.bfloat16)
    lag_half = lax.broadcasted_iota(jnp.int32, (16, LANES), 0).astype(jnp.float32).astype(jnp.bfloat16)
    ahead = lane_half - lag_half
    further = ahead - jnp.full((16, LANES), 16.0, jnp.bfloat16)
    none = jnp.zeros((16, LANES), jnp.bfloat16)

    def field(g, n, which):
        item = item_ref[g * PASS + n]
        return table_ref[lax.shift_right_logical(item, 7), lax.bitwise_and(item, LANES - 1) + which * slots]

    def turn_rows(g):
        for n in range(PASS):
            item = item_ref[g * PASS + n]
            slot = lax.shift_right_logical(item, 7) * slots + lax.bitwise_and(item, LANES - 1)
            rows = unit_ref[pl.ds(pl.multiple_of(slot * PLANE, PLANE), PLANE), :]
            turned_ref[n * PLANE : (n + 1) * PLANE, :] = pltpu.roll(rows, field(g, n, 1), 1)

    def build_slot(g, n):
        bound = jnp.full((16, LANES), field(g, n, 1), jnp.int32).astype(jnp.float32).astype(jnp.bfloat16)
        inside = [ahead >= bound, further >= bound]
        for c in range(comps):
            turned = []
            for part in range(parts):
                line = jnp.broadcast_to(turned_ref[n * PLANE + c * parts + part : n * PLANE + c * parts + part + 1, :], (8, LANES))
                lags = pltpu.roll(line, 0, 1, stride=1, stride_axis=0)
                low = jnp.concatenate([lags, pltpu.roll(lags, 8, 1)], axis=0).astype(jnp.bfloat16)
                turned.append((low, pltpu.roll(low, 16, 1)))
            edges = [(none, none)] + turned + [(none, none)]
            at = (n * comps + c) * LAGS
            for b in range(2):
                for p in range(parts + 1):
                    right_ref[at + 16 * b : at + 16 * b + 16, p * LANES : (p + 1) * LANES] = jnp.where(inside[b], edges[p + 1][b], edges[p][b])
        back = LANES - field(g, n, 1)
        for turn in range(TURNS):
            at = field(g, n, 4 + turn // 2)
            for c in range(comps):
                norm = norm_ref[pl.ds(at + c * hop * TURNS * PLANE + (turn % 2) * PLANE, 8), :]
                k = (n * comps + c) * TURNS + turn
                level_ref[k * 8 : k * 8 + 8, :] = pltpu.roll(norm, back, 1)

    def build(g):
        turn_rows(g)
        for n in range(PASS):
            build_slot(g, n)

    def multiply(g):
        for n in range(PASS):
            near = field(g, n, 2)
            far = field(g, n, 3)
            for c in range(comps):
                i = n * comps + c
                left = jnp.concatenate([
                    jnp.concatenate([hankel_ref[at + c * hop * 2 * AHEAD + p] for p in range(CHUNKS)], axis=1)
                    for at in (near, far)], axis=0)
                yield n, c, lax.dot_general(
                    left, right_ref[i * LAGS : (i + 1) * LAGS, :],
                    (((1,), (1,)), ((), ())), preferred_element_type=jnp.float32)

    def gather_slot(g, n, product):
        j = lax.shift_right_logical(item_ref[g * PASS + n], 7)
        added = []
        for turn in range(TURNS):
            value = None
            for c in range(comps):
                k = (n * comps + c) * TURNS + turn
                term = product(n, c, turn) * level_ref[k * 8 : k * 8 + 8, :LAGS]
                value = term if value is None else value + term
            added.append(value)
        sum_ref[j] += jnp.concatenate(added, axis=0)

    build(0)

    def body(g, _):
        products = {}
        for n, c, product in multiply(g):
            products[n, c] = product
            if c == comps - 1:
                gather_slot(g, n, lambda n, c, turn: products[n, c][8 * turn : 8 * turn + 8, :])
        build(g + 1)
        return 0

    lax.fori_loop(0, lax.div(total + PASS - 1, PASS), body, 0)

    def finish(j, _):
        value = sum_ref[j]
        result = jnp.concatenate([value[8 * turn : 8 * turn + 8, :] for turn in range(TURNS)], axis=1)
        used = jnp.full((8, LANES), table_ref[j, (FIELDS - 1) * slots], jnp.int32).astype(jnp.float32)
        done_ref[pl.ds(pl.multiple_of(j * 8, 8), 8), :] = result * jnp.sqrt(span / (3.0 * used))
        return 0

    lax.fori_loop(0, panel, finish, 0, unroll=16)
    for b in range(panel // 8):
        for a in range(out_ref.shape[1] // LANES):
            out_ref[b * 8 : b * 8 + 8, a * LANES : (a + 1) * LANES] = done_ref[pl.ds(b * 64 + a, 8, stride=8), :]


def stack(table, hankel, norm, panels, block, panel, slots, comps, hop, span, samples):
    smem = pl.BlockSpec(memory_space=pltpu.SMEM)
    vmem = pl.BlockSpec(memory_space=pltpu.VMEM)
    count = panel * slots
    return pl.pallas_call(
        functools.partial(stack_kernel, span, comps, hop, slots, panel, block),
        out_shape=(
            jax.ShapeDtypeStruct((panel, samples), jnp.float32),
            jax.ShapeDtypeStruct(hankel.shape, hankel.dtype),
            jax.ShapeDtypeStruct(norm.shape, norm.dtype),
        ),
        in_specs=[smem, vmem, vmem, vmem],
        out_specs=(vmem, vmem, vmem),
        input_output_aliases={1: 1, 2: 2},
        scratch_shapes=[
            pltpu.VMEM(((count + 1) * PLANE, LANES), jnp.float32),
            pltpu.VMEM((PASS * PLANE, LANES), jnp.float32),
            pltpu.VMEM((PASS * comps * LAGS, CHUNKS * LANES), jnp.bfloat16),
            pltpu.VMEM((PASS * comps * TURNS * 8, LANES), jnp.float32),
            pltpu.VMEM((panel + 1, TURNS * 8, LAGS), jnp.float32),
            pltpu.VMEM((panel * 8, LANES), jnp.float32),
            pltpu.SMEM((count + 3 * PASS,), jnp.int32),
        ],
        compiler_params=pltpu.CompilerParams(vmem_limit_bytes=(count * PLANE * LANES * 4) + (8 << 20)),
        cost_estimate=pl.CostEstimate(flops=6_000_000_000, bytes_accessed=20_000_000, transcendentals=0),
    )(table, hankel, norm, panels)


def per_device(data, templates, stations, shifts, used):
    mine, slots, comps, span = templates.shape
    hop, _, samples = data.shape
    reach = span + MAXSHIFT
    slabs = lax.axis_size("slab")
    blocks = lax.axis_size("tpl")
    local = jnp.transpose(data, (1, 0, 2)).reshape(-1, samples)
    rows = jnp.transpose(templates, (0, 2, 1, 3)).reshape(-1, span)
    inputs = [pltpu.with_memory_space_constraint(x, pltpu.HBM) for x in (local, rows, stations, shifts, used)]
    hankel, norm, panels, *tables = exchange(*inputs, reach, hop)
    panel = mine * slabs

    sent = []
    for d in range(1, blocks + 1):
        block = d % blocks
        total, hankel, norm = stack(tables[block], hankel, norm, panels, block, panel, slots, comps, hop, span, samples)
        if block:
            pairs = [(t, (t + d) % blocks) for t in range(blocks)]
            sent.append(lax.ppermute(total, "tpl", pairs))
    for piece in sent:
        total = total + piece
    return total


def solution(mesh):
    return jax.shard_map(
        per_device,
        mesh=mesh,
        in_specs=(
            P("tpl", None, "slab"),
            P(("tpl", "slab"), None, None, None),
            P(("tpl", "slab"), None),
            P(("tpl", "slab"), None),
            P(("tpl", "slab")),
        ),
        out_specs=P("tpl", "slab"),
        check_vma=False,
    )
```
